32 devices in a mesh: dp: 16 (over z, x, core), head: 2 (over y).
Axes of the slice: x: 2, y: 2, z: 4, core: 2. Of those that a mesh axis runs over, the one named last changes fastest.
Arguments:
- inputs: bfloat16 [16384, 768], P(('dp', 'head')), may hold values from -6 to 6
- lengths: int32 [32], P('dp'), may hold values from 16 to 512, as said below
- labels: int32 [32], P(('dp', 'head')), may hold values from 0 to 2
- state_cotangent: bfloat16 [16384, 768], P(('dp', 'head')), may hold values from -6 to 6
- query_weight: bfloat16 [768, 768], P(None, 'head'), may hold values from -0.4375 to 0.4375
- query_bias: bfloat16 [768], P('head'), may hold values from -4 to 4
- key_weight: bfloat16 [768, 768], P(None, 'head'), may hold values from -0.21875 to 0.21875
- value_weight: bfloat16 [768, 768], P(None, 'head'), may hold values from -0.21875 to 0.21875
- value_bias: bfloat16 [768], P('head'), may hold values from -4 to 4
- out_weight: bfloat16 [768, 768], replicated, may hold values from -0.625 to 0.625
- out_bias: bfloat16 [768], replicated, may hold values from -4 to 4
- first_gain: bfloat16 [768], replicated, may hold values from 0.5 to 1.5
- first_shift: bfloat16 [768], replicated, may hold values from -4 to 4
- up_weight: bfloat16 [768, 3072], replicated, may hold values from -0.21875 to 0.21875
- up_bias: bfloat16 [3072], replicated, may hold values from -4 to 4
- down_weight: bfloat16 [3072, 768], replicated, may hold values from -0.15625 to 0.15625
- down_bias: bfloat16 [768], replicated, may hold values from -4 to 4
- second_gain: bfloat16 [768], replicated, may hold values from 0.5 to 1.5
- second_shift: bfloat16 [768], replicated, may hold values from -4 to 4
- pool_weight: bfloat16 [768, 768], replicated, may hold values from -0.21875 to 0.21875
- pool_bias: bfloat16 [768], replicated, may hold values from -4 to 4
- class_weight: bfloat16 [768, 3], replicated, may hold values from -0.875 to 0.875
- class_bias: bfloat16 [3], replicated, may hold values from -4 to 4
Outputs:
- states: bfloat16 [16384, 768], P(('dp', 'head'))
- input_grad: bfloat16 [16384, 768], P(('dp', 'head'))
- logits: float32 [32, 3], P(('dp', 'head'))
- loss: float32 [], replicated
- query_weight_grad: float32 [768, 768], P('dp', 'head')
- query_bias_grad: float32 [768], P('head')
- key_weight_grad: float32 [768, 768], P('dp', 'head')
- value_weight_grad: float32 [768, 768], P('dp', 'head')
- value_bias_grad: float32 [768], P('head')
- out_weight_grad: float32 [768, 768], P('dp', 'head')
- out_bias_grad: float32 [768], replicated
- first_gain_grad: float32 [768], replicated
- first_shift_grad: float32 [768], replicated
- up_weight_grad: float32 [768, 3072], P('dp', 'head')
- up_bias_grad: float32 [3072], replicated
- down_weight_grad: float32 [3072, 768], P('dp', 'head')
- down_bias_grad: float32 [768], replicated
- second_gain_grad: float32 [768], replicated
- second_shift_grad: float32 [768], replicated
- pool_weight_grad: float32 [768, 768], P('dp', 'head')
- pool_bias_grad: float32 [768], replicated
- class_weight_grad: float32 [768, 3], replicated
- class_bias_grad: float32 [3], replicated
The draws below stay inside these ranges and needn't reach their ends.
Inputs may be any that keep to these rules, and one draw needn't show every extreme that they name: `lengths`: every sequence has at least one real token; some sequence is full and some has the fewest.
All inputs are finite; a program needn't handle non-finite values.
Results may differ from the reference program's by a relative error of at most 0.015.
The reference program's roundings to bfloat16 on the way count: a program that leaves them out, or rounds other values in their place, can miss the bound.
Values may be sent and summed in bfloat16 or wider, within the bound.
A program may use at most 192 MiB of HBM per device.

```python
import jax
import jax.numpy as jnp
from jax import lax

D = 768
FF = 3072
HEADS = 12
HEAD_DIM = 64
CLASSES = 3
SEQ_LEN = 512
SEQS = 32
TOKENS = 16384


def draw_lengths(key, part):
    drawn = jax.random.randint(jax.random.fold_in(key, 1), (SEQS,), SEQ_LEN // 32, SEQ_LEN + 1, dtype=jnp.int32)
    longest = jax.random.randint(jax.random.fold_in(key, 2), (), 0, SEQS, dtype=jnp.int32)
    offset = jax.random.randint(jax.random.fold_in(key, 3), (), 1, SEQS, dtype=jnp.int32)
    shortest = (longest + offset) % SEQS
    places = jnp.arange(SEQS, dtype=jnp.int32)
    drawn = jnp.where(places == longest, SEQ_LEN, drawn)
    drawn = jnp.where(places == shortest, SEQ_LEN // 32, drawn)
    return drawn


def with_ends(entries, rng, smallest, high):
    place = [jax.random.randint(jax.random.fold_in(rng, axis), (), 0, length) for axis, length in enumerate(entries.shape)]
    main_axis = entries.shape.index(max(entries.shape))
    beside = place[:main_axis] + [(place[main_axis] + 1) % entries.shape[main_axis]] + place[main_axis + 1:]
    return entries.at[tuple(place)].set(smallest).at[tuple(beside)].set(high)


def block_scale(rng, extent, pieces, least, high):
    def one(axis_at, blocks):
        draws = jax.random.uniform(jax.random.fold_in(jax.random.fold_in(rng, 6), axis_at), (blocks,), jnp.float32, least / len(pieces), high / len(pieces))
        return jnp.repeat(jnp.exp(draws), extent[axis_at] // blocks).reshape((-1,) + (1,) * (len(extent) - axis_at - 1))

    level = one(*pieces[0])
    for cut in pieces[1:]:
        level = level * one(*cut)
    return level


def normal_values(key, dims, scale, limit, cuts=(), kind=jnp.bfloat16):
    result = scale * jax.random.normal(key, dims, jnp.float32)
    if cuts:
        result = result * block_scale(key, dims, cuts, -0.22, 0.18)
    return jnp.clip(result, -limit, limit).astype(kind)


def setup_inputs(seed: int = 0) -> dict:
    seeds = jax.random.split(jax.random.key(seed), 24)
    return {
        "inputs": normal_values(seeds[0], (TOKENS, D), 1.0, 6.0, ((0, 32),)),
        "lengths": draw_lengths(jax.random.fold_in(seeds[23], 71), 0),
        "labels": with_ends(jax.random.randint(seeds[2], (SEQS,), 0, CLASSES), jax.random.fold_in(seeds[2], 1), 0, CLASSES - 1).astype(jnp.int32),
        "state_cotangent": normal_values(seeds[3], (TOKENS, D), 1.0, 6.0, ((0, 32),)),
        "query_weight": normal_values(seeds[4], (D, D), (D // 4) ** -0.5, 0.4375, ((1, 2),)),
        "query_bias": normal_values(seeds[5], (D,), 0.5, 4.0, ((0, 2),)),
        "key_weight": normal_values(seeds[6], (D, D), D ** -0.5, 0.21875, ((1, 2),)),
        "value_weight": normal_values(seeds[7], (D, D), D ** -0.5, 0.21875, ((1, 2),)),
        "value_bias": normal_values(seeds[8], (D,), 0.3, 4.0, ((0, 2),)),
        "out_weight": normal_values(seeds[9], (D, D), (D // 8) ** -0.5, 0.625),
        "out_bias": normal_values(seeds[10], (D,), 0.3, 4.0),
        "first_gain": jnp.clip(1.0 + 0.1 * jax.random.normal(seeds[11], (D,), jnp.float32), 0.5, 1.5).astype(jnp.bfloat16),
        "first_shift": normal_values(seeds[12], (D,), 0.3, 4.0),
        "up_weight": normal_values(seeds[13], (D, FF), D ** -0.5, 0.21875),
        "up_bias": normal_values(seeds[14], (FF,), 0.5, 4.0),
        "down_weight": normal_values(seeds[15], (FF, D), (FF // 2) ** -0.5, 0.15625),
        "down_bias": normal_values(seeds[16], (D,), 0.3, 4.0),
        "second_gain": jnp.clip(1.0 + 0.1 * jax.random.normal(seeds[17], (D,), jnp.float32), 0.5, 1.5).astype(jnp.bfloat16),
        "second_shift": normal_values(seeds[18], (D,), 0.3, 4.0),
        "pool_weight": normal_values(seeds[19], (D, D), D ** -0.5, 0.21875),
        "pool_bias": normal_values(seeds[20], (D,), 0.5, 4.0),
        "class_weight": normal_values(seeds[21], (D, CLASSES), (D // 16) ** -0.5, 0.875),
        "class_bias": normal_values(seeds[22], (CLASSES,), 0.5, 4.0),
    }


@jax.custom_vjp
def low(v):
    return lax.optimization_barrier(v.astype(jnp.bfloat16)).astype(jnp.float32)

@jax.custom_vjp
def low_back(v):
    return v

def low_keep(v):
    return (low(v), None)

def low_pass(kept, grad):
    return (grad,)

def back_keep(v):
    return (v, None)

def back_low(kept, grad):
    return (low(grad),)
low.defvjp(low_keep, low_pass)
low_back.defvjp(back_keep, back_low)
EPSILON = 1e-06
NEGATIVE = -1e+30
HIGHEST = lax.Precision.HIGHEST

def normalize(values, gain, shift):
    center = values - lax.optimization_barrier(jnp.mean(values, -1, keepdims=True))
    spread = lax.optimization_barrier(jnp.mean(center * center, -1, keepdims=True))
    return center * lax.rsqrt(spread + EPSILON) * gain + shift

def product(left, right):
    return jnp.dot(left, right, precision=HIGHEST)

def block_forward(params, rows, seq_lengths, seq_labels):
    query_weight, query_bias, key_weight, value_weight, value_bias, out_weight, out_bias, first_gain, first_shift, up_weight, up_bias, down_weight, down_bias, second_gain, second_shift, pool_weight, pool_bias, class_weight, class_bias = params
    seq_count = seq_lengths.shape[0]

    def heads(matrix):
        return matrix.reshape(seq_count, SEQ_LEN, HEADS, HEAD_DIM)
    queries = low(low_back(product(rows, query_weight) + query_bias))
    keys_all = low(low_back(product(rows, key_weight)))
    values_all = low(low_back(product(rows, value_weight) + value_bias))
    raw = jnp.einsum('sqhd,skhd->shqk', heads(queries), heads(keys_all), precision=HIGHEST) * HEAD_DIM ** (-0.5)
    scores = low_back(raw)
    positions = jnp.arange(SEQ_LEN, dtype=jnp.int32)
    visible = positions[None, None, None, :] < seq_lengths[:, None, None, None]
    probs = low(jax.nn.softmax(jnp.where(visible, scores, NEGATIVE), axis=-1))
    context = jnp.einsum('shqk,skhd->sqhd', probs, heads(values_all), precision=HIGHEST)
    context = low(low_back(context.reshape(rows.shape[0], HEADS * HEAD_DIM)))
    attended = low_back(product(context, out_weight) + out_bias)
    first_out = normalize(rows + attended, first_gain, first_shift)
    hidden_pre = low_back(product(low(first_out), up_weight) + up_bias)
    hidden = low(jax.nn.gelu(hidden_pre, approximate=False))
    branch = low_back(product(hidden, down_weight) + down_bias)
    normed = normalize(first_out + branch, second_gain, second_shift)
    leading = normed.reshape(seq_count, SEQ_LEN, -1)[:, 0]
    pooled_pre = low_back(product(low(leading), pool_weight) + pool_bias)
    pooled = low(jnp.tanh(pooled_pre))
    logits = low_back(product(pooled, class_weight) + class_bias)
    target = (jnp.arange(CLASSES, dtype=jnp.int32)[None, :] == seq_labels[:, None]).astype(logits.dtype)
    loss_part = jnp.sum(jax.nn.logsumexp(logits, axis=-1) - lax.optimization_barrier(jnp.sum(target * logits, -1))) / SEQS
    return ((normed, loss_part), logits)

def reference(inputs, lengths, labels, state_cotangent, query_weight, query_bias, key_weight, value_weight, value_bias, out_weight, out_bias, first_gain, first_shift, up_weight, up_bias, down_weight, down_bias, second_gain, second_shift, pool_weight, pool_bias, class_weight, class_bias):
    params = tuple((weight.astype(jnp.float32) for weight in (query_weight, query_bias, key_weight, value_weight, value_bias, out_weight, out_bias, first_gain, first_shift, up_weight, up_bias, down_weight, down_bias, second_gain, second_shift, pool_weight, pool_bias, class_weight, class_bias)))
    block_seqs = 8
    blocks = SEQS // block_seqs
    rows_all = inputs.astype(jnp.float32).reshape(blocks, block_seqs * SEQ_LEN, D)
    cotangent_all = state_cotangent.astype(jnp.float32).reshape(blocks, block_seqs * SEQ_LEN, D)
    lengths_all = lengths.reshape(blocks, block_seqs)
    labels_all = labels.reshape(blocks, block_seqs)

    def step(carry, item):
        totals, loss_sum = carry
        rows, cotangent, seq_lengths, seq_labels = item

        def forward(params_in, rows_in):
            return block_forward(params_in, rows_in, seq_lengths, seq_labels)
        (normed, loss_part), pullback, logits = jax.vjp(forward, params, rows, has_aux=True)
        grad_params, grad_rows = pullback((cotangent, jnp.ones((), jnp.float32)))
        totals = jax.tree.map(jnp.add, totals, grad_params)
        return ((totals, loss_sum + loss_part), (normed.astype(jnp.bfloat16), grad_rows.astype(jnp.bfloat16), logits))
    zeros = jax.tree.map(jnp.zeros_like, params)
    (totals, loss), (states, input_grad, logits) = lax.scan(step, (zeros, jnp.zeros((), jnp.float32)), (rows_all, cotangent_all, lengths_all, labels_all))
    return (states.reshape(TOKENS, D), input_grad.reshape(TOKENS, D), logits.reshape(SEQS, CLASSES), loss, totals[0], totals[1], totals[2], totals[3], totals[4], totals[5], totals[6], totals[7], totals[8], totals[9], totals[10], totals[11], totals[12], totals[13], totals[14], totals[15], totals[16], totals[17], totals[18])
```

```python
from functools import partial

import jax
import jax.numpy as jnp
from jax import lax
from jax.experimental import pallas as pl
from jax.experimental.pallas import tpu as pltpu
from jax.sharding import PartitionSpec as P

HEAD_DIM = 64
SEQ_LEN = 512
NEGATIVE = -1e30
EPSILON = 1e-06
MESH = pl.DeviceIdType.MESH
F32 = jnp.float32
BF16 = jnp.bfloat16
VMEM_LIMIT = 62 << 20


def normalize(values, gain, shift):
    center = values - jnp.mean(values, -1, keepdims=True)
    spread = jnp.mean(center * center, -1, keepdims=True)
    return center * lax.rsqrt(spread + EPSILON) * gain + shift


def matmul(left, right):
    return jnp.dot(left, right, preferred_element_type=F32)


def column_sums(values):
    return jnp.sum(values.astype(F32), 0)


class Place:
    def __init__(self, bits):
        self.bits = bits
        self.dp = lax.axis_index("dp")
        self.head = lax.axis_index("head")
        self.mine = [lax.rem(self.dp // (1 << b), 2) for b in range(bits - 1)] + [self.head]

    def partner(self, bit):
        if bit == self.bits - 1:
            return (self.dp, 1 - self.head)
        return (self.dp + (1 - 2 * self.mine[bit]) * (1 << bit), self.head)

    def greet(self, bits):
        barrier = pltpu.get_barrier_semaphore()
        for bit in bits:
            pl.semaphore_signal(barrier, inc=1, device_id=self.partner(bit), device_id_type=MESH)
        pl.semaphore_wait(barrier, len(bits))


def gather_weights(weights, biases, bits):
    count = len(weights)
    total = count + 1
    rows, columns = weights[0].shape
    half = rows // 2

    def kernel(*refs):
        ins, outs, (send, recv) = refs[:total], refs[total : 2 * total], refs[2 * total :]
        place = Place(bits)
        place.greet([0, bits - 1])
        own = pl.ds(pl.multiple_of(place.mine[0] * half, half), half)
        bias_copy = pltpu.make_async_remote_copy(
            src_ref=ins[count], dst_ref=outs[count], send_sem=send.at[2 * count], recv_sem=recv.at[2 * count],
            device_id=place.partner(bits - 1), device_id_type=MESH)
        bias_copy.start()
        first, second = [], []
        for i in range(count):
            copy = pltpu.make_async_remote_copy(
                src_ref=ins[i].at[own], dst_ref=outs[i].at[own], send_sem=send.at[i], recv_sem=recv.at[i],
                device_id=place.partner(bits - 1), device_id_type=MESH)
            copy.start()
            first.append(copy)
        for i in range(count):
            first[i].wait_recv()
            copy = pltpu.make_async_remote_copy(
                src_ref=outs[i].at[own], dst_ref=outs[i].at[own], send_sem=send.at[count + i],
                recv_sem=recv.at[count + i], device_id=place.partner(0), device_id_type=MESH)
            copy.start()
            second.append(copy)
        for copy in second + [bias_copy]:
            copy.wait_recv()
        for copy in first + second + [bias_copy]:
            copy.wait_send()

    spec = pl.BlockSpec(memory_space=pltpu.VMEM)
    return pl.pallas_call(
        kernel,
        out_shape=[jax.ShapeDtypeStruct(w.shape, w.dtype) for w in weights + [biases]],
        in_specs=[spec] * total,
        out_specs=[spec] * total,
        scratch_shapes=[pltpu.SemaphoreType.DMA((2 * count + 1,))] * 2,
        compiler_params=pltpu.CompilerParams(collective_id=0, has_side_effects=True, vmem_limit_bytes=VMEM_LIMIT),
        name="gather_weights",
    )(*weights, biases)


def orders(bits):
    head = bits - 1
    rest = list(range(2, head))
    return [[0, 1, head] + rest, [0, head, 1] + rest, [0] + rest + [1, head]]


def reduce_pieces(pieces, small, factors, bits):
    count = len(pieces)
    rows, columns = pieces[0].shape[1:]
    plans = [orders(bits)[i % 3] for i in range(count)]
    grid_dims = (2,) * bits
    stages = bits
    head = bits - 1
    small_order = [0, 1, head] + list(range(2, head))

    def kernel(*refs):
        ins = refs[:count]
        small_in, factor_in = refs[count : count + 2]
        outs = refs[count + 2 : 2 * count + 2]
        small_out, factor_out = refs[2 * count + 2 : 2 * count + 4]
        held = refs[2 * count + 4]
        got = refs[2 * count + 5 : 2 * count + 5 + stages]
        small_buf, small_got, load_sem, send, recv, side_send, side_recv = refs[2 * count + 5 + stages :]
        place = Place(bits)

        loads = []
        for i in range(count):
            load = pltpu.make_async_copy(ins[i], held.at[i], load_sem.at[i])
            load.start()
            loads.append(load)
        slot = sum(place.mine[bit] * (1 << k) for k, bit in enumerate(small_order))
        factor_out[slot] = factor_in[...]
        small_buf[0] = small_in[...]
        place.greet(range(bits))

        def index(i, done, fixed, free_bits):
            out = [i]
            for bit in reversed(range(bits)):
                if bit in fixed:
                    out.append(fixed[bit])
                elif bit in done:
                    out.append(place.mine[bit])
                else:
                    out.append(free_bits[bit] if free_bits is not None else slice(None))
            return tuple(out)

        started = {}

        def send_piece(i, s):
            bit = plans[i][s]
            source = held.at[index(i, plans[i][:s], {bit: 1 - place.mine[bit]}, None)]
            copy = pltpu.make_async_remote_copy(
                src_ref=source, dst_ref=got[s].at[i], send_sem=send.at[i, s], recv_sem=recv.at[i, s],
                device_id=place.partner(bit), device_id_type=MESH)
            copy.start()
            started[i, s] = copy

        def add_piece(i, s):
            started[i, s].wait_recv()
            done = plans[i][: s + 1]
            free = [bit for bit in reversed(range(bits)) if bit not in done]
            if not free:
                where = index(i, done, {}, None)
                outs[i][...] = held[where].astype(F32) + got[s][i].astype(F32)
                return

            def step(n, carry):
                free_bits = {bit: lax.rem(n // (1 << (len(free) - 1 - k)), 2) for k, bit in enumerate(free)}
                where = index(i, done, {}, free_bits)
                there = (i,) + tuple(free_bits[bit] for bit in free)
                held[where] = (held[where].astype(F32) + got[s][there].astype(F32)).astype(BF16)
                return carry

            lax.fori_loop(0, 1 << len(free), step, 0)

        def side_send_stage(s):
            partner = place.partner(small_order[s])
            copies = []
            start = (slot // (1 << s)) * (1 << s)
            block = pl.ds(start, 1 << s)
            for k, (source, target) in enumerate(
                ((small_buf.at[s], small_got.at[s]), (factor_out.at[block], factor_out.at[block]))
            ):
                copy = pltpu.make_async_remote_copy(
                    src_ref=source, dst_ref=target, send_sem=side_send.at[k, s], recv_sem=side_recv.at[k, s],
                    device_id=partner, device_id_type=MESH)
                copy.start()
                copies.append(copy)
            started["side", s] = copies

        def side_add_stage(s):
            for copy in started["side", s]:
                copy.wait_recv()
            total = small_buf[s] + small_got[s]
            if s < stages - 1:
                small_buf[s + 1] = total
            else:
                small_out[...] = total

        for t in range(count + stages):
            for s in reversed(range(stages + 1)):
                i = t - s
                if 0 <= i < count:
                    if s == 0:
                        loads[i].wait()
                    else:
                        add_piece(i, s - 1)
                    if s < stages:
                        send_piece(i, s)
            if t <= stages:
                if t > 0:
                    side_add_stage(t - 1)
                if t < stages:
                    side_send_stage(t)
        for key, copy in started.items():
            for one in copy if isinstance(copy, list) else [copy]:
                one.wait_send()

    vmem = pl.BlockSpec(memory_space=pltpu.VMEM)
    anywhere = pl.BlockSpec(memory_space=pl.ANY)
    devices = 1 << bits
    pieces = [p.reshape(grid_dims + (rows, columns)) for p in pieces]
    results = pl.pallas_call(
        kernel,
        out_shape=[jax.ShapeDtypeStruct((rows, columns), F32)] * count
        + [jax.ShapeDtypeStruct(small.shape, F32), jax.ShapeDtypeStruct((devices,) + factors.shape, factors.dtype)],
        in_specs=[anywhere] * count + [vmem] * 2,
        out_specs=[vmem] * (count + 2),
        scratch_shapes=[pltpu.VMEM((count,) + grid_dims + (rows, columns), BF16)]
        + [pltpu.VMEM((count,) + (2,) * (stages - 1 - s) + (rows, columns), BF16) for s in range(stages)]
        + [
            pltpu.VMEM((stages,) + small.shape, F32),
            pltpu.VMEM((stages,) + small.shape, F32),
            pltpu.SemaphoreType.DMA((count,)),
            pltpu.SemaphoreType.DMA((count, stages)),
            pltpu.SemaphoreType.DMA((count, stages)),
            pltpu.SemaphoreType.DMA((2, stages)),
            pltpu.SemaphoreType.DMA((2, stages)),
        ],
        compiler_params=pltpu.CompilerParams(collective_id=1, has_side_effects=True, vmem_limit_bytes=VMEM_LIMIT),
        name="reduce_pieces",
    )(*pieces, small, factors)
    return results[:count], results[count], results[count + 1]


def body(
    inputs, lengths, labels, state_cotangent, query_weight, query_bias, key_weight, value_weight, value_bias,
    out_weight, out_bias, first_gain, first_shift, up_weight, up_bias, down_weight, down_bias, second_gain,
    second_shift, pool_weight, pool_bias, class_weight, class_bias,
):
    scale = HEAD_DIM ** (-0.5)
    dp_size, head_size = lax.axis_size("dp"), lax.axis_size("head")
    dp_at, head_at = lax.axis_index("dp"), lax.axis_index("head")
    devices = dp_size * head_size
    bits = devices.bit_length() - 1
    width = inputs.shape[1]
    hidden = up_weight.shape[1]
    block_rows, block_columns = width // dp_size, width // head_size
    direct = block_rows % 16 == 0 and block_columns % 128 == 0 and head_size == 2
    row_seqs = labels.shape[0]
    assert row_seqs == 1 and inputs.shape[0] == SEQ_LEN
    length = lax.dynamic_index_in_dim(lengths, head_at, keepdims=False)

    weights = [query_weight, key_weight, value_weight]
    if direct:
        own_biases = jnp.concatenate([query_bias, value_bias]).reshape(-1, 128)
        bias_rows = own_biases.shape[0]
        own_biases = jnp.pad(own_biases, ((0, -bias_rows % 16), (0, 0)))
        others = gather_weights(weights, own_biases, bits)
        first = head_at == 0

        def join(mine, other):
            return jnp.concatenate([jnp.where(first, mine, other), jnp.where(first, other, mine)], -1)

        full = [join(mine, other) for mine, other in zip(weights, others)]
        half = bias_rows // 2
        query_bias = join(query_bias, others[3][:half].reshape(-1))
        value_bias = join(value_bias, others[3][half:bias_rows].reshape(-1))
    else:
        full = [lax.all_gather(w, "head", axis=1, tiled=True) for w in weights]
        biases = lax.all_gather(jnp.stack([query_bias, value_bias]), "head", axis=1, tiled=True)
        query_bias, value_bias = biases[0], biases[1]
    wq, wk, wv = full
    head_count = width // HEAD_DIM

    def heads(matrix):
        return matrix.reshape(SEQ_LEN, head_count, HEAD_DIM)

    queries = (matmul(inputs, wq) + query_bias).astype(BF16)
    keys_low = matmul(inputs, wk).astype(BF16)
    values_low = (matmul(inputs, wv) + value_bias).astype(BF16)
    visible = lax.broadcasted_iota(jnp.int32, (1, 1, SEQ_LEN), 2) < length

    def scores_of():
        raw = jnp.einsum("qhd,khd->hqk", heads(queries), heads(keys_low), preferred_element_type=F32) * scale
        return jnp.where(visible, raw, NEGATIVE)

    scores = scores_of()
    peak = jnp.max(scores, -1, keepdims=True)
    raised = jnp.exp(scores - peak)
    denominator = jnp.sum(raised, -1, keepdims=True)
    probs = raised / denominator
    log_total = peak + jnp.log(denominator)
    context = jnp.einsum("hqk,khd->qhd", probs.astype(BF16), heads(values_low), preferred_element_type=F32)
    context_rows = context.astype(BF16).reshape(SEQ_LEN, width)
    attended = matmul(context_rows, out_weight) + out_bias
    first_out, first_back = jax.vjp(
        normalize, inputs.astype(F32) + attended, first_gain.astype(F32), first_shift.astype(F32))
    first_low = first_out.astype(BF16)
    hidden_pre = matmul(first_low, up_weight) + up_bias
    hidden_act, gelu_back = jax.vjp(partial(jax.nn.gelu, approximate=False), hidden_pre)
    hidden_low = hidden_act.astype(BF16)
    branch = matmul(hidden_low, down_weight) + down_bias
    normed, second_back = jax.vjp(normalize, first_out + branch, second_gain.astype(F32), second_shift.astype(F32))
    leading_low = normed.reshape(row_seqs, SEQ_LEN, -1)[:, 0].astype(BF16)
    pooled = jnp.tanh(matmul(leading_low, pool_weight) + pool_bias)
    pooled_low = pooled.astype(BF16)
    logits = matmul(pooled_low, class_weight) + class_bias
    classes = lax.broadcasted_iota(jnp.int32, logits.shape, 1)
    target = (classes == labels[:, None]).astype(F32)
    log_norm = jax.nn.logsumexp(logits, axis=-1)
    loss_part = jnp.sum(log_norm - jnp.sum(target * logits, -1)) / devices
    grad_logits = ((jnp.exp(logits - log_norm[:, None]) - target) / devices).astype(BF16)
    grad_class_weight = matmul(pooled_low.T, grad_logits)
    grad_class_bias = column_sums(grad_logits)
    grad_pooled = (matmul(grad_logits, class_weight.T) * (1.0 - pooled * pooled)).astype(BF16)
    grad_pool_bias = column_sums(grad_pooled)
    grad_leading = matmul(grad_pooled, pool_weight.T)
    grad_normed = state_cotangent.astype(F32).reshape(row_seqs, SEQ_LEN, -1)
    grad_normed = grad_normed.at[:, 0].add(grad_leading).reshape(normed.shape)
    grad_second, grad_second_gain, grad_second_shift = second_back(grad_normed)
    grad_branch = grad_second.astype(BF16)
    grad_down_weight = matmul(hidden_low.T, grad_branch)
    grad_down_bias = column_sums(grad_branch)
    grad_hidden = gelu_back(matmul(grad_branch, down_weight.T))[0].astype(BF16)
    grad_up_weight = matmul(first_low.T, grad_hidden)
    grad_up_bias = column_sums(grad_hidden)
    grad_first_out = grad_second + matmul(grad_hidden, up_weight.T)
    grad_first, grad_first_gain, grad_first_shift = first_back(grad_first_out)
    grad_attended = grad_first.astype(BF16)
    grad_out_weight = matmul(context_rows.T, grad_attended)
    grad_out_bias = column_sums(grad_attended)
    grad_context = heads(matmul(grad_attended, out_weight.T).astype(BF16))
    probs_again = jnp.exp(scores_of() - log_total)
    grad_values = jnp.einsum(
        "hqk,qhd->khd", probs_again.astype(BF16), grad_context, preferred_element_type=F32).astype(BF16)
    grad_probs = jnp.einsum("qhd,khd->hqk", grad_context, heads(values_low), preferred_element_type=F32)
    grad_scores = probs_again * (grad_probs - jnp.sum(probs_again * grad_probs, -1, keepdims=True))
    grad_scores = grad_scores.astype(BF16)
    grad_queries = (
        jnp.einsum("hqk,khd->qhd", grad_scores, heads(keys_low), preferred_element_type=F32) * scale).astype(BF16)
    grad_keys = (
        jnp.einsum("hqk,qhd->khd", grad_scores, heads(queries), preferred_element_type=F32) * scale).astype(BF16)
    grad_queries = grad_queries.reshape(SEQ_LEN, width)
    grad_keys = grad_keys.reshape(SEQ_LEN, width)
    grad_values = grad_values.reshape(SEQ_LEN, width)
    grad_query_weight = matmul(inputs.T, grad_queries)
    grad_key_weight = matmul(inputs.T, grad_keys)
    grad_value_weight = matmul(inputs.T, grad_values)
    input_grad = (
        grad_first + matmul(grad_queries, wq.T) + matmul(grad_keys, wk.T) + matmul(grad_values, wv.T)).astype(BF16)

    small_parts = (
        grad_out_bias, grad_first_gain, grad_first_shift, grad_up_bias, grad_down_bias, grad_second_gain,
        grad_second_shift, grad_pool_bias, column_sums(grad_queries), column_sums(grad_values),
        grad_class_weight.reshape(-1), grad_class_bias, loss_part.reshape(1),
    )
    grads = (grad_up_weight, grad_down_weight, grad_out_weight, grad_query_weight, grad_key_weight, grad_value_weight)
    if direct:
        flat = jnp.concatenate(small_parts)
        small_rows = -(-flat.shape[0] // 1024) * 8
        small = jnp.pad(flat, (0, small_rows * 128 - flat.shape[0])).reshape(small_rows, 128)
        factors = jnp.concatenate([leading_low[0], grad_pooled[0]]).reshape(-1, 128)
        factors = jnp.pad(factors, ((0, -factors.shape[0] % 16), (0, 0)))

        def blocks(matrix, row_parts, column_parts):
            rows = matrix.shape[0] // dp_size // row_parts
            columns = matrix.shape[1] // head_size // column_parts
            cut = matrix.astype(BF16).reshape(dp_size, row_parts, rows, head_size, column_parts, columns)
            cut = cut.transpose(1, 4, 3, 0, 2, 5).reshape(row_parts * column_parts, devices, rows, columns)
            return [cut[i] for i in range(row_parts * column_parts)]

        times = hidden // width
        pieces = blocks(grads[0], 1, times) + blocks(grads[1], times, 1)
        for grad in grads[2:]:
            pieces += blocks(grad, 1, 1)
        sums, small_total, gathered = reduce_pieces(pieces, small, factors, bits)
        up_total = jnp.concatenate(sums[:times], 1)
        down_total = jnp.concatenate(sums[times : 2 * times], 0)
        out_total, query_total, key_total, value_total = sums[2 * times :]
        lanes = width // 128
        left = gathered[:, :lanes].reshape(devices, width)
        right = gathered[:, lanes : 2 * lanes].reshape(devices, width)
        left = lax.dynamic_slice_in_dim(left, dp_at * block_rows, block_rows, 1)
        right = lax.dynamic_slice_in_dim(right, head_at * block_columns, block_columns, 1)
        pool_total = matmul(left.T, right)
        flat_total = small_total.reshape(-1)
        totals, at = [], 0
        for part in small_parts:
            totals.append(lax.slice_in_dim(flat_total, at, at + part.shape[0]))
            at += part.shape[0]
    else:
        grads = grads + (matmul(leading_low.T, grad_pooled),)

        def scatter(matrix):
            part = lax.psum_scatter(matrix, "dp", scatter_dimension=0, tiled=True)
            return lax.psum_scatter(part.astype(BF16), "head", scatter_dimension=1, tiled=True).astype(F32)

        up_total, down_total, out_total, query_total, key_total, value_total, pool_total = map(scatter, grads)
        totals = lax.psum(small_parts, ("dp", "head"))
    (
        out_bias_total, first_gain_total, first_shift_total, up_bias_total, down_bias_total, second_gain_total,
        second_shift_total, pool_bias_total, query_bias_total, value_bias_total, class_weight_total,
        class_bias_total, loss,
    ) = totals
    query_bias_total = lax.dynamic_slice_in_dim(query_bias_total, head_at * block_columns, block_columns)
    value_bias_total = lax.dynamic_slice_in_dim(value_bias_total, head_at * block_columns, block_columns)
    return (
        normed.astype(BF16), input_grad, logits, loss.reshape(()), query_total, query_bias_total, key_total,
        value_total, value_bias_total, out_total, out_bias_total, first_gain_total, first_shift_total, up_total,
        up_bias_total, down_total, down_bias_total, second_gain_total, second_shift_total, pool_total,
        pool_bias_total, class_weight_total.reshape(class_weight.shape), class_bias_total,
    )


def solution(mesh):
    rows, column, both = P(("dp", "head"), None), P(None, "head"), P("dp", "head")
    one, none = P("head"), P()
    return jax.shard_map(
        body,
        mesh=mesh,
        in_specs=(rows, P("dp"), P(("dp", "head")), rows, column, one, column, column, one) + (none,) * 14,
        out_specs=(
            rows, rows, rows, none, both, one, both, both, one, both, none, none, none, both, none, both, none,
            none, none, both, none, none, none,
        ),
        check_vma=False,
    )
```

```python
from functools import partial

import jax
import jax.numpy as jnp
from jax import lax
from jax.experimental import pallas as pl
from jax.experimental.pallas import tpu as pltpu
from jax.sharding import PartitionSpec as P

HEAD_DIM = 64
SEQ_LEN = 512
NEGATIVE = -1e30
EPSILON = 1e-06
MESH = pl.DeviceIdType.MESH
F32 = jnp.float32
BF16 = jnp.bfloat16
VMEM_LIMIT = 62 << 20


def normalize(values, gain, shift):
    center = values - jnp.mean(values, -1, keepdims=True)
    spread = jnp.mean(center * center, -1, keepdims=True)
    return center * lax.rsqrt(spread + EPSILON) * gain + shift


def matmul(left, right):
    return jnp.dot(left, right, preferred_element_type=F32)


def column_sums(values):
    return jnp.sum(values.astype(F32), 0)


class Place:
    def __init__(self, bits):
        self.bits = bits
        self.dp = lax.axis_index("dp")
        self.head = lax.axis_index("head")
        self.mine = [lax.rem(self.dp // (1 << b), 2) for b in range(bits - 1)] + [self.head]

    def partner(self, bit):
        if bit == self.bits - 1:
            return (self.dp, 1 - self.head)
        return (self.dp + (1 - 2 * self.mine[bit]) * (1 << bit), self.head)

    def greet(self, bits):
        barrier = pltpu.get_barrier_semaphore()
        for bit in bits:
            pl.semaphore_signal(barrier, inc=1, device_id=self.partner(bit), device_id_type=MESH)
        pl.semaphore_wait(barrier, len(bits))


def shared_rows(bits):
    return 1, 2


def lane_iota(shape):
    return lax.broadcasted_iota(jnp.int32, shape, 1)


def first_lanes(shape):
    return lane_iota(shape) < HEAD_DIM


def pair_operands(q2, k2, length, parity):
    lanes = lane_iota(q2.shape)
    rows = lax.broadcasted_iota(jnp.int32, q2.shape, 0)
    mine = (lanes < HEAD_DIM) if parity == 0 else (lanes >= HEAD_DIM)
    spare = lanes == (HEAD_DIM if parity == 0 else 0)
    hidden = jnp.where(rows < length, 0.0, NEGATIVE)
    qa = jnp.where(mine, q2.astype(F32) * HEAD_DIM ** -0.5, jnp.where(spare, 1.0, 0.0)).astype(BF16)
    ka = jnp.where(mine, k2.astype(F32), jnp.where(spare, hidden, 0.0)).astype(BF16)
    return qa, ka


def nt(left, right):
    return lax.dot_general(left, right, (((1,), (1,)), ((), ())), preferred_element_type=F32)


def tn(left, right):
    return lax.dot_general(left, right, (((0,), (0,)), ((), ())), preferred_element_type=F32)


def attend_pair(q_ref, k_ref, v_ref, ctx_ref, lse_ref, pair, length):
    at = pl.ds(pl.multiple_of(pair * 128, 128), 128)
    q2, k2, v2 = q_ref[:, at], k_ref[:, at], v_ref[:, at]
    v2t = v2.T
    rows = lax.broadcasted_iota(jnp.int32, (128, SEQ_LEN), 0)
    parts = []
    for parity in range(2):
        qa, ka = pair_operands(q2, k2, length, parity)
        scores = nt(ka, qa)
        peak = jnp.max(scores, 0, keepdims=True)
        raised = jnp.exp(scores - peak)
        total = jnp.sum(raised, 0, keepdims=True)
        probs = (raised * (1.0 / total)).astype(BF16)
        parts.append(matmul(v2t, probs))
        lse_ref[pair, parity : parity + 1, :] = peak + jnp.log(total)
    joined = jnp.where(rows < HEAD_DIM, parts[0], parts[1])
    ctx_ref[:, at] = joined.T.astype(BF16)


def attention_forward(inputs, weights, biases, lengths, bits):
    rows, width = inputs.shape
    depth, half = weights[0].shape
    part = depth // 8
    pairs = half // 128
    kinds = 10

    def kernel(lengths_ref, x_ref, wq_ref, wk_ref, wv_ref, bias_ref, q_ref, k_ref, v_ref, ctx_ref, lse_ref, fq_ref,
               fk_ref, fv_ref, bias_got, send, recv, bias_send, bias_recv):
        place = Place(bits)
        head = place.head
        bit_x, bit_z = shared_rows(bits)
        place.greet([0, bit_x, bit_z, bits - 1])
        length = lengths_ref[head]
        own_refs, full_refs = (wq_ref, wk_ref, wv_ref), (fq_ref, fk_ref, fv_ref)
        own = pl.ds(pl.multiple_of(head * half, half), half)
        other = pl.ds(pl.multiple_of((1 - head) * half, half), half)
        core, x, z = place.mine[0], place.mine[bit_x], place.mine[bit_z]

        def rows_of(at_x, at_z, lower=None):
            start = core * (4 * part) + (at_z * 2 + at_x) * part
            if lower is None:
                return pl.ds(pl.multiple_of(start, part), part)
            return pl.ds(pl.multiple_of(start + lower * (part // 2), part // 2), part // 2)

        started = {}

        def start(j, kind, source, where, bit):
            copy = pltpu.make_async_remote_copy(
                src_ref=source, dst_ref=full_refs[j].at[where], send_sem=send.at[j, kind], recv_sem=recv.at[j, kind],
                device_id=place.partner(bit), device_id_type=MESH)
            copy.start()
            started[j, kind] = copy

        bias_copy = pltpu.make_async_remote_copy(
            src_ref=bias_ref, dst_ref=bias_got, send_sem=bias_send, recv_sem=bias_recv,
            device_id=place.partner(bits - 1), device_id_type=MESH)
        for j in range(3):
            mine = rows_of(x, z)
            start(j, 0, own_refs[j].at[mine, :], (mine, own), bits - 1)
        bias_copy.start()

        def forward(j, kind, where, bit):
            start(j, kind, full_refs[j].at[where], where, bit)

        def stage_one(j):
            started[j, 0].wait_recv()
            where = (rows_of(x, z), other)
            forward(j, 1, where, bit_x)
            forward(j, 2, where, bit_z)
            forward(j, 5, where, 0)

        def stage_two(j):
            started[j, 1].wait_recv()
            forward(j, 4, (rows_of(1 - x, z, 1), other), bit_z)
            forward(j, 6, (rows_of(1 - x, z), other), 0)
            started[j, 2].wait_recv()
            forward(j, 3, (rows_of(x, 1 - z, 0), other), bit_x)
            forward(j, 7, (rows_of(x, 1 - z), other), 0)

        def stage_three(j):
            for kind, lower in ((3, 0), (4, 1)):
                started[j, kind].wait_recv()
                forward(j, kind + 5, (rows_of(1 - x, 1 - z, lower), other), 0)

        def stage_four(j):
            for kind in range(5, 10):
                started[j, kind].wait_recv()

        def project(j, where, bias):
            value = matmul(x_ref[...], full_refs[j][:, where])
            if bias is not None:
                value = value + bias
            (q_ref, k_ref, v_ref)[j][:, where] = value.astype(BF16)

        for j in range(3):
            full_refs[j][:, own] = own_refs[j][...]
        project(0, own, bias_ref[0:1, :])
        project(1, own, None)
        project(2, own, bias_ref[1:2, :])

        def attend(pair):
            attend_pair(q_ref, k_ref, v_ref, ctx_ref, lse_ref, pair, length)

        stage_one(0)
        attend(head * pairs)
        stage_one(1)
        stage_two(0)
        attend(head * pairs + 1)
        stage_one(2)
        stage_two(1)
        stage_three(0)
        attend(head * pairs + 2)
        stage_two(2)
        stage_three(1)
        stage_three(2)
        bias_copy.wait_recv()
        stage_four(0)
        project(0, other, bias_got[0:1, :])
        stage_four(1)
        project(1, other, None)
        stage_four(2)
        project(2, other, bias_got[1:2, :])

        def late(n, carry):
            attend((1 - head) * pairs + n)
            return carry

        lax.fori_loop(0, pairs, late, 0)
        for copy in started.values():
            copy.wait_send()
        bias_copy.wait_send()

    vmem = pl.BlockSpec(memory_space=pltpu.VMEM)
    act = jax.ShapeDtypeStruct((rows, width), BF16)
    full = jax.ShapeDtypeStruct((depth, width), BF16)
    return pl.pallas_call(
        kernel,
        out_shape=[act] * 4 + [jax.ShapeDtypeStruct((2 * pairs, 2, rows), F32)] + [full] * 3,
        in_specs=[pl.BlockSpec(memory_space=pltpu.SMEM)] + [vmem] * 5,
        out_specs=[vmem] * 8,
        scratch_shapes=[pltpu.VMEM(biases.shape, F32), pltpu.SemaphoreType.DMA((3, kinds)),
                        pltpu.SemaphoreType.DMA((3, kinds)), pltpu.SemaphoreType.DMA, pltpu.SemaphoreType.DMA],
        compiler_params=pltpu.CompilerParams(collective_id=0, has_side_effects=True, vmem_limit_bytes=VMEM_LIMIT),
        name="attention_forward",
    )(lengths, inputs, *weights, biases)


def gelu_parts(v):
    x = jnp.abs(v) * 0.7071067811865476
    t = 1.0 / (1.0 + 0.3275911 * x)
    bell = jnp.exp(-0.5 * (v * v))
    tail = 0.5 * bell * t * (
        0.254829592 + t * (-0.284496736 + t * (1.421413741 + t * (-1.453152027 + t * 1.061405429))))
    phi = jnp.where(v >= 0, 1.0 - tail, tail)
    return v * phi, phi + v * bell * 0.3989422804014327


ROW_BLOCK = 64


def over_rows(rows, step, carry):
    def one(n, kept):
        return step(pl.ds(pl.multiple_of(n * ROW_BLOCK, ROW_BLOCK), ROW_BLOCK), kept)

    return lax.fori_loop(0, rows // ROW_BLOCK, one, carry)


OUT_BIAS, FIRST_GAIN, FIRST_SHIFT, DOWN_BIAS, SECOND_GAIN, SECOND_SHIFT, POOL_BIAS, CLASS_BIAS, UP_BIAS = range(9)
QUERY_BIAS, VALUE_BIAS, LOSS = 6, 7, 12


def row_side(context, inputs, cotangent, vectors, class_padded, labels, out_weight, up_weight, down_weight, pool_weight,
             devices, head_size):
    rows, width = inputs.shape
    hidden = up_weight.shape[1]
    half = width // 2
    chunk = half
    chunks = hidden // chunk
    times = hidden // width
    dp_size = devices // head_size
    block = width // dp_size
    classes_padded = class_padded.shape[1]
    per_width = width // 128

    def kernel(labels_ref, ctx_ref, x_ref, vec_ref, cls_ref, ow_ref, cot_hbm, up_hbm, down_hbm, pool_hbm,
               states_ref, gfirst_ref, gctx_ref, small_ref, fact_ref, logit_ref, up_out, down_out, out_out,
               cot, up_w, down_w, pool_w, first, low_ref, n1, r1, n2, r2, hid, slope, acc, gb_ref, ga_ref,
               frow, up_buf, down_buf, out_buf, load_sem, store_sem):
        loads = []
        for i, (source, target) in enumerate(
            ((up_hbm, up_w), (down_hbm, down_w), (pool_hbm, pool_w), (cot_hbm, cot))):
            load = pltpu.make_async_copy(source, target, load_sem.at[i])
            load.start()
            loads.append(load)

        def vec(i):
            return vec_ref[i : i + 1, :]

        acc[...] = matmul(ctx_ref[...], ow_ref[...])

        def norm_one(at, carry):
            value = x_ref[at, :].astype(F32) + (acc[at, :] + vec(OUT_BIAS))
            center = value - jnp.mean(value, -1, keepdims=True)
            scale = lax.rsqrt(jnp.mean(center * center, -1, keepdims=True) + EPSILON)
            normal = center * scale
            out = normal * vec(FIRST_GAIN) + vec(FIRST_SHIFT)
            n1[at, :] = normal
            r1[at, :] = scale
            first[at, :] = out
            low_ref[at, :] = out.astype(BF16)
            acc[at, :] = jnp.zeros_like(out)
            return carry

        over_rows(rows, norm_one, 0)
        loads[0].wait()
        loads[1].wait()

        def forward(c, carry):
            at = pl.ds(pl.multiple_of(c * chunk, chunk), chunk)
            pre = matmul(low_ref[...], up_w[:, at]) + vec_ref[pl.ds(UP_BIAS + c // 2, 1), pl.ds(pl.multiple_of(lax.rem(c, 2) * half, half), half)]
            act, deriv = gelu_parts(pre)
            act = act.astype(BF16)
            hid[:, at] = act
            slope[:, at] = deriv
            acc[...] += matmul(act, down_w[at, :])
            return carry

        lax.fori_loop(0, chunks, forward, 0)

        def norm_two(at, carry):
            value = first[at, :] + (acc[at, :] + vec(DOWN_BIAS))
            center = value - jnp.mean(value, -1, keepdims=True)
            scale = lax.rsqrt(jnp.mean(center * center, -1, keepdims=True) + EPSILON)
            normal = center * scale
            n2[at, :] = normal
            r2[at, :] = scale
            states_ref[at, :] = (normal * vec(SECOND_GAIN) + vec(SECOND_SHIFT)).astype(BF16)
            return carry

        over_rows(rows, norm_two, 0)

        loads[2].wait()
        loads[3].wait()
        lead = states_ref[0:16, :]
        pooled = jnp.tanh(matmul(lead, pool_w[...]) + vec(POOL_BIAS))
        pooled_low = pooled.astype(BF16)
        logits = matmul(pooled_low, cls_ref[...]) + vec_ref[CLASS_BIAS : CLASS_BIAS + 1, 0:classes_padded]
        lanes = lane_iota(logits.shape)
        logits = jnp.where(lanes < 3, logits, NEGATIVE)
        top = jnp.max(logits, -1, keepdims=True)
        norm = top + jnp.log(jnp.sum(jnp.exp(logits - top), -1, keepdims=True))
        target = jnp.where(lanes == labels_ref[0], 1.0, 0.0)
        loss = (norm - jnp.sum(jnp.where(lanes < 3, target * logits, 0.0), -1, keepdims=True)) / devices
        grad_logits = (jnp.where(lanes < 3, jnp.exp(logits - norm) - target, 0.0) / devices).astype(BF16)
        grad_pooled = (nt(grad_logits, cls_ref[...]) * (1.0 - pooled * pooled)).astype(BF16)
        grad_lead = nt(grad_pooled, pool_w[...])
        logit_ref[...] = logits[0:8, :]
        frow[...] = jnp.zeros_like(frow)
        for k, value in enumerate((lead, grad_pooled, pooled_low)):
            wide = value.astype(F32)
            for j in range(per_width):
                frow[k * per_width + j : k * per_width + j + 1, :] = wide[0:1, j * 128 : (j + 1) * 128]
        frow[3 * per_width : 3 * per_width + 1, :] = grad_logits.astype(F32)[0:1, 0:128]
        fact_ref[...] = frow[...].astype(BF16)

        def back_two(at, sums):
            gain_sum, shift_sum, bias_sum = sums
            row = at.start + lax.broadcasted_iota(jnp.int32, (ROW_BLOCK, width), 0)
            grad = cot[at, :].astype(F32) + jnp.where(row == 0, grad_lead[0:1, :], 0.0)
            normal = n2[at, :]
            e = grad * vec(SECOND_GAIN)
            value = (e - jnp.mean(e, -1, keepdims=True) - normal * jnp.mean(e * normal, -1, keepdims=True)) * r2[at, :]
            rounded = value.astype(BF16)
            acc[at, :] = value
            gb_ref[at, :] = rounded
            return (gain_sum + jnp.sum(grad * normal, 0, keepdims=True), shift_sum + jnp.sum(grad, 0, keepdims=True),
                    bias_sum + jnp.sum(rounded.astype(F32), 0, keepdims=True))

        zero = jnp.zeros((1, width), F32)
        gain_sum, shift_sum, bias_sum = over_rows(rows, back_two, (zero, zero, zero))
        small_ref[...] = jnp.zeros_like(small_ref)
        small_ref[SECOND_GAIN : SECOND_GAIN + 1, :] = gain_sum
        small_ref[SECOND_SHIFT : SECOND_SHIFT + 1, :] = shift_sum
        small_ref[DOWN_BIAS : DOWN_BIAS + 1, :] = bias_sum
        small_ref[LOSS : LOSS + 1, :] = jnp.broadcast_to(loss[0:1, 0:1], (1, width))

        def stores_of(c):
            slot = lax.rem(c, 2)
            up = pltpu.make_async_copy(up_buf.at[slot], up_out.at[lax.rem(c, times), c // times], store_sem.at[0, slot])
            down = pltpu.make_async_copy(
                down_buf.at[slot], down_out.at[:, :, pl.ds(c * (chunk // (times * block)), chunk // (times * block))],
                store_sem.at[1, slot])
            return up, down

        def backward(c, carry):
            at = pl.ds(pl.multiple_of(c * chunk, chunk), chunk)
            slot = lax.rem(c, 2)
            grad = (nt(gb_ref[...], down_w[at, :]) * slope[:, at]).astype(BF16)
            small_ref[pl.ds(UP_BIAS + c // 2, 1), pl.ds(pl.multiple_of(lax.rem(c, 2) * half, half), half)] = jnp.sum(
                grad.astype(F32), 0, keepdims=True)

            @pl.when(c >= 2)
            def _():
                for copy in stores_of(c - 2):
                    copy.wait()

            up_buf[slot] = tn(low_ref[...], grad).astype(BF16).reshape(dp_size, block, half)
            wide = tn(hid[:, at], gb_ref[...]).astype(BF16).reshape(chunk // (times * block), times, block, width)
            for t in range(times):
                for h in range(2):
                    down_buf[slot, t, h] = wide[:, t, :, h * half : (h + 1) * half]
            for copy in stores_of(c):
                copy.start()
            acc[...] += nt(grad, up_w[:, at])
            return carry

        lax.fori_loop(0, chunks, backward, 0)

        def back_one(at, sums):
            gain_sum, shift_sum, bias_sum = sums
            grad = acc[at, :]
            normal = n1[at, :]
            e = grad * vec(FIRST_GAIN)
            value = (e - jnp.mean(e, -1, keepdims=True) - normal * jnp.mean(e * normal, -1, keepdims=True)) * r1[at, :]
            rounded = value.astype(BF16)
            gfirst_ref[at, :] = value
            ga_ref[at, :] = rounded
            return (gain_sum + jnp.sum(grad * normal, 0, keepdims=True), shift_sum + jnp.sum(grad, 0, keepdims=True),
                    bias_sum + jnp.sum(rounded.astype(F32), 0, keepdims=True))

        gain_sum, shift_sum, bias_sum = over_rows(rows, back_one, (zero, zero, zero))
        small_ref[FIRST_GAIN : FIRST_GAIN + 1, :] = gain_sum
        small_ref[FIRST_SHIFT : FIRST_SHIFT + 1, :] = shift_sum
        small_ref[OUT_BIAS : OUT_BIAS + 1, :] = bias_sum
        gctx_ref[...] = nt(ga_ref[...], ow_ref[...]).astype(BF16)
        grad_out = tn(ctx_ref[...], ga_ref[...]).astype(BF16).reshape(dp_size, block, width)
        for h in range(2):
            out_buf[h] = grad_out[:, :, h * half : (h + 1) * half]
        out_copy = pltpu.make_async_copy(out_buf, out_out, store_sem.at[2, 0])
        out_copy.start()
        for c in range(chunks - 2, chunks):
            for copy in stores_of(c):
                copy.wait()
        out_copy.wait()

    vmem = pl.BlockSpec(memory_space=pltpu.VMEM)
    anywhere = pl.BlockSpec(memory_space=pl.ANY)
    act_low, act = jax.ShapeDtypeStruct((rows, width), BF16), jax.ShapeDtypeStruct((rows, width), F32)
    pieces = jax.ShapeDtypeStruct((times, 2, dp_size, block, half), BF16)
    fact_rows = -(-(3 * per_width + 1) // 16) * 16
    return pl.pallas_call(
        kernel,
        out_shape=[
            act_low, act, act_low, jax.ShapeDtypeStruct((16, width), F32), jax.ShapeDtypeStruct((fact_rows, 128), BF16),
            jax.ShapeDtypeStruct((8, classes_padded), F32), pieces, pieces,
            jax.ShapeDtypeStruct((2, dp_size, block, half), BF16),
        ],
        in_specs=[pl.BlockSpec(memory_space=pltpu.SMEM)] + [vmem] * 5 + [anywhere] * 4,
        out_specs=[vmem] * 6 + [anywhere] * 3,
        scratch_shapes=[
            pltpu.VMEM((rows, width), BF16),
            pltpu.VMEM((width, hidden), BF16),
            pltpu.VMEM((hidden, width), BF16),
            pltpu.VMEM((width, width), BF16),
            pltpu.VMEM((rows, width), F32),
            pltpu.VMEM((rows, width), BF16),
            pltpu.VMEM((rows, width), F32),
            pltpu.VMEM((rows, 1), F32),
            pltpu.VMEM((rows, width), F32),
            pltpu.VMEM((rows, 1), F32),
            pltpu.VMEM((rows, hidden), BF16),
            pltpu.VMEM((rows, hidden), F32),
            pltpu.VMEM((rows, width), F32),
            pltpu.VMEM((rows, width), BF16),
            pltpu.VMEM((rows, width), BF16),
            pltpu.VMEM((fact_rows, 128), F32),
            pltpu.VMEM((2, dp_size, block, half), BF16),
            pltpu.VMEM((2, times, 2, chunk // (times * block), block, half), BF16),
            pltpu.VMEM((2, dp_size, block, half), BF16),
            pltpu.SemaphoreType.DMA((4,)),
            pltpu.SemaphoreType.DMA((3, 2)),
        ],
        compiler_params=pltpu.CompilerParams(vmem_limit_bytes=VMEM_LIMIT),
        name="row_side",
    )(labels, context, inputs, vectors, class_padded, out_weight, cotangent, up_weight, down_weight, pool_weight)


def orders(bits):
    head = bits - 1
    rest = list(range(2, head))
    return [[0, 1, head] + rest, [0, head, 1] + rest, [0] + rest[:1] + [1, head] + rest[1:]]


def attention_backward(queries, keys, values, grad_context, inputs, full, grad_first, log_totals, lengths, up_pieces,
                       down_pieces, out_piece, small, factors, bits):
    times, _, dp_size, block, half = up_pieces.shape
    rows, width = inputs.shape
    plans = orders(bits)
    group = len(plans)
    count = 2 * times + 4
    groups = count // group
    grid_dims = (2,) * bits
    stages = bits
    head = bits - 1
    small_order = [0, 1, head] + list(range(2, head))
    pairs = width // 128

    def kernel(lengths_ref, q_ref, k_ref, v_ref, gc_ref, x_ref, wq_ref, wk_ref, wv_ref, gfirst_ref, lse_ref, small_in,
               factor_in, up_in, down_in, out_in, grad_ref, sums_ref, small_out, factor_out, held, *rest):
        got = rest[:stages]
        (dq_ref, dk_ref, dv_ref, small_buf, small_got, load_sem, send, recv, side_send, side_recv) = rest[stages:]
        place = Place(bits)
        loads = []
        sources = [up_in.at[i] for i in range(times)] + [down_in.at[i] for i in range(times)] + [out_in]
        for i, source in enumerate(sources):
            load = pltpu.make_async_copy(source, held.at[i], load_sem.at[i])
            load.start()
            loads.append(load)
        slot = sum(place.mine[bit] * (1 << k) for k, bit in enumerate(small_order))
        factor_out[slot] = factor_in[...]
        place.greet(range(bits))
        length = lengths_ref[place.head]

        def index(i, done, fixed, free_bits):
            out = [i]
            for bit in reversed(range(bits)):
                if bit in fixed:
                    out.append(fixed[bit])
                elif bit in done:
                    out.append(place.mine[bit])
                else:
                    out.append(free_bits[bit] if free_bits is not None else slice(None))
            return tuple(out)

        started = {}

        def send_piece(i, s):
            plan = plans[i % group]
            bit = plan[s]
            source = held.at[index(i, plan[:s], {bit: 1 - place.mine[bit]}, None)]
            copy = pltpu.make_async_remote_copy(
                src_ref=source, dst_ref=got[s].at[i], send_sem=send.at[i, s], recv_sem=recv.at[i, s],
                device_id=place.partner(bit), device_id_type=MESH)
            copy.start()
            started[i, s] = copy

        def add_piece(i, s):
            started[i, s].wait_recv()
            done = plans[i % group][: s + 1]
            free = [bit for bit in reversed(range(bits)) if bit not in done]
            if not free:
                where = index(i, done, {}, None)
                sums_ref[i] = held[where].astype(F32) + got[s][i].astype(F32)
                return

            def step(n, carry):
                free_bits = {bit: lax.rem(n // (1 << (len(free) - 1 - k)), 2) for k, bit in enumerate(free)}
                where = index(i, done, {}, free_bits)
                there = (i,) + tuple(free_bits[bit] for bit in free)
                held[where] = (held[where].astype(F32) + got[s][there].astype(F32)).astype(BF16)
                return carry

            lax.fori_loop(0, 1 << len(free), step, 0)

        def advance(g, s):
            for i in range(g * group, (g + 1) * group):
                if s == 0:
                    if i < len(loads):
                        loads[i].wait()
                else:
                    add_piece(i, s - 1)
                if s < stages:
                    send_piece(i, s)

        def side_send_stage(s):
            partner = place.partner(small_order[s])
            copies = []
            start = (slot // (1 << s)) * (1 << s)
            rows_at = pl.ds(start, 1 << s)
            for k, (source, target) in enumerate(
                ((small_buf.at[s], small_got.at[s]), (factor_out.at[rows_at], factor_out.at[rows_at]))
            ):
                copy = pltpu.make_async_remote_copy(
                    src_ref=source, dst_ref=target, send_sem=side_send.at[k, s], recv_sem=side_recv.at[k, s],
                    device_id=partner, device_id_type=MESH)
                copy.start()
                copies.append(copy)
            started["side", s] = copies

        def side_add_stage(s):
            for copy in started["side", s]:
                copy.wait_recv()
            total = small_buf[s] + small_got[s]
            if s < stages - 1:
                small_buf[s + 1] = total
            else:
                small_out[...] = total

        lanes_row = lax.broadcasted_iota(jnp.int32, (128, rows), 0)
        lanes = lane_iota((rows, 128))

        def attend(pair, carry):
            at = pl.ds(pl.multiple_of(pair * 128, 128), 128)
            q2, k2, v2, g2 = q_ref[:, at], k_ref[:, at], v_ref[:, at], gc_ref[:, at]
            k2t = k2.T
            parts = []
            for parity in range(2):
                qa, ka = pair_operands(q2, k2, length, parity)
                mine = (lanes < HEAD_DIM) if parity == 0 else (lanes >= HEAD_DIM)
                va = jnp.where(mine, v2.astype(F32), 0.0).astype(BF16)
                probs = jnp.exp(nt(ka, qa) - lse_ref[pair, parity : parity + 1, :])
                grad_v = matmul(probs.astype(BF16), g2)
                grad_probs = nt(va, g2)
                inner = jnp.sum(probs * grad_probs, 0, keepdims=True)
                grad_scores = (probs * (grad_probs - inner)).astype(BF16)
                parts.append((grad_v, matmul(grad_scores, qa), matmul(k2t, grad_scores)))
            first = lanes < HEAD_DIM
            dv_ref[:, at] = jnp.where(first, parts[0][0], parts[1][0]).astype(BF16)
            dk_ref[:, at] = jnp.where(first, parts[0][1], parts[1][1]).astype(BF16)
            turned = jnp.where(lanes_row < HEAD_DIM, parts[0][2], parts[1][2]) * HEAD_DIM ** -0.5
            dq_ref[:, at] = turned.T.astype(BF16)
            return carry

        ready = groups - 1
        for g in range(ready):
            advance(g, 0)
        lax.fori_loop(0, 1, attend, 0)
        advance(0, 1)
        advance(1, 1)
        lax.fori_loop(1, 3, attend, 0)
        advance(0, 2)
        advance(2, 1)
        lax.fori_loop(3, 5, attend, 0)
        advance(0, 3)
        advance(1, 2)
        lax.fori_loop(5, pairs, attend, 0)
        advance(0, 4)

        for j, ref in enumerate((dq_ref, dk_ref, dv_ref)):
            for h in range(2):
                value = tn(x_ref[...], ref[:, h * half : (h + 1) * half]).astype(BF16)
                shape = (2,) * (bits - 1) + (block, half)
                held[group * ready + j, h] = value.reshape(shape)
        advance(ready, 0)

        def total_of(ref):
            return jnp.sum(ref[...].astype(F32), 0, keepdims=True)

        small_buf[0] = small_in[...]
        small_buf[0, QUERY_BIAS : QUERY_BIAS + 1, :] = total_of(dq_ref)
        small_buf[0, VALUE_BIAS : VALUE_BIAS + 1, :] = total_of(dv_ref)
        side_send_stage(0)
        advance(ready, 1)
        advance(1, 3)
        advance(2, 2)
        side_add_stage(0)
        side_send_stage(1)
        grad_ref[...] = (gfirst_ref[...] + nt(dq_ref[...], wq_ref[...]) + nt(dk_ref[...], wk_ref[...])
                         + nt(dv_ref[...], wv_ref[...])).astype(BF16)
        todo = [(0, 5), (1, 4), (2, 3), (3, 2), (1, 5), (2, 4), (3, 3), (2, 5), (3, 4), (3, 5)]
        for n, (g, s) in enumerate(todo):
            advance(g, s)
            if n in (1, 3, 5, 7):
                k = 1 + n // 2
                side_add_stage(k)
                if k + 1 < stages:
                    side_send_stage(k + 1)
        for key, copy in started.items():
            for one in copy if isinstance(copy, list) else [copy]:
                one.wait_send()

    vmem = pl.BlockSpec(memory_space=pltpu.VMEM)
    anywhere = pl.BlockSpec(memory_space=pl.ANY)
    devices = 1 << bits
    pieces = [p.reshape((-1,) + grid_dims + (block, half)) for p in (up_pieces, down_pieces)]
    return pl.pallas_call(
        kernel,
        out_shape=[
            jax.ShapeDtypeStruct((rows, width), BF16), jax.ShapeDtypeStruct((count, block, half), F32),
            jax.ShapeDtypeStruct(small.shape, F32), jax.ShapeDtypeStruct((devices,) + factors.shape, factors.dtype),
        ],
        in_specs=[pl.BlockSpec(memory_space=pltpu.SMEM)] + [vmem] * 12 + [anywhere] * 3,
        out_specs=[vmem] * 4,
        scratch_shapes=[pltpu.VMEM((count,) + grid_dims + (block, half), BF16)]
        + [pltpu.VMEM((count,) + (2,) * (stages - 1 - s) + (block, half), BF16) for s in range(stages)]
        + [pltpu.VMEM((rows, width), BF16)] * 3
        + [
            pltpu.VMEM((stages,) + small.shape, F32),
            pltpu.VMEM((stages,) + small.shape, F32),
            pltpu.SemaphoreType.DMA((count - 3,)),
            pltpu.SemaphoreType.DMA((count, stages)),
            pltpu.SemaphoreType.DMA((count, stages)),
            pltpu.SemaphoreType.DMA((2, stages)),
            pltpu.SemaphoreType.DMA((2, stages)),
        ],
        compiler_params=pltpu.CompilerParams(collective_id=1, has_side_effects=True, vmem_limit_bytes=VMEM_LIMIT),
        name="attention_backward",
    )(lengths, queries, keys, values, grad_context, inputs, *full, grad_first, log_totals, small, factors,
      *pieces, out_piece.reshape(grid_dims + (block, half)))


def spread(sums, small, gathered, classes, head_size):
    count, block, half = sums.shape
    devices = gathered.shape[0]
    width = small.shape[1]
    times = (count - 4) // 2
    lanes = width // 128

    def kernel(sums_ref, small_ref, got_ref, up, down, out, query, key, value, pool, query_bias, value_bias, out_bias,
               first_gain, first_shift, up_bias, down_bias, second_gain, second_shift, pool_bias, class_weight,
               class_bias, loss, left, right):
        dp, head = lax.axis_index("dp"), lax.axis_index("head")
        for t in range(times):
            up[:, t * half : (t + 1) * half] = sums_ref[t]
            down[t * block : (t + 1) * block, :] = sums_ref[times + t]
        for k, ref in enumerate((out, query, key, value)):
            ref[...] = sums_ref[2 * times + k]
        got = got_ref[...].astype(F32)

        def wide(k):
            return jnp.concatenate([got[:, k * lanes + j, :] for j in range(lanes)], 1)

        lead, grad_pooled, pooled = wide(0), wide(1), wide(2)
        grad_logits = got[:, 3 * lanes, :]
        left[...] = lead.T
        right[...] = grad_pooled
        pool[...] = matmul(
            left[pl.ds(pl.multiple_of(dp * block, 8), block), :].astype(BF16),
            right[:, pl.ds(pl.multiple_of(head * half, half), half)].astype(BF16))
        pool_bias[...] = jnp.sum(grad_pooled, 0, keepdims=True)
        class_weight[...] = tn(pooled.astype(BF16), grad_logits.astype(BF16))[:, 0:classes]
        class_bias[...] = jnp.sum(grad_logits, 0, keepdims=True)[:, 0:classes]
        at = pl.ds(pl.multiple_of(head * half, half), half)
        query_bias[...] = small_ref[QUERY_BIAS : QUERY_BIAS + 1, at]
        value_bias[...] = small_ref[VALUE_BIAS : VALUE_BIAS + 1, at]
        for ref, row in ((out_bias, OUT_BIAS), (first_gain, FIRST_GAIN), (first_shift, FIRST_SHIFT),
                         (down_bias, DOWN_BIAS), (second_gain, SECOND_GAIN), (second_shift, SECOND_SHIFT)):
            ref[...] = small_ref[row : row + 1, :]
        for t in range(times):
            up_bias[:, t * width : (t + 1) * width] = small_ref[UP_BIAS + t : UP_BIAS + t + 1, :]
        loss[...] = small_ref[LOSS : LOSS + 1, 0:1]

    def f32(*shape):
        return jax.ShapeDtypeStruct(shape, F32)

    square = f32(block, half)
    row = f32(1, width)
    return pl.pallas_call(
        kernel,
        out_shape=[
            f32(block, times * half), f32(times * block, half), square, square, square, square, square, f32(1, half),
            f32(1, half), row, row, row, f32(1, times * width), row, row, row, row, f32(width, classes),
            f32(1, classes), f32(1, 1),
        ],
        in_specs=[pl.BlockSpec(memory_space=pltpu.VMEM)] * 3,
        out_specs=[pl.BlockSpec(memory_space=pltpu.VMEM)] * 20,
        scratch_shapes=[pltpu.VMEM((width, devices), F32), pltpu.VMEM((devices, width), F32)],
        compiler_params=pltpu.CompilerParams(vmem_limit_bytes=VMEM_LIMIT),
        name="spread",
    )(sums, small, gathered)


def plain_body(
    inputs, lengths, labels, state_cotangent, query_weight, query_bias, key_weight, value_weight, value_bias,
    out_weight, out_bias, first_gain, first_shift, up_weight, up_bias, down_weight, down_bias, second_gain,
    second_shift, pool_weight, pool_bias, class_weight, class_bias,
):
    scale = HEAD_DIM ** (-0.5)
    dp_size, head_size = lax.axis_size("dp"), lax.axis_size("head")
    dp_at, head_at = lax.axis_index("dp"), lax.axis_index("head")
    devices = dp_size * head_size
    width = inputs.shape[1]
    block_columns = width // head_size
    row_seqs = labels.shape[0]
    assert row_seqs == 1 and inputs.shape[0] == SEQ_LEN
    length = lax.dynamic_index_in_dim(lengths, head_at, keepdims=False)

    weights = [query_weight, key_weight, value_weight]
    full = [lax.all_gather(w, "head", axis=1, tiled=True) for w in weights]
    biases = lax.all_gather(jnp.stack([query_bias, value_bias]), "head", axis=1, tiled=True)
    query_bias, value_bias = biases[0], biases[1]
    wq, wk, wv = full
    head_count = width // HEAD_DIM

    def heads(matrix):
        return matrix.reshape(SEQ_LEN, head_count, HEAD_DIM)

    queries = (matmul(inputs, wq) + query_bias).astype(BF16)
    keys_low = matmul(inputs, wk).astype(BF16)
    values_low = (matmul(inputs, wv) + value_bias).astype(BF16)
    visible = lax.broadcasted_iota(jnp.int32, (1, 1, SEQ_LEN), 2) < length

    def scores_of():
        raw = jnp.einsum("qhd,khd->hqk", heads(queries), heads(keys_low), preferred_element_type=F32) * scale
        return jnp.where(visible, raw, NEGATIVE)

    scores = scores_of()
    peak = jnp.max(scores, -1, keepdims=True)
    raised = jnp.exp(scores - peak)
    denominator = jnp.sum(raised, -1, keepdims=True)
    probs = raised / denominator
    log_total = peak + jnp.log(denominator)
    context = jnp.einsum("hqk,khd->qhd", probs.astype(BF16), heads(values_low), preferred_element_type=F32)
    context_rows = context.astype(BF16).reshape(SEQ_LEN, width)
    attended = matmul(context_rows, out_weight) + out_bias
    first_out, first_back = jax.vjp(
        normalize, inputs.astype(F32) + attended, first_gain.astype(F32), first_shift.astype(F32))
    first_low = first_out.astype(BF16)
    hidden_pre = matmul(first_low, up_weight) + up_bias
    hidden_act, gelu_back = jax.vjp(partial(jax.nn.gelu, approximate=False), hidden_pre)
    hidden_low = hidden_act.astype(BF16)
    branch = matmul(hidden_low, down_weight) + down_bias
    normed, second_back = jax.vjp(normalize, first_out + branch, second_gain.astype(F32), second_shift.astype(F32))
    leading_low = normed.reshape(row_seqs, SEQ_LEN, -1)[:, 0].astype(BF16)
    pooled = jnp.tanh(matmul(leading_low, pool_weight) + pool_bias)
    pooled_low = pooled.astype(BF16)
    logits = matmul(pooled_low, class_weight) + class_bias
    classes = lax.broadcasted_iota(jnp.int32, logits.shape, 1)
    target = (classes == labels[:, None]).astype(F32)
    log_norm = jax.nn.logsumexp(logits, axis=-1)
    loss_part = jnp.sum(log_norm - jnp.sum(target * logits, -1)) / devices
    grad_logits = ((jnp.exp(logits - log_norm[:, None]) - target) / devices).astype(BF16)
    grad_class_weight = matmul(pooled_low.T, grad_logits)
    grad_class_bias = column_sums(grad_logits)
    grad_pooled = (matmul(grad_logits, class_weight.T) * (1.0 - pooled * pooled)).astype(BF16)
    grad_pool_bias = column_sums(grad_pooled)
    grad_leading = matmul(grad_pooled, pool_weight.T)
    grad_normed = state_cotangent.astype(F32).reshape(row_seqs, SEQ_LEN, -1)
    grad_normed = grad_normed.at[:, 0].add(grad_leading).reshape(normed.shape)
    grad_second, grad_second_gain, grad_second_shift = second_back(grad_normed)
    grad_branch = grad_second.astype(BF16)
    grad_down_weight = matmul(hidden_low.T, grad_branch)
    grad_down_bias = column_sums(grad_branch)
    grad_hidden = gelu_back(matmul(grad_branch, down_weight.T))[0].astype(BF16)
    grad_up_weight = matmul(first_low.T, grad_hidden)
    grad_up_bias = column_sums(grad_hidden)
    grad_first_out = grad_second + matmul(grad_hidden, up_weight.T)
    grad_first, grad_first_gain, grad_first_shift = first_back(grad_first_out)
    grad_attended = grad_first.astype(BF16)
    grad_out_weight = matmul(context_rows.T, grad_attended)
    grad_out_bias = column_sums(grad_attended)
    grad_context = heads(matmul(grad_attended, out_weight.T).astype(BF16))
    probs_again = jnp.exp(scores_of() - log_total)
    grad_values = jnp.einsum(
        "hqk,qhd->khd", probs_again.astype(BF16), grad_context, preferred_element_type=F32).astype(BF16)
    grad_probs = jnp.einsum("qhd,khd->hqk", grad_context, heads(values_low), preferred_element_type=F32)
    grad_scores = probs_again * (grad_probs - jnp.sum(probs_again * grad_probs, -1, keepdims=True))
    grad_scores = grad_scores.astype(BF16)
    grad_queries = (
        jnp.einsum("hqk,khd->qhd", grad_scores, heads(keys_low), preferred_element_type=F32) * scale).astype(BF16)
    grad_keys = (
        jnp.einsum("hqk,qhd->khd", grad_scores, heads(queries), preferred_element_type=F32) * scale).astype(BF16)
    grad_queries = grad_queries.reshape(SEQ_LEN, width)
    grad_keys = grad_keys.reshape(SEQ_LEN, width)
    grad_values = grad_values.reshape(SEQ_LEN, width)
    grad_query_weight = matmul(inputs.T, grad_queries)
    grad_key_weight = matmul(inputs.T, grad_keys)
    grad_value_weight = matmul(inputs.T, grad_values)
    input_grad = (
        grad_first + matmul(grad_queries, wq.T) + matmul(grad_keys, wk.T) + matmul(grad_values, wv.T)).astype(BF16)

    small_parts = (
        grad_out_bias, grad_first_gain, grad_first_shift, grad_up_bias, grad_down_bias, grad_second_gain,
        grad_second_shift, grad_pool_bias, column_sums(grad_queries), column_sums(grad_values),
        grad_class_weight.reshape(-1), grad_class_bias, loss_part.reshape(1),
    )
    grads = (grad_up_weight, grad_down_weight, grad_out_weight, grad_query_weight, grad_key_weight, grad_value_weight)
    grads = grads + (matmul(leading_low.T, grad_pooled),)

    def scatter(matrix):
        part = lax.psum_scatter(matrix, "dp", scatter_dimension=0, tiled=True)
        return lax.psum_scatter(part.astype(BF16), "head", scatter_dimension=1, tiled=True).astype(F32)

    up_total, down_total, out_total, query_total, key_total, value_total, pool_total = map(scatter, grads)
    totals = lax.psum(small_parts, ("dp", "head"))
    (
        out_bias_total, first_gain_total, first_shift_total, up_bias_total, down_bias_total, second_gain_total,
        second_shift_total, pool_bias_total, query_bias_total, value_bias_total, class_weight_total,
        class_bias_total, loss,
    ) = totals
    query_bias_total = lax.dynamic_slice_in_dim(query_bias_total, head_at * block_columns, block_columns)
    value_bias_total = lax.dynamic_slice_in_dim(value_bias_total, head_at * block_columns, block_columns)
    return (
        normed.astype(BF16), input_grad, logits, loss.reshape(()), query_total, query_bias_total, key_total,
        value_total, value_bias_total, out_total, out_bias_total, first_gain_total, first_shift_total, up_total,
        up_bias_total, down_total, down_bias_total, second_gain_total, second_shift_total, pool_total,
        pool_bias_total, class_weight_total.reshape(class_weight.shape), class_bias_total,
    )


def body(*args):
    (
        inputs, lengths, labels, state_cotangent, query_weight, query_bias, key_weight, value_weight, value_bias,
        out_weight, out_bias, first_gain, first_shift, up_weight, up_bias, down_weight, down_bias, second_gain,
        second_shift, pool_weight, pool_bias, class_weight, class_bias,
    ) = args
    dp_size, head_size = lax.axis_size("dp"), lax.axis_size("head")
    devices = dp_size * head_size
    bits = devices.bit_length() - 1
    rows, width = inputs.shape
    hidden = up_weight.shape[1]
    classes = class_weight.shape[1]
    times = hidden // width
    direct = (
        (width // dp_size) % 16 == 0 and head_size == 2 and bits == 5 and times == 4 and rows == SEQ_LEN
        and labels.shape[0] == 1
    )
    if not direct:
        return plain_body(*args)

    def row(vector):
        return jnp.pad(vector.astype(F32), (0, width - vector.shape[0]))

    vectors = jnp.concatenate(
        [row(v) for v in (out_bias, first_gain, first_shift, down_bias, second_gain, second_shift, pool_bias,
                          class_bias)] + [up_bias.astype(F32), jnp.zeros((4 * width,), F32)]).reshape(16, width)
    own_biases = jnp.concatenate(
        [query_bias.astype(F32), value_bias.astype(F32), jnp.zeros((6 * (width // 2),), F32)]).reshape(8, width // 2)
    class_padded = jnp.pad(class_weight, ((0, 0), (0, 128 - classes)))
    queries, keys, values, context, log_totals, *full = attention_forward(
        inputs, [query_weight, key_weight, value_weight], own_biases, lengths, bits)
    states, grad_first, grad_context, small, factors, logits, up_pieces, down_pieces, out_piece = row_side(
        context, inputs, state_cotangent, vectors, class_padded, labels, out_weight, up_weight, down_weight, pool_weight,
        devices, head_size)
    input_grad, sums, small_total, gathered = attention_backward(
        queries, keys, values, grad_context, inputs, full, grad_first, log_totals, lengths, up_pieces, down_pieces,
        out_piece, small, factors, bits)
    (
        up, down, out, query, key, value, pool, query_sum, value_sum, out_sum, first_gain_sum, first_shift_sum, up_sum,
        down_sum, second_gain_sum, second_shift_sum, pool_sum, class_sum, class_bias_sum, loss,
    ) = spread(sums, small_total, gathered, classes, head_size)

    def flat(array):
        return array.reshape(-1)

    return (
        states, input_grad, logits[0:1, 0:classes], loss.reshape(()), query, flat(query_sum), key, value,
        flat(value_sum), out, flat(out_sum), flat(first_gain_sum), flat(first_shift_sum), up, flat(up_sum), down,
        flat(down_sum), flat(second_gain_sum), flat(second_shift_sum), pool, flat(pool_sum), class_sum,
        flat(class_bias_sum),
    )


def solution(mesh):
    rows, column, both = P(("dp", "head"), None), P(None, "head"), P("dp", "head")
    one, none = P("head"), P()
    return jax.shard_map(
        body,
        mesh=mesh,
        in_specs=(rows, P("dp"), P(("dp", "head")), rows, column, one, column, column, one) + (none,) * 14,
        out_specs=(
            rows, rows, rows, none, both, one, both, both, one, both, none, none, none, both, none, both, none,
            none, none, both, none, none, none,
        ),
        check_vma=False,
    )
```

```python
from functools import partial

import jax
import jax.numpy as jnp
from jax import lax
from jax.experimental import pallas as pl
from jax.experimental.pallas import tpu as pltpu
from jax.sharding import PartitionSpec as P

HEAD_DIM = 64
SEQ_LEN = 512
NEGATIVE = -1e30
EPSILON = 1e-06
MESH = pl.DeviceIdType.MESH
F32 = jnp.float32
BF16 = jnp.bfloat16
VMEM_LIMIT = 62 << 20


def normalize(values, gain, shift):
    center = values - jnp.mean(values, -1, keepdims=True)
    spread = jnp.mean(center * center, -1, keepdims=True)
    return center * lax.rsqrt(spread + EPSILON) * gain + shift


def matmul(left, right):
    return jnp.dot(left, right, preferred_element_type=F32)


def column_sums(values):
    return jnp.sum(values.astype(F32), 0)


class Place:
    def __init__(self, bits):
        self.bits = bits
        self.dp = lax.axis_index("dp")
        self.head = lax.axis_index("head")
        self.mine = [lax.rem(self.dp // (1 << b), 2) for b in range(bits - 1)] + [self.head]

    def partner(self, bit):
        if bit == self.bits - 1:
            return (self.dp, 1 - self.head)
        return (self.dp + (1 - 2 * self.mine[bit]) * (1 << bit), self.head)

    def greet(self, bits):
        barrier = pltpu.get_barrier_semaphore()
        for bit in bits:
            pl.semaphore_signal(barrier, inc=1, device_id=self.partner(bit), device_id_type=MESH)
        pl.semaphore_wait(barrier, len(bits))


def shared_rows(bits):
    return 1, 2


def lane_iota(shape):
    return lax.broadcasted_iota(jnp.int32, shape, 1)


def first_lanes(shape):
    return lane_iota(shape) < HEAD_DIM


def pair_operands(q2, k2, length, parity):
    lanes = lane_iota(q2.shape)
    rows = lax.broadcasted_iota(jnp.int32, q2.shape, 0)
    mine = (lanes < HEAD_DIM) if parity == 0 else (lanes >= HEAD_DIM)
    spare = lanes == (HEAD_DIM if parity == 0 else 0)
    hidden = jnp.where(rows < length, 0.0, NEGATIVE)
    qa = jnp.where(mine, q2.astype(F32) * HEAD_DIM ** -0.5, jnp.where(spare, 1.0, 0.0)).astype(BF16)
    ka = jnp.where(mine, k2.astype(F32), jnp.where(spare, hidden, 0.0)).astype(BF16)
    return qa, ka


def nt(left, right):
    return lax.dot_general(left, right, (((1,), (1,)), ((), ())), preferred_element_type=F32)


def tn(left, right):
    return lax.dot_general(left, right, (((0,), (0,)), ((), ())), preferred_element_type=F32)


def attend_pair(q_ref, k_ref, v_ref, ctx_ref, lse_ref, pair, length):
    at = pl.ds(pl.multiple_of(pair * 128, 128), 128)
    q2, k2, v2 = q_ref[:, at], k_ref[:, at], v_ref[:, at]
    v2t = v2.T
    rows = lax.broadcasted_iota(jnp.int32, (128, SEQ_LEN), 0)
    parts = []
    for parity in range(2):
        qa, ka = pair_operands(q2, k2, length, parity)
        scores = nt(ka, qa)
        peak = jnp.max(scores, 0, keepdims=True)
        raised = jnp.exp(scores - peak)
        total = jnp.sum(raised, 0, keepdims=True)
        probs = (raised * (1.0 / total)).astype(BF16)
        parts.append(matmul(v2t, probs))
        lse_ref[pair, parity : parity + 1, :] = peak + jnp.log(total)
    joined = jnp.where(rows < HEAD_DIM, parts[0], parts[1])
    ctx_ref[:, at] = joined.T.astype(BF16)


def attention_forward(inputs, weights, biases, lengths, bits):
    rows, width = inputs.shape
    depth, half = weights[0].shape
    part = depth // 8
    pairs = half // 128
    kinds = 10

    def kernel(lengths_ref, x_ref, wq_ref, wk_ref, wv_ref, qb_ref, vb_ref, q_ref, k_ref, v_ref, ctx_ref, lse_ref,
               fq_ref, fk_ref, fv_ref, qb_got, vb_got, send, recv, bias_send, bias_recv):
        place = Place(bits)
        head = place.head
        bit_x, bit_z = shared_rows(bits)
        place.greet([0, bit_x, bit_z, bits - 1])
        length = lengths_ref[head]
        own_refs, full_refs = (wq_ref, wk_ref, wv_ref), (fq_ref, fk_ref, fv_ref)
        own = pl.ds(pl.multiple_of(head * half, half), half)
        other = pl.ds(pl.multiple_of((1 - head) * half, half), half)
        core, x, z = place.mine[0], place.mine[bit_x], place.mine[bit_z]

        def rows_of(at_x, at_z, lower=None):
            start = core * (4 * part) + (at_z * 2 + at_x) * part
            if lower is None:
                return pl.ds(pl.multiple_of(start, part), part)
            return pl.ds(pl.multiple_of(start + lower * (part // 2), part // 2), part // 2)

        started = {}

        def start(j, kind, source, where, bit):
            copy = pltpu.make_async_remote_copy(
                src_ref=source, dst_ref=full_refs[j].at[where], send_sem=send.at[j, kind], recv_sem=recv.at[j, kind],
                device_id=place.partner(bit), device_id_type=MESH)
            copy.start()
            started[j, kind] = copy

        bias_copies = [
            pltpu.make_async_remote_copy(
                src_ref=source, dst_ref=target, send_sem=bias_send.at[n], recv_sem=bias_recv.at[n],
                device_id=place.partner(bits - 1), device_id_type=MESH)
            for n, (source, target) in enumerate(((qb_ref, qb_got), (vb_ref, vb_got)))
        ]
        for j in range(3):
            mine = rows_of(x, z)
            start(j, 0, own_refs[j].at[mine, :], (mine, own), bits - 1)
        for copy in bias_copies:
            copy.start()

        def forward(j, kind, where, bit):
            start(j, kind, full_refs[j].at[where], where, bit)

        def stage_one(j):
            started[j, 0].wait_recv()
            where = (rows_of(x, z), other)
            forward(j, 1, where, bit_x)
            forward(j, 2, where, bit_z)
            forward(j, 5, where, 0)

        def stage_two(j):
            started[j, 1].wait_recv()
            forward(j, 4, (rows_of(1 - x, z, 1), other), bit_z)
            forward(j, 6, (rows_of(1 - x, z), other), 0)
            started[j, 2].wait_recv()
            forward(j, 3, (rows_of(x, 1 - z, 0), other), bit_x)
            forward(j, 7, (rows_of(x, 1 - z), other), 0)

        def stage_three(j):
            for kind, lower in ((3, 0), (4, 1)):
                started[j, kind].wait_recv()
                forward(j, kind + 5, (rows_of(1 - x, 1 - z, lower), other), 0)

        def stage_four(j):
            for kind in range(5, 10):
                started[j, kind].wait_recv()

        def project(j, where, bias):
            value = matmul(x_ref[...], full_refs[j][:, where])
            if bias is not None:
                value = value + bias[...].astype(F32).reshape(1, half)
            (q_ref, k_ref, v_ref)[j][:, where] = value.astype(BF16)

        for j in range(3):
            full_refs[j][:, own] = own_refs[j][...]
        project(0, own, qb_ref)
        project(1, own, None)
        project(2, own, vb_ref)

        def attend(pair):
            attend_pair(q_ref, k_ref, v_ref, ctx_ref, lse_ref, pair, length)

        stage_one(0)
        attend(head * pairs)
        stage_one(1)
        stage_two(0)
        attend(head * pairs + 1)
        stage_one(2)
        stage_two(1)
        stage_three(0)
        attend(head * pairs + 2)
        stage_two(2)
        stage_three(1)
        stage_three(2)
        for copy in bias_copies:
            copy.wait_recv()
        stage_four(0)
        project(0, other, qb_got)
        stage_four(1)
        project(1, other, None)
        stage_four(2)
        project(2, other, vb_got)

        def late(n, carry):
            attend((1 - head) * pairs + n)
            return carry

        lax.fori_loop(0, pairs, late, 0)
        for copy in started.values():
            copy.wait_send()
        for copy in bias_copies:
            copy.wait_send()

    vmem = pl.BlockSpec(memory_space=pltpu.VMEM)
    act = jax.ShapeDtypeStruct((rows, width), BF16)
    full = jax.ShapeDtypeStruct((depth, width), BF16)
    return pl.pallas_call(
        kernel,
        out_shape=[act] * 4 + [jax.ShapeDtypeStruct((2 * pairs, 2, rows), F32)] + [full] * 3,
        in_specs=[pl.BlockSpec(memory_space=pltpu.SMEM)] + [vmem] * 6,
        out_specs=[vmem] * 8,
        scratch_shapes=[pltpu.VMEM((half,), BF16)] * 2 + [pltpu.SemaphoreType.DMA((3, kinds))] * 2
        + [pltpu.SemaphoreType.DMA((2,))] * 2,
        compiler_params=pltpu.CompilerParams(collective_id=0, has_side_effects=True, vmem_limit_bytes=VMEM_LIMIT),
        name="attention_forward",
    )(lengths, inputs, *weights, *biases)


def gelu_parts(v):
    x = jnp.abs(v) * 0.7071067811865476
    t = 1.0 / (1.0 + 0.3275911 * x)
    bell = jnp.exp(-0.5 * (v * v))
    tail = 0.5 * bell * t * (
        0.254829592 + t * (-0.284496736 + t * (1.421413741 + t * (-1.453152027 + t * 1.061405429))))
    phi = jnp.where(v >= 0, 1.0 - tail, tail)
    return v * phi, phi + v * bell * 0.3989422804014327


ROW_BLOCK = 64


def over_rows(rows, step, carry):
    def one(n, kept):
        return step(pl.ds(pl.multiple_of(n * ROW_BLOCK, ROW_BLOCK), ROW_BLOCK), kept)

    return lax.fori_loop(0, rows // ROW_BLOCK, one, carry)


OUT_BIAS, FIRST_GAIN, FIRST_SHIFT, DOWN_BIAS, SECOND_GAIN, SECOND_SHIFT, POOL_BIAS, CLASS_BIAS, UP_BIAS = range(9)
QUERY_BIAS, VALUE_BIAS, LOSS = 6, 7, 12


def row_side(context, inputs, cotangent, vectors, class_turned, labels, out_weight, up_weight, down_weight, pool_weight,
             devices, head_size):
    rows, width = inputs.shape
    hidden = up_weight.shape[1]
    half = width // 2
    chunk = half
    chunks = hidden // chunk
    times = hidden // width
    dp_size = devices // head_size
    block = width // dp_size
    classes = class_turned.shape[0]
    per_width = width // 128

    def kernel(labels_ref, ctx_ref, x_ref, cls_in, ow_ref, v0, v1, v2, v3, v4, v5, v6, v7, v8, cot_hbm, up_hbm, down_hbm, pool_hbm,
               states_ref, gfirst_ref, gctx_ref, small_ref, fact_ref, logit_ref, up_out, down_out, out_out,
               cot, up_w, down_w, pool_w, first, low_ref, n1, r1, n2, r2, hid, slope, acc, gb_ref, ga_ref,
               frow, vec_ref, cls_ref, up_buf, down_buf, out_buf, load_sem, store_sem):
        loads = []
        for i, (source, target) in enumerate(
            ((up_hbm, up_w), (down_hbm, down_w), (pool_hbm, pool_w), (cot_hbm, cot))):
            load = pltpu.make_async_copy(source, target, load_sem.at[i])
            load.start()
            loads.append(load)

        for i, ref in enumerate((v0, v1, v2, v3, v4, v5, v6)):
            vec_ref[i : i + 1, :] = ref[...].astype(F32).reshape(1, width)
        vec_ref[CLASS_BIAS : CLASS_BIAS + 1, 0:classes] = v7[...].astype(F32).reshape(1, classes)
        wide_bias = v8[...].astype(F32).reshape(1, hidden)
        for t in range(times):
            vec_ref[UP_BIAS + t : UP_BIAS + t + 1, :] = wide_bias[:, t * width : (t + 1) * width]
        cls_ref[...] = jnp.zeros_like(cls_ref)
        cls_ref[0:classes, :] = cls_in[...]

        def vec(i):
            return vec_ref[i : i + 1, :]

        acc[...] = matmul(ctx_ref[...], ow_ref[...])

        def norm_one(at, carry):
            value = x_ref[at, :].astype(F32) + (acc[at, :] + vec(OUT_BIAS))
            center = value - jnp.mean(value, -1, keepdims=True)
            scale = lax.rsqrt(jnp.mean(center * center, -1, keepdims=True) + EPSILON)
            normal = center * scale
            out = normal * vec(FIRST_GAIN) + vec(FIRST_SHIFT)
            n1[at, :] = normal
            r1[at, :] = scale
            first[at, :] = out
            low_ref[at, :] = out.astype(BF16)
            acc[at, :] = jnp.zeros_like(out)
            return carry

        over_rows(rows, norm_one, 0)
        loads[0].wait()
        loads[1].wait()

        def forward(c, carry):
            at = pl.ds(pl.multiple_of(c * chunk, chunk), chunk)
            pre = matmul(low_ref[...], up_w[:, at]) + vec_ref[pl.ds(UP_BIAS + c // 2, 1), pl.ds(pl.multiple_of(lax.rem(c, 2) * half, half), half)]
            act, deriv = gelu_parts(pre)
            act = act.astype(BF16)
            hid[:, at] = act
            slope[:, at] = deriv
            acc[...] += matmul(act, down_w[at, :])
            return carry

        lax.fori_loop(0, chunks, forward, 0)

        def norm_two(at, carry):
            value = first[at, :] + (acc[at, :] + vec(DOWN_BIAS))
            center = value - jnp.mean(value, -1, keepdims=True)
            scale = lax.rsqrt(jnp.mean(center * center, -1, keepdims=True) + EPSILON)
            normal = center * scale
            n2[at, :] = normal
            r2[at, :] = scale
            states_ref[at, :] = (normal * vec(SECOND_GAIN) + vec(SECOND_SHIFT)).astype(BF16)
            return carry

        over_rows(rows, norm_two, 0)

        loads[2].wait()
        loads[3].wait()
        lead = states_ref[0:16, :]
        pooled = jnp.tanh(matmul(lead, pool_w[...]) + vec(POOL_BIAS))
        pooled_low = pooled.astype(BF16)
        logits = nt(pooled_low, cls_ref[...]) + vec_ref[CLASS_BIAS : CLASS_BIAS + 1, 0:128]
        lanes = lane_iota(logits.shape)
        logits = jnp.where(lanes < classes, logits, NEGATIVE)
        top = jnp.max(logits, -1, keepdims=True)
        norm = top + jnp.log(jnp.sum(jnp.exp(logits - top), -1, keepdims=True))
        target = jnp.where(lanes == labels_ref[0], 1.0, 0.0)
        loss = (norm - jnp.sum(jnp.where(lanes < classes, target * logits, 0.0), -1, keepdims=True)) / devices
        grad_logits = (jnp.where(lanes < classes, jnp.exp(logits - norm) - target, 0.0) / devices).astype(BF16)
        grad_pooled = (matmul(grad_logits, cls_ref[...]) * (1.0 - pooled * pooled)).astype(BF16)
        grad_lead = nt(grad_pooled, pool_w[...])
        logit_ref[...] = logits[0:1, 0:classes]
        frow[...] = jnp.zeros_like(frow)
        for k, value in enumerate((lead, grad_pooled, pooled_low)):
            wide = value.astype(F32)
            for j in range(per_width):
                frow[k * per_width + j : k * per_width + j + 1, :] = wide[0:1, j * 128 : (j + 1) * 128]
        frow[3 * per_width : 3 * per_width + 1, :] = grad_logits.astype(F32)[0:1, 0:128]
        fact_ref[...] = frow[...].astype(BF16)

        def back_two(at, sums):
            gain_sum, shift_sum, bias_sum = sums
            row = at.start + lax.broadcasted_iota(jnp.int32, (ROW_BLOCK, width), 0)
            grad = cot[at, :].astype(F32) + jnp.where(row == 0, grad_lead[0:1, :], 0.0)
            normal = n2[at, :]
            e = grad * vec(SECOND_GAIN)
            value = (e - jnp.mean(e, -1, keepdims=True) - normal * jnp.mean(e * normal, -1, keepdims=True)) * r2[at, :]
            rounded = value.astype(BF16)
            acc[at, :] = value
            gb_ref[at, :] = rounded
            return (gain_sum + jnp.sum(grad * normal, 0, keepdims=True), shift_sum + jnp.sum(grad, 0, keepdims=True),
                    bias_sum + jnp.sum(rounded.astype(F32), 0, keepdims=True))

        zero = jnp.zeros((1, width), F32)
        gain_sum, shift_sum, bias_sum = over_rows(rows, back_two, (zero, zero, zero))
        small_ref[...] = jnp.zeros_like(small_ref)
        small_ref[SECOND_GAIN : SECOND_GAIN + 1, :] = gain_sum
        small_ref[SECOND_SHIFT : SECOND_SHIFT + 1, :] = shift_sum
        small_ref[DOWN_BIAS : DOWN_BIAS + 1, :] = bias_sum
        small_ref[LOSS : LOSS + 1, :] = jnp.broadcast_to(loss[0:1, 0:1], (1, width))

        def stores_of(c):
            slot = lax.rem(c, 2)
            up = pltpu.make_async_copy(up_buf.at[slot], up_out.at[lax.rem(c, times), c // times], store_sem.at[0, slot])
            down = pltpu.make_async_copy(
                down_buf.at[slot], down_out.at[:, :, pl.ds(c * (chunk // (times * block)), chunk // (times * block))],
                store_sem.at[1, slot])
            return up, down

        def backward(c, carry):
            at = pl.ds(pl.multiple_of(c * chunk, chunk), chunk)
            slot = lax.rem(c, 2)
            grad = (nt(gb_ref[...], down_w[at, :]) * slope[:, at]).astype(BF16)
            small_ref[pl.ds(UP_BIAS + c // 2, 1), pl.ds(pl.multiple_of(lax.rem(c, 2) * half, half), half)] = jnp.sum(
                grad.astype(F32), 0, keepdims=True)

            @pl.when(c >= 2)
            def _():
                for copy in stores_of(c - 2):
                    copy.wait()

            up_buf[slot] = tn(low_ref[...], grad).astype(BF16).reshape(dp_size, block, half)
            wide = tn(hid[:, at], gb_ref[...]).astype(BF16).reshape(chunk // (times * block), times, block, width)
            for t in range(times):
                for h in range(2):
                    down_buf[slot, t, h] = wide[:, t, :, h * half : (h + 1) * half]
            for copy in stores_of(c):
                copy.start()
            acc[...] += nt(grad, up_w[:, at])
            return carry

        lax.fori_loop(0, chunks, backward, 0)

        def back_one(at, sums):
            gain_sum, shift_sum, bias_sum = sums
            grad = acc[at, :]
            normal = n1[at, :]
            e = grad * vec(FIRST_GAIN)
            value = (e - jnp.mean(e, -1, keepdims=True) - normal * jnp.mean(e * normal, -1, keepdims=True)) * r1[at, :]
            rounded = value.astype(BF16)
            gfirst_ref[at, :] = value
            ga_ref[at, :] = rounded
            return (gain_sum + jnp.sum(grad * normal, 0, keepdims=True), shift_sum + jnp.sum(grad, 0, keepdims=True),
                    bias_sum + jnp.sum(rounded.astype(F32), 0, keepdims=True))

        gain_sum, shift_sum, bias_sum = over_rows(rows, back_one, (zero, zero, zero))
        small_ref[FIRST_GAIN : FIRST_GAIN + 1, :] = gain_sum
        small_ref[FIRST_SHIFT : FIRST_SHIFT + 1, :] = shift_sum
        small_ref[OUT_BIAS : OUT_BIAS + 1, :] = bias_sum
        gctx_ref[...] = nt(ga_ref[...], ow_ref[...]).astype(BF16)
        grad_out = tn(ctx_ref[...], ga_ref[...]).astype(BF16).reshape(dp_size, block, width)
        for h in range(2):
            out_buf[h] = grad_out[:, :, h * half : (h + 1) * half]
        out_copy = pltpu.make_async_copy(out_buf, out_out, store_sem.at[2, 0])
        out_copy.start()
        for c in range(chunks - 2, chunks):
            for copy in stores_of(c):
                copy.wait()
        out_copy.wait()

    vmem = pl.BlockSpec(memory_space=pltpu.VMEM)
    anywhere = pl.BlockSpec(memory_space=pl.ANY)
    act_low, act = jax.ShapeDtypeStruct((rows, width), BF16), jax.ShapeDtypeStruct((rows, width), F32)
    pieces = jax.ShapeDtypeStruct((times, 2, dp_size, block, half), BF16)
    fact_rows = -(-(3 * per_width + 1) // 16) * 16
    return pl.pallas_call(
        kernel,
        out_shape=[
            act_low, act, act_low, jax.ShapeDtypeStruct((16, width), F32), jax.ShapeDtypeStruct((fact_rows, 128), BF16),
            jax.ShapeDtypeStruct((1, classes), F32), pieces, pieces,
            jax.ShapeDtypeStruct((2, dp_size, block, half), BF16),
        ],
        in_specs=[pl.BlockSpec(memory_space=pltpu.SMEM)] + [vmem] * 13 + [anywhere] * 4,
        out_specs=[vmem] * 6 + [anywhere] * 3,
        scratch_shapes=[
            pltpu.VMEM((rows, width), BF16),
            pltpu.VMEM((width, hidden), BF16),
            pltpu.VMEM((hidden, width), BF16),
            pltpu.VMEM((width, width), BF16),
            pltpu.VMEM((rows, width), F32),
            pltpu.VMEM((rows, width), BF16),
            pltpu.VMEM((rows, width), F32),
            pltpu.VMEM((rows, 1), F32),
            pltpu.VMEM((rows, width), F32),
            pltpu.VMEM((rows, 1), F32),
            pltpu.VMEM((rows, hidden), BF16),
            pltpu.VMEM((rows, hidden), F32),
            pltpu.VMEM((rows, width), F32),
            pltpu.VMEM((rows, width), BF16),
            pltpu.VMEM((rows, width), BF16),
            pltpu.VMEM((fact_rows, 128), F32),
            pltpu.VMEM((16, width), F32),
            pltpu.VMEM((128, width), BF16),
            pltpu.VMEM((2, dp_size, block, half), BF16),
            pltpu.VMEM((2, times, 2, chunk // (times * block), block, half), BF16),
            pltpu.VMEM((2, dp_size, block, half), BF16),
            pltpu.SemaphoreType.DMA((4,)),
            pltpu.SemaphoreType.DMA((3, 2)),
        ],
        compiler_params=pltpu.CompilerParams(vmem_limit_bytes=VMEM_LIMIT),
        name="row_side",
    )(labels, context, inputs, class_turned, out_weight, *vectors, cotangent, up_weight, down_weight, pool_weight)


def orders(bits):
    head = bits - 1
    rest = list(range(2, head))
    return [[0, 1, head] + rest, [0, head, 1] + rest, [0] + rest[:1] + [1, head] + rest[1:]]


def attention_backward(queries, keys, values, grad_context, inputs, full, grad_first, log_totals, lengths, up_pieces,
                       down_pieces, out_piece, small, factors, bits):
    times, _, dp_size, block, half = up_pieces.shape
    rows, width = inputs.shape
    plans = orders(bits)
    group = len(plans)
    count = 2 * times + 4
    groups = count // group
    grid_dims = (2,) * bits
    stages = bits
    head = bits - 1
    small_order = [0, 1, head] + list(range(2, head))
    pairs = width // 128

    def kernel(lengths_ref, q_ref, k_ref, v_ref, gc_ref, x_ref, wq_ref, wk_ref, wv_ref, gfirst_ref, lse_ref, small_in,
               factor_in, up_in, down_in, out_in, grad_ref, sums_ref, small_out, factor_out, held, *rest):
        got = rest[:stages]
        (dq_ref, dk_ref, dv_ref, small_buf, small_got, load_sem, send, recv, side_send, side_recv) = rest[stages:]
        place = Place(bits)
        loads = []
        sources = [up_in.at[i] for i in range(times)] + [down_in.at[i] for i in range(times)] + [out_in]
        for i, source in enumerate(sources):
            load = pltpu.make_async_copy(source, held.at[i], load_sem.at[i])
            load.start()
            loads.append(load)
        slot = sum(place.mine[bit] * (1 << k) for k, bit in enumerate(small_order))
        factor_out[slot] = factor_in[...]
        place.greet(range(bits))
        length = lengths_ref[place.head]

        def index(i, done, fixed, free_bits):
            out = [i]
            for bit in reversed(range(bits)):
                if bit in fixed:
                    out.append(fixed[bit])
                elif bit in done:
                    out.append(place.mine[bit])
                else:
                    out.append(free_bits[bit] if free_bits is not None else slice(None))
            return tuple(out)

        started = {}

        def send_piece(i, s):
            plan = plans[i % group]
            bit = plan[s]
            source = held.at[index(i, plan[:s], {bit: 1 - place.mine[bit]}, None)]
            copy = pltpu.make_async_remote_copy(
                src_ref=source, dst_ref=got[s].at[i], send_sem=send.at[i, s], recv_sem=recv.at[i, s],
                device_id=place.partner(bit), device_id_type=MESH)
            copy.start()
            started[i, s] = copy

        def add_piece(i, s):
            started[i, s].wait_recv()
            done = plans[i % group][: s + 1]
            free = [bit for bit in reversed(range(bits)) if bit not in done]
            if not free:
                where = index(i, done, {}, None)
                sums_ref[i] = held[where].astype(F32) + got[s][i].astype(F32)
                return

            def step(n, carry):
                free_bits = {bit: lax.rem(n // (1 << (len(free) - 1 - k)), 2) for k, bit in enumerate(free)}
                where = index(i, done, {}, free_bits)
                there = (i,) + tuple(free_bits[bit] for bit in free)
                held[where] = (held[where].astype(F32) + got[s][there].astype(F32)).astype(BF16)
                return carry

            lax.fori_loop(0, 1 << len(free), step, 0)

        def advance(g, s):
            for i in range(g * group, (g + 1) * group):
                if s == 0:
                    if i < len(loads):
                        loads[i].wait()
                else:
                    add_piece(i, s - 1)
                if s < stages:
                    send_piece(i, s)

        def side_send_stage(s):
            partner = place.partner(small_order[s])
            copies = []
            start = (slot // (1 << s)) * (1 << s)
            rows_at = pl.ds(start, 1 << s)
            for k, (source, target) in enumerate(
                ((small_buf.at[s], small_got.at[s]), (factor_out.at[rows_at], factor_out.at[rows_at]))
            ):
                copy = pltpu.make_async_remote_copy(
                    src_ref=source, dst_ref=target, send_sem=side_send.at[k, s], recv_sem=side_recv.at[k, s],
                    device_id=partner, device_id_type=MESH)
                copy.start()
                copies.append(copy)
            started["side", s] = copies

        def side_add_stage(s):
            for copy in started["side", s]:
                copy.wait_recv()
            total = small_buf[s] + small_got[s]
            if s < stages - 1:
                small_buf[s + 1] = total
            else:
                small_out[...] = total

        lanes_row = lax.broadcasted_iota(jnp.int32, (128, rows), 0)
        lanes = lane_iota((rows, 128))

        def attend(pair, carry):
            at = pl.ds(pl.multiple_of(pair * 128, 128), 128)
            q2, k2, v2, g2 = q_ref[:, at], k_ref[:, at], v_ref[:, at], gc_ref[:, at]
            k2t = k2.T
            parts = []
            for parity in range(2):
                qa, ka = pair_operands(q2, k2, length, parity)
                mine = (lanes < HEAD_DIM) if parity == 0 else (lanes >= HEAD_DIM)
                va = jnp.where(mine, v2.astype(F32), 0.0).astype(BF16)
                probs = jnp.exp(nt(ka, qa) - lse_ref[pair, parity : parity + 1, :])
                grad_v = matmul(probs.astype(BF16), g2)
                grad_probs = nt(va, g2)
                inner = jnp.sum(probs * grad_probs, 0, keepdims=True)
                grad_scores = (probs * (grad_probs - inner)).astype(BF16)
                parts.append((grad_v, matmul(grad_scores, qa), matmul(k2t, grad_scores)))
            first = lanes < HEAD_DIM
            dv_ref[:, at] = jnp.where(first, parts[0][0], parts[1][0]).astype(BF16)
            dk_ref[:, at] = jnp.where(first, parts[0][1], parts[1][1]).astype(BF16)
            turned = jnp.where(lanes_row < HEAD_DIM, parts[0][2], parts[1][2]) * HEAD_DIM ** -0.5
            dq_ref[:, at] = turned.T.astype(BF16)
            return carry

        ready = groups - 1
        for g in range(ready):
            advance(g, 0)
        lax.fori_loop(0, 1, attend, 0)
        advance(0, 1)
        advance(1, 1)
        lax.fori_loop(1, 3, attend, 0)
        advance(0, 2)
        advance(2, 1)
        lax.fori_loop(3, 5, attend, 0)
        advance(0, 3)
        advance(1, 2)
        lax.fori_loop(5, pairs, attend, 0)
        advance(0, 4)

        for j, ref in enumerate((dq_ref, dk_ref, dv_ref)):
            for h in range(2):
                value = tn(x_ref[...], ref[:, h * half : (h + 1) * half]).astype(BF16)
                shape = (2,) * (bits - 1) + (block, half)
                held[group * ready + j, h] = value.reshape(shape)
        advance(ready, 0)

        def total_of(ref):
            return jnp.sum(ref[...].astype(F32), 0, keepdims=True)

        small_buf[0] = small_in[...]
        small_buf[0, QUERY_BIAS : QUERY_BIAS + 1, :] = total_of(dq_ref)
        small_buf[0, VALUE_BIAS : VALUE_BIAS + 1, :] = total_of(dv_ref)
        side_send_stage(0)
        advance(ready, 1)
        advance(1, 3)
        advance(2, 2)
        side_add_stage(0)
        side_send_stage(1)
        grad_ref[...] = (gfirst_ref[...] + nt(dq_ref[...], wq_ref[...]) + nt(dk_ref[...], wk_ref[...])
                         + nt(dv_ref[...], wv_ref[...])).astype(BF16)
        todo = [(0, 5), (1, 4), (2, 3), (3, 2), (1, 5), (2, 4), (3, 3), (2, 5), (3, 4), (3, 5)]
        for n, (g, s) in enumerate(todo):
            advance(g, s)
            if n in (1, 3, 5, 7):
                k = 1 + n // 2
                side_add_stage(k)
                if k + 1 < stages:
                    side_send_stage(k + 1)
        for key, copy in started.items():
            for one in copy if isinstance(copy, list) else [copy]:
                one.wait_send()

    vmem = pl.BlockSpec(memory_space=pltpu.VMEM)
    anywhere = pl.BlockSpec(memory_space=pl.ANY)
    devices = 1 << bits
    pieces = [p.reshape((-1,) + grid_dims + (block, half)) for p in (up_pieces, down_pieces)]
    return pl.pallas_call(
        kernel,
        out_shape=[
            jax.ShapeDtypeStruct((rows, width), BF16), jax.ShapeDtypeStruct((count, block, half), F32),
            jax.ShapeDtypeStruct(small.shape, F32), jax.ShapeDtypeStruct((devices,) + factors.shape, factors.dtype),
        ],
        in_specs=[pl.BlockSpec(memory_space=pltpu.SMEM)] + [vmem] * 12 + [anywhere] * 3,
        out_specs=[vmem] * 4,
        scratch_shapes=[pltpu.VMEM((count,) + grid_dims + (block, half), BF16)]
        + [pltpu.VMEM((count,) + (2,) * (stages - 1 - s) + (block, half), BF16) for s in range(stages)]
        + [pltpu.VMEM((rows, width), BF16)] * 3
        + [
            pltpu.VMEM((stages,) + small.shape, F32),
            pltpu.VMEM((stages,) + small.shape, F32),
            pltpu.SemaphoreType.DMA((count - 3,)),
            pltpu.SemaphoreType.DMA((count, stages)),
            pltpu.SemaphoreType.DMA((count, stages)),
            pltpu.SemaphoreType.DMA((2, stages)),
            pltpu.SemaphoreType.DMA((2, stages)),
        ],
        compiler_params=pltpu.CompilerParams(collective_id=1, has_side_effects=True, vmem_limit_bytes=VMEM_LIMIT),
        name="attention_backward",
    )(lengths, queries, keys, values, grad_context, inputs, *full, grad_first, log_totals, small, factors,
      *pieces, out_piece.reshape(grid_dims + (block, half)))


def spread(sums, small, gathered, classes, head_size):
    count, block, half = sums.shape
    devices = gathered.shape[0]
    width = small.shape[1]
    times = (count - 4) // 2
    lanes = width // 128

    def kernel(sums_ref, small_ref, got_ref, up, down, out, query, key, value, pool, query_bias, value_bias, out_bias,
               first_gain, first_shift, up_bias, down_bias, second_gain, second_shift, pool_bias, class_weight,
               class_bias, loss, left, right):
        dp, head = lax.axis_index("dp"), lax.axis_index("head")
        for t in range(times):
            up[:, t * half : (t + 1) * half] = sums_ref[t]
            down[t * block : (t + 1) * block, :] = sums_ref[times + t]
        for k, ref in enumerate((out, query, key, value)):
            ref[...] = sums_ref[2 * times + k]
        got = got_ref[...].astype(F32)

        def wide(k):
            return jnp.concatenate([got[:, k * lanes + j, :] for j in range(lanes)], 1)

        lead, grad_pooled, pooled = wide(0), wide(1), wide(2)
        grad_logits = got[:, 3 * lanes, :]
        left[...] = lead.T
        right[...] = grad_pooled
        pool[...] = matmul(
            left[pl.ds(pl.multiple_of(dp * block, 8), block), :].astype(BF16),
            right[:, pl.ds(pl.multiple_of(head * half, half), half)].astype(BF16))
        pool_bias[...] = jnp.sum(grad_pooled, 0)
        class_weight[...] = tn(grad_logits.astype(BF16), pooled.astype(BF16))[0:classes, :]
        class_bias[...] = jnp.sum(grad_logits, 0, keepdims=True)[:, 0:classes].reshape(classes)
        at = pl.ds(pl.multiple_of(head * half, half), half)
        query_bias[...] = small_ref[QUERY_BIAS : QUERY_BIAS + 1, at].reshape(half)
        value_bias[...] = small_ref[VALUE_BIAS : VALUE_BIAS + 1, at].reshape(half)
        for ref, row in ((out_bias, OUT_BIAS), (first_gain, FIRST_GAIN), (first_shift, FIRST_SHIFT),
                         (down_bias, DOWN_BIAS), (second_gain, SECOND_GAIN), (second_shift, SECOND_SHIFT)):
            ref[...] = small_ref[row, :]
        up_bias[...] = jnp.concatenate(
            [small_ref[UP_BIAS + t : UP_BIAS + t + 1, :] for t in range(times)], 1).reshape(times * width)
        loss[()] = small_ref[LOSS, 0]

    def f32(*shape):
        return jax.ShapeDtypeStruct(shape, F32)

    square = f32(block, half)
    row = f32(width)
    return pl.pallas_call(
        kernel,
        out_shape=[
            f32(block, times * half), f32(times * block, half), square, square, square, square, square, f32(half),
            f32(half), row, row, row, f32(times * width), row, row, row, row, f32(classes, width),
            f32(classes), f32(),
        ],
        in_specs=[pl.BlockSpec(memory_space=pltpu.VMEM)] * 3,
        out_specs=[pl.BlockSpec(memory_space=pltpu.VMEM)] * 19 + [pl.BlockSpec(memory_space=pltpu.SMEM)],
        scratch_shapes=[pltpu.VMEM((width, devices), F32), pltpu.VMEM((devices, width), F32)],
        compiler_params=pltpu.CompilerParams(vmem_limit_bytes=VMEM_LIMIT),
        name="spread",
    )(sums, small, gathered)


def plain_body(
    inputs, lengths, labels, state_cotangent, query_weight, query_bias, key_weight, value_weight, value_bias,
    out_weight, out_bias, first_gain, first_shift, up_weight, up_bias, down_weight, down_bias, second_gain,
    second_shift, pool_weight, pool_bias, class_weight, class_bias,
):
    scale = HEAD_DIM ** (-0.5)
    dp_size, head_size = lax.axis_size("dp"), lax.axis_size("head")
    dp_at, head_at = lax.axis_index("dp"), lax.axis_index("head")
    devices = dp_size * head_size
    width = inputs.shape[1]
    block_columns = width // head_size
    row_seqs = labels.shape[0]
    assert row_seqs == 1 and inputs.shape[0] == SEQ_LEN
    length = lax.dynamic_index_in_dim(lengths, head_at, keepdims=False)

    weights = [query_weight, key_weight, value_weight]
    full = [lax.all_gather(w, "head", axis=1, tiled=True) for w in weights]
    biases = lax.all_gather(jnp.stack([query_bias, value_bias]), "head", axis=1, tiled=True)
    query_bias, value_bias = biases[0], biases[1]
    wq, wk, wv = full
    head_count = width // HEAD_DIM

    def heads(matrix):
        return matrix.reshape(SEQ_LEN, head_count, HEAD_DIM)

    queries = (matmul(inputs, wq) + query_bias).astype(BF16)
    keys_low = matmul(inputs, wk).astype(BF16)
    values_low = (matmul(inputs, wv) + value_bias).astype(BF16)
    visible = lax.broadcasted_iota(jnp.int32, (1, 1, SEQ_LEN), 2) < length

    def scores_of():
        raw = jnp.einsum("qhd,khd->hqk", heads(queries), heads(keys_low), preferred_element_type=F32) * scale
        return jnp.where(visible, raw, NEGATIVE)

    scores = scores_of()
    peak = jnp.max(scores, -1, keepdims=True)
    raised = jnp.exp(scores - peak)
    denominator = jnp.sum(raised, -1, keepdims=True)
    probs = raised / denominator
    log_total = peak + jnp.log(denominator)
    context = jnp.einsum("hqk,khd->qhd", probs.astype(BF16), heads(values_low), preferred_element_type=F32)
    context_rows = context.astype(BF16).reshape(SEQ_LEN, width)
    attended = matmul(context_rows, out_weight) + out_bias
    first_out, first_back = jax.vjp(
        normalize, inputs.astype(F32) + attended, first_gain.astype(F32), first_shift.astype(F32))
    first_low = first_out.astype(BF16)
    hidden_pre = matmul(first_low, up_weight) + up_bias
    hidden_act, gelu_back = jax.vjp(partial(jax.nn.gelu, approximate=False), hidden_pre)
    hidden_low = hidden_act.astype(BF16)
    branch = matmul(hidden_low, down_weight) + down_bias
    normed, second_back = jax.vjp(normalize, first_out + branch, second_gain.astype(F32), second_shift.astype(F32))
    leading_low = normed.reshape(row_seqs, SEQ_LEN, -1)[:, 0].astype(BF16)
    pooled = jnp.tanh(matmul(leading_low, pool_weight) + pool_bias)
    pooled_low = pooled.astype(BF16)
    logits = matmul(pooled_low, class_weight) + class_bias
    classes = lax.broadcasted_iota(jnp.int32, logits.shape, 1)
    target = (classes == labels[:, None]).astype(F32)
    log_norm = jax.nn.logsumexp(logits, axis=-1)
    loss_part = jnp.sum(log_norm - jnp.sum(target * logits, -1)) / devices
    grad_logits = ((jnp.exp(logits - log_norm[:, None]) - target) / devices).astype(BF16)
    grad_class_weight = matmul(pooled_low.T, grad_logits)
    grad_class_bias = column_sums(grad_logits)
    grad_pooled = (matmul(grad_logits, class_weight.T) * (1.0 - pooled * pooled)).astype(BF16)
    grad_pool_bias = column_sums(grad_pooled)
    grad_leading = matmul(grad_pooled, pool_weight.T)
    grad_normed = state_cotangent.astype(F32).reshape(row_seqs, SEQ_LEN, -1)
    grad_normed = grad_normed.at[:, 0].add(grad_leading).reshape(normed.shape)
    grad_second, grad_second_gain, grad_second_shift = second_back(grad_normed)
    grad_branch = grad_second.astype(BF16)
    grad_down_weight = matmul(hidden_low.T, grad_branch)
    grad_down_bias = column_sums(grad_branch)
    grad_hidden = gelu_back(matmul(grad_branch, down_weight.T))[0].astype(BF16)
    grad_up_weight = matmul(first_low.T, grad_hidden)
    grad_up_bias = column_sums(grad_hidden)
    grad_first_out = grad_second + matmul(grad_hidden, up_weight.T)
    grad_first, grad_first_gain, grad_first_shift = first_back(grad_first_out)
    grad_attended = grad_first.astype(BF16)
    grad_out_weight = matmul(context_rows.T, grad_attended)
    grad_out_bias = column_sums(grad_attended)
    grad_context = heads(matmul(grad_attended, out_weight.T).astype(BF16))
    probs_again = jnp.exp(scores_of() - log_total)
    grad_values = jnp.einsum(
        "hqk,qhd->khd", probs_again.astype(BF16), grad_context, preferred_element_type=F32).astype(BF16)
    grad_probs = jnp.einsum("qhd,khd->hqk", grad_context, heads(values_low), preferred_element_type=F32)
    grad_scores = probs_again * (grad_probs - jnp.sum(probs_again * grad_probs, -1, keepdims=True))
    grad_scores = grad_scores.astype(BF16)
    grad_queries = (
        jnp.einsum("hqk,khd->qhd", grad_scores, heads(keys_low), preferred_element_type=F32) * scale).astype(BF16)
    grad_keys = (
        jnp.einsum("hqk,qhd->khd", grad_scores, heads(queries), preferred_element_type=F32) * scale).astype(BF16)
    grad_queries = grad_queries.reshape(SEQ_LEN, width)
    grad_keys = grad_keys.reshape(SEQ_LEN, width)
    grad_values = grad_values.reshape(SEQ_LEN, width)
    grad_query_weight = matmul(inputs.T, grad_queries)
    grad_key_weight = matmul(inputs.T, grad_keys)
    grad_value_weight = matmul(inputs.T, grad_values)
    input_grad = (
        grad_first + matmul(grad_queries, wq.T) + matmul(grad_keys, wk.T) + matmul(grad_values, wv.T)).astype(BF16)

    small_parts = (
        grad_out_bias, grad_first_gain, grad_first_shift, grad_up_bias, grad_down_bias, grad_second_gain,
        grad_second_shift, grad_pool_bias, column_sums(grad_queries), column_sums(grad_values),
        grad_class_weight.reshape(-1), grad_class_bias, loss_part.reshape(1),
    )
    grads = (grad_up_weight, grad_down_weight, grad_out_weight, grad_query_weight, grad_key_weight, grad_value_weight)
    grads = grads + (matmul(leading_low.T, grad_pooled),)

    def scatter(matrix):
        part = lax.psum_scatter(matrix, "dp", scatter_dimension=0, tiled=True)
        return lax.psum_scatter(part.astype(BF16), "head", scatter_dimension=1, tiled=True).astype(F32)

    up_total, down_total, out_total, query_total, key_total, value_total, pool_total = map(scatter, grads)
    totals = lax.psum(small_parts, ("dp", "head"))
    (
        out_bias_total, first_gain_total, first_shift_total, up_bias_total, down_bias_total, second_gain_total,
        second_shift_total, pool_bias_total, query_bias_total, value_bias_total, class_weight_total,
        class_bias_total, loss,
    ) = totals
    query_bias_total = lax.dynamic_slice_in_dim(query_bias_total, head_at * block_columns, block_columns)
    value_bias_total = lax.dynamic_slice_in_dim(value_bias_total, head_at * block_columns, block_columns)
    return (
        normed.astype(BF16), input_grad, logits, loss.reshape(()), query_total, query_bias_total, key_total,
        value_total, value_bias_total, out_total, out_bias_total, first_gain_total, first_shift_total, up_total,
        up_bias_total, down_total, down_bias_total, second_gain_total, second_shift_total, pool_total,
        pool_bias_total, class_weight_total.reshape(class_weight.shape), class_bias_total,
    )


def body(*args):
    (
        inputs, lengths, labels, state_cotangent, query_weight, query_bias, key_weight, value_weight, value_bias,
        out_weight, out_bias, first_gain, first_shift, up_weight, up_bias, down_weight, down_bias, second_gain,
        second_shift, pool_weight, pool_bias, class_weight, class_bias,
    ) = args
    dp_size, head_size = lax.axis_size("dp"), lax.axis_size("head")
    devices = dp_size * head_size
    bits = devices.bit_length() - 1
    rows, width = inputs.shape
    hidden = up_weight.shape[1]
    classes = class_weight.shape[1]
    times = hidden // width
    direct = (
        (width // dp_size) % 16 == 0 and head_size == 2 and bits == 5 and times == 4 and rows == SEQ_LEN
        and labels.shape[0] == 1
    )
    if not direct:
        return plain_body(*args)

    vectors = (out_bias, first_gain, first_shift, down_bias, second_gain, second_shift, pool_bias, class_bias, up_bias)
    queries, keys, values, context, log_totals, *full = attention_forward(
        inputs, [query_weight, key_weight, value_weight], [query_bias, value_bias], lengths, bits)
    states, grad_first, grad_context, small, factors, logits, up_pieces, down_pieces, out_piece = row_side(
        context, inputs, state_cotangent, vectors, class_weight.T, labels, out_weight, up_weight, down_weight, pool_weight,
        devices, head_size)
    input_grad, sums, small_total, gathered = attention_backward(
        queries, keys, values, grad_context, inputs, full, grad_first, log_totals, lengths, up_pieces, down_pieces,
        out_piece, small, factors, bits)
    (
        up, down, out, query, key, value, pool, query_sum, value_sum, out_sum, first_gain_sum, first_shift_sum, up_sum,
        down_sum, second_gain_sum, second_shift_sum, pool_sum, class_sum, class_bias_sum, loss,
    ) = spread(sums, small_total, gathered, classes, head_size)

    return (
        states, input_grad, logits, loss, query, query_sum, key, value, value_sum, out, out_sum, first_gain_sum,
        first_shift_sum, up, up_sum, down, down_sum, second_gain_sum, second_shift_sum, pool, pool_sum, class_sum.T,
        class_bias_sum,
    )


def solution(mesh):
    rows, column, both = P(("dp", "head"), None), P(None, "head"), P("dp", "head")
    one, none = P("head"), P()
    return jax.shard_map(
        body,
        mesh=mesh,
        in_specs=(rows, P("dp"), P(("dp", "head")), rows, column, one, column, column, one) + (none,) * 14,
        out_specs=(
            rows, rows, rows, none, both, one, both, both, one, both, none, none, none, both, none, both, none,
            none, none, both, none, none, none,
        ),
        check_vma=False,
    )
```

```python
from functools import partial

import jax
import jax.numpy as jnp
from jax import lax
from jax.experimental import pallas as pl
from jax.experimental.pallas import tpu as pltpu
from jax.sharding import PartitionSpec as P

HEAD_DIM = 64
SEQ_LEN = 512
NEGATIVE = -1e30
EPSILON = 1e-06
MESH = pl.DeviceIdType.MESH
F32 = jnp.float32
BF16 = jnp.bfloat16
VMEM_LIMIT = 67_000_000


def normalize(values, gain, shift):
    center = values - jnp.mean(values, -1, keepdims=True)
    spread = jnp.mean(center * center, -1, keepdims=True)
    return center * lax.rsqrt(spread + EPSILON) * gain + shift


def matmul(left, right):
    return jnp.dot(left, right, preferred_element_type=F32)


def column_sums(values):
    return jnp.sum(values.astype(F32), 0)


class Place:
    def __init__(self, bits):
        self.bits = bits
        self.dp = lax.axis_index("dp")
        self.head = lax.axis_index("head")
        self.mine = [lax.rem(self.dp // (1 << b), 2) for b in range(bits - 1)] + [self.head]

    def partner(self, bit):
        if bit == self.bits - 1:
            return (self.dp, 1 - self.head)
        return (self.dp + (1 - 2 * self.mine[bit]) * (1 << bit), self.head)

    def greet(self, bits):
        barrier = pltpu.get_barrier_semaphore()
        for bit in bits:
            pl.semaphore_signal(barrier, inc=1, device_id=self.partner(bit), device_id_type=MESH)
        pl.semaphore_wait(barrier, len(bits))


def shared_rows(bits):
    return 1, 2


def lane_iota(shape):
    return lax.broadcasted_iota(jnp.int32, shape, 1)


def first_lanes(shape):
    return lane_iota(shape) < HEAD_DIM


def pair_operands(q2, k2, length, parity):
    lanes = lane_iota(q2.shape)
    rows = lax.broadcasted_iota(jnp.int32, q2.shape, 0)
    mine = (lanes < HEAD_DIM) if parity == 0 else (lanes >= HEAD_DIM)
    spare = lanes == (HEAD_DIM if parity == 0 else 0)
    hidden = jnp.where(rows < length, 0.0, NEGATIVE)
    qa = jnp.where(mine, q2.astype(F32) * HEAD_DIM ** -0.5, jnp.where(spare, 1.0, 0.0)).astype(BF16)
    ka = jnp.where(mine, k2.astype(F32), jnp.where(spare, hidden, 0.0)).astype(BF16)
    return qa, ka


def nt(left, right):
    return lax.dot_general(left, right, (((1,), (1,)), ((), ())), preferred_element_type=F32)


def tn(left, right):
    return lax.dot_general(left, right, (((0,), (0,)), ((), ())), preferred_element_type=F32)


def attend_pair(q_ref, k_ref, v_ref, ctx_ref, lse_ref, pair, length):
    at = pl.ds(pl.multiple_of(pair * 128, 128), 128)
    q2, k2, v2 = q_ref[:, at], k_ref[:, at], v_ref[:, at]
    v2t = v2.T
    rows = lax.broadcasted_iota(jnp.int32, (128, SEQ_LEN), 0)
    parts = []
    for parity in range(2):
        qa, ka = pair_operands(q2, k2, length, parity)
        scores = nt(ka, qa)
        peak = jnp.max(scores, 0, keepdims=True)
        raised = jnp.exp(scores - peak)
        total = jnp.sum(raised, 0, keepdims=True)
        probs = (raised * (1.0 / total)).astype(BF16)
        parts.append(matmul(v2t, probs))
        lse_ref[pair, parity : parity + 1, :] = peak + jnp.log(total)
    joined = jnp.where(rows < HEAD_DIM, parts[0], parts[1])
    ctx_ref[:, at] = joined.T.astype(BF16)


def attention_forward(inputs, weights, biases, lengths, bits):
    rows, width = inputs.shape
    depth, half = weights[0].shape
    part = depth // 8
    pairs = half // 128
    kinds = 10

    def kernel(lengths_ref, x_ref, wq_ref, wk_ref, wv_ref, qb_ref, vb_ref, q_ref, k_ref, v_ref, ctx_ref, lse_ref,
               fq_ref, fk_ref, fv_ref, qb_got, vb_got, send, recv, bias_send, bias_recv):
        place = Place(bits)
        head = place.head
        bit_x, bit_z = shared_rows(bits)
        place.greet([0, bit_x, bit_z, bits - 1])
        length = lengths_ref[head]
        own_refs, full_refs = (wq_ref, wk_ref, wv_ref), (fq_ref, fk_ref, fv_ref)
        own = pl.ds(pl.multiple_of(head * half, half), half)
        other = pl.ds(pl.multiple_of((1 - head) * half, half), half)
        core, x, z = place.mine[0], place.mine[bit_x], place.mine[bit_z]

        def rows_of(at_x, at_z, lower=None):
            start = core * (4 * part) + (at_z * 2 + at_x) * part
            if lower is None:
                return pl.ds(pl.multiple_of(start, part), part)
            return pl.ds(pl.multiple_of(start + lower * (part // 2), part // 2), part // 2)

        started = {}

        def start(j, kind, source, where, bit):
            copy = pltpu.make_async_remote_copy(
                src_ref=source, dst_ref=full_refs[j].at[where], send_sem=send.at[j, kind], recv_sem=recv.at[j, kind],
                device_id=place.partner(bit), device_id_type=MESH)
            copy.start()
            started[j, kind] = copy

        bias_copies = [
            pltpu.make_async_remote_copy(
                src_ref=source, dst_ref=target, send_sem=bias_send.at[n], recv_sem=bias_recv.at[n],
                device_id=place.partner(bits - 1), device_id_type=MESH)
            for n, (source, target) in enumerate(((qb_ref, qb_got), (vb_ref, vb_got)))
        ]
        for j in range(3):
            mine = rows_of(x, z)
            start(j, 0, own_refs[j].at[mine, :], (mine, own), bits - 1)
        for copy in bias_copies:
            copy.start()

        def forward(j, kind, where, bit):
            start(j, kind, full_refs[j].at[where], where, bit)

        def stage_one(j):
            started[j, 0].wait_recv()
            where = (rows_of(x, z), other)
            forward(j, 1, where, bit_x)
            forward(j, 2, where, bit_z)
            forward(j, 5, where, 0)

        def stage_two(j):
            started[j, 1].wait_recv()
            forward(j, 4, (rows_of(1 - x, z, 1), other), bit_z)
            forward(j, 6, (rows_of(1 - x, z), other), 0)
            started[j, 2].wait_recv()
            forward(j, 3, (rows_of(x, 1 - z, 0), other), bit_x)
            forward(j, 7, (rows_of(x, 1 - z), other), 0)

        def stage_three(j):
            for kind, lower in ((3, 0), (4, 1)):
                started[j, kind].wait_recv()
                forward(j, kind + 5, (rows_of(1 - x, 1 - z, lower), other), 0)

        def stage_four(j):
            for kind in range(5, 10):
                started[j, kind].wait_recv()

        def project(j, where, bias):
            value = matmul(x_ref[...], full_refs[j][:, where])
            if bias is not None:
                value = value + bias[...].astype(F32).reshape(1, half)
            (q_ref, k_ref, v_ref)[j][:, where] = value.astype(BF16)

        for j in range(3):
            full_refs[j][:, own] = own_refs[j][...]
        project(0, own, qb_ref)
        project(1, own, None)
        project(2, own, vb_ref)

        def attend(pair):
            attend_pair(q_ref, k_ref, v_ref, ctx_ref, lse_ref, pair, length)

        stage_one(0)
        attend(head * pairs)
        stage_one(1)
        stage_two(0)
        attend(head * pairs + 1)
        stage_one(2)
        stage_two(1)
        stage_three(0)
        attend(head * pairs + 2)
        stage_two(2)
        stage_three(1)
        stage_three(2)
        for copy in bias_copies:
            copy.wait_recv()
        stage_four(0)
        project(0, other, qb_got)
        stage_four(1)
        project(1, other, None)
        stage_four(2)
        project(2, other, vb_got)

        def late(n, carry):
            attend((1 - head) * pairs + n)
            return carry

        lax.fori_loop(0, pairs, late, 0)
        for copy in started.values():
            copy.wait_send()
        for copy in bias_copies:
            copy.wait_send()

    vmem = pl.BlockSpec(memory_space=pltpu.VMEM)
    act = jax.ShapeDtypeStruct((rows, width), BF16)
    full = jax.ShapeDtypeStruct((depth, width), BF16)
    return pl.pallas_call(
        kernel,
        out_shape=[act] * 4 + [jax.ShapeDtypeStruct((2 * pairs, 2, rows), F32)] + [full] * 3,
        in_specs=[pl.BlockSpec(memory_space=pltpu.SMEM)] + [vmem] * 6,
        out_specs=[vmem] * 8,
        scratch_shapes=[pltpu.VMEM((half,), BF16)] * 2 + [pltpu.SemaphoreType.DMA((3, kinds))] * 2
        + [pltpu.SemaphoreType.DMA((2,))] * 2,
        compiler_params=pltpu.CompilerParams(collective_id=0, has_side_effects=True, vmem_limit_bytes=VMEM_LIMIT),
        name="attention_forward",
    )(lengths, inputs, *weights, *biases)


def gelu_parts(v):
    x = jnp.abs(v) * 0.7071067811865476
    t = 1.0 / (1.0 + 0.3275911 * x)
    bell = jnp.exp(-0.5 * (v * v))
    tail = 0.5 * bell * t * (
        0.254829592 + t * (-0.284496736 + t * (1.421413741 + t * (-1.453152027 + t * 1.061405429))))
    phi = jnp.where(v >= 0, 1.0 - tail, tail)
    return v * phi, phi + v * bell * 0.3989422804014327


ROW_BLOCK = 64


def over_rows(rows, step, carry):
    def one(n, kept):
        return step(pl.ds(pl.multiple_of(n * ROW_BLOCK, ROW_BLOCK), ROW_BLOCK), kept)

    return lax.fori_loop(0, rows // ROW_BLOCK, one, carry)


OUT_BIAS, FIRST_GAIN, FIRST_SHIFT, DOWN_BIAS, SECOND_GAIN, SECOND_SHIFT, POOL_BIAS, CLASS_BIAS, UP_BIAS = range(9)
LOSS = 12


def orders(bits):
    head = bits - 1
    rest = list(range(2, head))
    both = [[0, 1, head] + rest, [0, head, 1] + rest]
    return [both + [[0] + rest[:1] + pair + rest[1:]] for pair in ([1, head], [head, 1])]


def rest_of_layer(context, inputs, class_turned, out_weight, vectors, log_totals, cotangent, up_weight, down_weight,
                  pool_weight, queries, keys, values, full, lengths, labels, bits):
    rows, width = inputs.shape
    hidden = up_weight.shape[1]
    half = width // 2
    times = hidden // width
    devices = 1 << bits
    block = 2 * width // devices
    classes = class_turned.shape[0]
    per_width = width // 128
    fact_rows = -(-(3 * per_width + 1) // 16) * 16
    plans = orders(bits)
    parts = len(plans[0])
    lanes_part = half // parts
    count = 2 * times + 4
    out_at, query_at = 2 * times, 2 * times + 1
    stages = bits
    head = bits - 1
    small_order = [0, 1, head] + list(range(2, head))
    pairs = width // 128
    dp_dims = (2,) * (bits - 1)

    def kernel(lengths_ref, labels_ref, ctx_ref, x_ref, cls_in, ow_ref, v0, v1, v2, v3, v4, v5, v6, v7, v8, lse_ref,
               cot_hbm, up_hbm, down_hbm, pool_hbm, q_hbm, k_hbm, v_hbm, wq_hbm, wk_hbm, wv_hbm,
               states_out, grad_out, logit_ref, sums_ref, small_out, late_out, factor_out, held, *rest):
        got = rest[:stages]
        (gb_ref, up_w, down_w, pool_w, low_ref, n1, r1, n2, r2, hid_even, hid_odd, slope_even, slope_odd, acc, whole, frow, vec_ref, cls_ref, small_buf,
         small_got, late_buf, late_got, load_sem, late_sem, send, recv, side_send, side_recv, whole_sem) = rest[stages:]
        place = Place(bits)
        loads = []
        for i, (source, target) in enumerate(
            ((up_hbm, up_w), (down_hbm, down_w), (pool_hbm, pool_w), (cot_hbm, gb_ref))):
            load = pltpu.make_async_copy(source, target, load_sem.at[i])
            load.start()
            loads.append(load)
        place.greet(range(bits))
        length = lengths_ref[place.head]
        slot = sum(place.mine[bit] * (1 << k) for k, bit in enumerate(small_order))
        small_ref = small_buf.at[0]
        hids, slopes = (hid_even, hid_odd), (slope_even, slope_odd)

        def index(i, done, fixed):
            out = [i]
            for bit in reversed(range(bits)):
                out.append(fixed[bit] if bit in fixed else place.mine[bit] if bit in done else slice(None))
            return tuple(out)

        def part_copy(i, s):
            plan = plans[i // parts % 2][i % parts]
            bit = plan[s]
            return pltpu.make_async_remote_copy(
                src_ref=held.at[index(i, plan[:s], {bit: 1 - place.mine[bit]})], dst_ref=got[s].at[i],
                send_sem=send.at[i, s], recv_sem=recv.at[i, s], device_id=place.partner(bit), device_id_type=MESH)

        def add_part(i, s):
            part_copy(i, s).wait_recv()
            where = index(i, plans[i // parts % 2][i % parts][: s + 1], {})
            if s == stages - 1:
                sums_ref[i] = held[where].astype(F32) + got[s][i].astype(F32)
            else:
                held[where] = held[where] + got[s][i]

        def take(name):
            for code in SCHEDULE[name]:
                if code >= 2000:
                    side_advance(code // 1000 - 2, code % 10)
                    continue
                i, s = code // 100 * parts + code // 10 % 10, code % 10
                if s > 0:
                    add_part(i, s - 1)
                if s < stages:
                    part_copy(i, s).start()

        def take_after(step, prefix, steps):
            for n in steps:
                if not SCHEDULE[prefix + str(n)]:
                    continue

                @pl.when(step == n)
                def _():
                    take(prefix + str(n))

        def put(i, wide, lead):
            for h in range(2):
                for m in range(parts):
                    at = h * half + m * lanes_part
                    held[(i * parts + m, h) + lead] = wide[..., at : at + lanes_part]

        def side_copy(kind, s):
            partner = place.partner(small_order[s])
            if kind == 0:
                start = (slot // (1 << s)) * (1 << s)
                source = target = factor_out.at[pl.ds(start, 1 << s)]
            else:
                buf, other = ((small_buf, small_got), (late_buf, late_got))[kind - 1]
                source, target = buf.at[s], other.at[s]
            return pltpu.make_async_remote_copy(
                src_ref=source, dst_ref=target, send_sem=side_send.at[kind, s], recv_sem=side_recv.at[kind, s],
                device_id=partner, device_id_type=MESH)

        def side_advance(kind, s):
            if s > 0:
                side_copy(kind, s - 1).wait_recv()
                if kind > 0:
                    buf, other, result = ((small_buf, small_got, small_out), (late_buf, late_got, late_out))[kind - 1]
                    total = buf[s - 1] + other[s - 1]
                    if s < stages:
                        buf[s] = total
                    else:
                        result[...] = total
            if s < stages:
                side_copy(kind, s).start()

        for i, ref in enumerate((v0, v1, v2, v3, v4, v5, v6)):
            vec_ref[i : i + 1, :] = ref[...].astype(F32).reshape(1, width)
        vec_ref[CLASS_BIAS : CLASS_BIAS + 1, 0:classes] = v7[...].astype(F32).reshape(1, classes)
        wide_bias = v8[...].astype(F32).reshape(1, hidden)
        for t in range(times):
            vec_ref[UP_BIAS + t : UP_BIAS + t + 1, :] = wide_bias[:, t * width : (t + 1) * width]
        cls_ref[...] = jnp.zeros_like(cls_ref)
        cls_ref[0:classes, :] = cls_in[...]

        def vec(i):
            return vec_ref[i : i + 1, :]

        acc[...] = matmul(ctx_ref[...], ow_ref[...])

        def norm_one(at, carry):
            value = x_ref[at, :].astype(F32) + (acc[at, :] + vec(OUT_BIAS))
            center = value - jnp.mean(value, -1, keepdims=True)
            scale = lax.rsqrt(jnp.mean(center * center, -1, keepdims=True) + EPSILON)
            normal = center * scale
            n1[at, :] = normal
            r1[at, :] = scale
            low_ref[at, :] = (normal * vec(FIRST_GAIN) + vec(FIRST_SHIFT)).astype(BF16)
            acc[at, :] = jnp.zeros_like(normal)
            return carry

        over_rows(rows, norm_one, 0)
        loads[0].wait()
        loads[1].wait()

        def at_chunk(c):
            return pl.ds(pl.multiple_of(c * width, width), width)

        def pre_of(c, parity):
            slopes[parity][:, at_chunk(c // 2)] = matmul(low_ref[...], up_w[:, at_chunk(c)]) + vec_ref[pl.ds(UP_BIAS + c, 1), :]

        def activate(c, parity):
            at = at_chunk(c // 2)
            act, deriv = gelu_parts(slopes[parity][:, at])
            hids[parity][:, at] = act.astype(BF16)
            slopes[parity][:, at] = deriv

        def add_branch(c, parity):
            acc[...] += matmul(hids[parity][:, at_chunk(c // 2)], down_w[at_chunk(c), :])

        pre_of(0, 0)
        pre_of(1, 1)
        activate(0, 0)

        def forward(n, carry):
            c = 2 * n
            pre_of(c + 2, 0)
            activate(c + 1, 1)
            add_branch(c, 0)
            pre_of(c + 3, 1)
            activate(c + 2, 0)
            add_branch(c + 1, 1)
            return carry

        lax.fori_loop(0, times // 2 - 1, forward, 0)
        activate(times - 1, 1)
        add_branch(times - 2, 0)
        add_branch(times - 1, 1)

        def norm_two(at, carry):
            first = n1[at, :] * vec(FIRST_GAIN) + vec(FIRST_SHIFT)
            value = first + (acc[at, :] + vec(DOWN_BIAS))
            center = value - jnp.mean(value, -1, keepdims=True)
            scale = lax.rsqrt(jnp.mean(center * center, -1, keepdims=True) + EPSILON)
            normal = center * scale
            n2[at, :] = normal
            r2[at, :] = scale
            whole[at, :] = (normal * vec(SECOND_GAIN) + vec(SECOND_SHIFT)).astype(BF16)
            return carry

        over_rows(rows, norm_two, 0)
        states_copy = pltpu.make_async_copy(whole, states_out, whole_sem.at[0])
        states_copy.start()

        loads[2].wait()
        loads[3].wait()
        lead = whole[0:16, :]
        pooled = jnp.tanh(matmul(lead, pool_w[...]) + vec(POOL_BIAS))
        pooled_low = pooled.astype(BF16)
        logits = nt(pooled_low, cls_ref[...]) + vec_ref[CLASS_BIAS : CLASS_BIAS + 1, 0:128]
        lanes = lane_iota(logits.shape)
        logits = jnp.where(lanes < classes, logits, NEGATIVE)
        top = jnp.max(logits, -1, keepdims=True)
        norm = top + jnp.log(jnp.sum(jnp.exp(logits - top), -1, keepdims=True))
        target = jnp.where(lanes == labels_ref[0], 1.0, 0.0)
        loss = (norm - jnp.sum(jnp.where(lanes < classes, target * logits, 0.0), -1, keepdims=True)) / devices
        grad_logits = (jnp.where(lanes < classes, jnp.exp(logits - norm) - target, 0.0) / devices).astype(BF16)
        grad_pooled = (matmul(grad_logits, cls_ref[...]) * (1.0 - pooled * pooled)).astype(BF16)
        grad_lead = nt(grad_pooled, pool_w[...])
        logit_ref[...] = logits[0:1, 0:classes]
        frow[...] = jnp.zeros_like(frow)
        for k, value in enumerate((lead, grad_pooled, pooled_low)):
            wide = value.astype(F32)
            for j in range(per_width):
                frow[k * per_width + j : k * per_width + j + 1, :] = wide[0:1, j * 128 : (j + 1) * 128]
        frow[3 * per_width : 3 * per_width + 1, :] = grad_logits.astype(F32)[0:1, 0:128]
        factor_out[slot] = frow[...].astype(BF16)
        take("R")

        def back_two(at, sums):
            gain_sum, shift_sum, bias_sum = sums
            row = at.start + lax.broadcasted_iota(jnp.int32, (ROW_BLOCK, width), 0)
            grad = gb_ref[at, :].astype(F32) + jnp.where(row == 0, grad_lead[0:1, :], 0.0)
            normal = n2[at, :]
            e = grad * vec(SECOND_GAIN)
            value = (e - jnp.mean(e, -1, keepdims=True) - normal * jnp.mean(e * normal, -1, keepdims=True)) * r2[at, :]
            rounded = value.astype(BF16)
            acc[at, :] = value
            gb_ref[at, :] = rounded
            return (gain_sum + jnp.sum(grad * normal, 0, keepdims=True), shift_sum + jnp.sum(grad, 0, keepdims=True),
                    bias_sum + jnp.sum(rounded.astype(F32), 0, keepdims=True))

        zero = jnp.zeros((1, width), F32)
        gain_sum, shift_sum, bias_sum = over_rows(rows, back_two, (zero, zero, zero))
        small_ref[...] = jnp.zeros(small_ref.shape, F32)
        small_ref[SECOND_GAIN : SECOND_GAIN + 1, :] = gain_sum
        small_ref[SECOND_SHIFT : SECOND_SHIFT + 1, :] = shift_sum
        small_ref[DOWN_BIAS : DOWN_BIAS + 1, :] = bias_sum
        small_ref[LOSS : LOSS + 1, :] = jnp.broadcast_to(loss[0:1, 0:1], (1, width))

        take("B")

        def down_grads(n, carry):
            for parity in range(2):
                c = 2 * n + parity
                wide = tn(hids[parity][:, at_chunk(n)], gb_ref[...]).astype(BF16).reshape(2, 2, times, block, width)
                for t in range(times):
                    put(t, wide[:, :, t], (lax.rem(c // 2, 2), lax.rem(c, 2)))
                take_after(c, "D", range(parity, times, 2))
            return carry

        lax.fori_loop(0, times // 2, down_grads, 0)

        for parity in range(2):

            def up_grads(h, carry):
                c = 2 * h + parity
                step = 4 * parity + 2 * h
                grad = (nt(gb_ref[...], down_w[at_chunk(c), :]) * slopes[parity][:, at_chunk(h)]).astype(BF16)
                small_buf[0, pl.ds(UP_BIAS + c, 1), :] = jnp.sum(grad.astype(F32), 0, keepdims=True)
                wide = tn(low_ref[...], grad).astype(BF16)
                for t in range(2):
                    for m in range(parts):
                        at = t * half + m * lanes_part
                        held[(times + 2 * parity + t) * parts + m, h] = wide[:, at : at + lanes_part].reshape(
                            dp_dims + (block, lanes_part))
                take_after(step, "U", range(4 * parity, 4 * parity + 4, 2))
                acc[...] += nt(grad, up_w[:, at_chunk(c)])
                take_after(step + 1, "U", range(4 * parity + 1, 4 * parity + 4, 2))
                return carry

            lax.fori_loop(0, 2, up_grads, 0)

        late = []
        for i, (source, target) in enumerate((
            (q_hbm, down_w.at[0:rows, :]), (k_hbm, down_w.at[rows : 2 * rows, :]),
            (v_hbm, down_w.at[2 * rows : 3 * rows, :]), (wq_hbm, up_w.at[:, 0:width]),
            (wk_hbm, up_w.at[:, width : 2 * width]), (wv_hbm, up_w.at[:, 2 * width : 3 * width]),
        )):
            load = pltpu.make_async_copy(source, target, late_sem.at[i])
            load.start()
            late.append(load)

        def back_one(at, sums):
            gain_sum, shift_sum, bias_sum = sums
            grad = acc[at, :]
            normal = n1[at, :]
            e = grad * vec(FIRST_GAIN)
            value = (e - jnp.mean(e, -1, keepdims=True) - normal * jnp.mean(e * normal, -1, keepdims=True)) * r1[at, :]
            rounded = value.astype(BF16)
            acc[at, :] = value
            low_ref[at, :] = rounded
            return (gain_sum + jnp.sum(grad * normal, 0, keepdims=True), shift_sum + jnp.sum(grad, 0, keepdims=True),
                    bias_sum + jnp.sum(rounded.astype(F32), 0, keepdims=True))

        gain_sum, shift_sum, bias_sum = over_rows(rows, back_one, (zero, zero, zero))
        small_ref[FIRST_GAIN : FIRST_GAIN + 1, :] = gain_sum
        small_ref[FIRST_SHIFT : FIRST_SHIFT + 1, :] = shift_sum
        small_ref[OUT_BIAS : OUT_BIAS + 1, :] = bias_sum
        take("L0")
        put(out_at, tn(ctx_ref[...], low_ref[...]).astype(BF16).reshape(dp_dims + (block, width)), ())
        take("L1")
        hids[1][:, width : 2 * width] = nt(low_ref[...], ow_ref[...]).astype(BF16)
        take("L2")

        lanes_row = lax.broadcasted_iota(jnp.int32, (128, rows), 0)
        pair_lanes = lane_iota((rows, 128))
        for load in late:
            load.wait()

        def attend(pair, carry):
            def at(n):
                return pl.ds(pl.multiple_of(n % 2 * width + pair * 128, 128), 128)

            q2 = down_w[0:rows, at(0)]
            k2 = down_w[rows : 2 * rows, at(0)]
            v2 = down_w[2 * rows : 3 * rows, at(0)]
            g2 = hids[1][:, at(3)]
            k2t = k2.T
            heads_of = []
            for parity in range(2):
                qa, ka = pair_operands(q2, k2, length, parity)
                mine = (pair_lanes < HEAD_DIM) if parity == 0 else (pair_lanes >= HEAD_DIM)
                va = jnp.where(mine, v2.astype(F32), 0.0).astype(BF16)
                probs = jnp.exp(nt(ka, qa) - lse_ref[pair, parity : parity + 1, :])
                grad_v = matmul(probs.astype(BF16), g2)
                grad_probs = nt(va, g2)
                inner = jnp.sum(probs * grad_probs, 0, keepdims=True)
                grad_scores = (probs * (grad_probs - inner)).astype(BF16)
                heads_of.append((grad_v, matmul(grad_scores, qa), matmul(k2t, grad_scores)))
                take_after(2 * pair + parity, "P", range(parity, 2 * pairs, 2))
            first = pair_lanes < HEAD_DIM
            turned = jnp.where(lanes_row < HEAD_DIM, heads_of[0][2], heads_of[1][2]) * HEAD_DIM ** -0.5
            hids[0][:, at(0)] = turned.T.astype(BF16)
            hids[0][:, at(1)] = jnp.where(first, heads_of[0][1], heads_of[1][1]).astype(BF16)
            hids[1][:, at(2)] = jnp.where(first, heads_of[0][0], heads_of[1][0]).astype(BF16)
            return carry

        lax.fori_loop(0, pairs, attend, 0)

        def grads_of(n):
            return hids[n // 2][:, n % 2 * width : (n % 2 + 1) * width]

        late_buf[0] = jnp.zeros(late_buf.shape[1:], F32)
        late_buf[0, 0:1, :] = jnp.sum(grads_of(0).astype(F32), 0, keepdims=True)
        late_buf[0, 1:2, :] = jnp.sum(grads_of(2).astype(F32), 0, keepdims=True)
        take("Q")
        for n in range(3):
            put(query_at + n, tn(x_ref[...], grads_of(n)).astype(BF16).reshape(dp_dims + (block, width)), ())
            take("W" + str(n))
        states_copy.wait()
        for n in range(3):
            acc[...] += nt(grads_of(n), up_w[:, n * width : (n + 1) * width])
            take("I" + str(n))
        whole[...] = acc[...].astype(BF16)
        grad_copy = pltpu.make_async_copy(whole, grad_out, whole_sem.at[1])
        grad_copy.start()
        for n in range(4):
            take("T" + str(n))
        grad_copy.wait()
        for i in range(count * parts):
            for s in range(stages):
                part_copy(i, s).wait_send()
        for s in range(stages):
            for kind in range(3):
                side_copy(kind, s).wait_send()

    vmem = pl.BlockSpec(memory_space=pltpu.VMEM)
    anywhere = pl.BlockSpec(memory_space=pl.ANY)
    smem = pl.BlockSpec(memory_space=pltpu.SMEM)
    act = jax.ShapeDtypeStruct((rows, width), BF16)
    return pl.pallas_call(
        kernel,
        out_shape=[
            act, act, jax.ShapeDtypeStruct((1, classes), F32), jax.ShapeDtypeStruct((count * parts, block, lanes_part), F32),
            jax.ShapeDtypeStruct((16, width), F32), jax.ShapeDtypeStruct((8, width), F32),
            jax.ShapeDtypeStruct((devices, fact_rows, 128), BF16),
        ],
        in_specs=[smem] * 2 + [vmem] * 14 + [anywhere] * 10,
        out_specs=[anywhere] * 2 + [vmem] * 5,
        scratch_shapes=[pltpu.VMEM((count * parts, 2) + dp_dims + (block, lanes_part), BF16)]
        + [pltpu.VMEM((count * parts,) + (2,) * (stages - 1 - s) + (block, lanes_part), BF16) for s in range(stages)]
        + [
            pltpu.VMEM((rows, width), BF16),
            pltpu.VMEM((width, hidden), BF16),
            pltpu.VMEM((hidden, width), BF16),
            pltpu.VMEM((width, width), BF16),
            pltpu.VMEM((rows, width), BF16),
            pltpu.VMEM((rows, width), F32),
            pltpu.VMEM((rows, 1), F32),
            pltpu.VMEM((rows, width), F32),
            pltpu.VMEM((rows, 1), F32),
            pltpu.VMEM((rows, hidden // 2), BF16),
            pltpu.VMEM((rows, hidden // 2), BF16),
            pltpu.VMEM((rows, hidden // 2), F32),
            pltpu.VMEM((rows, hidden // 2), F32),
            pltpu.VMEM((rows, width), F32),
            pltpu.VMEM((rows, width), BF16),
            pltpu.VMEM((fact_rows, 128), F32),
            pltpu.VMEM((16, width), F32),
            pltpu.VMEM((128, width), BF16),
            pltpu.VMEM((stages, 16, width), F32),
            pltpu.VMEM((stages, 16, width), F32),
            pltpu.VMEM((stages, 8, width), F32),
            pltpu.VMEM((stages, 8, width), F32),
            pltpu.SemaphoreType.DMA((4,)),
            pltpu.SemaphoreType.DMA((6,)),
            pltpu.SemaphoreType.DMA((count * parts, stages)),
            pltpu.SemaphoreType.DMA((count * parts, stages)),
            pltpu.SemaphoreType.DMA((3, stages)),
            pltpu.SemaphoreType.DMA((3, stages)),
            pltpu.SemaphoreType.DMA((2,)),
        ],
        compiler_params=pltpu.CompilerParams(collective_id=1, has_side_effects=True, vmem_limit_bytes=VMEM_LIMIT),
        name="rest_of_layer",
    )(lengths, labels, context, inputs, class_turned, out_weight, *vectors, log_totals, cotangent, up_weight,
      down_weight, pool_weight, queries, keys, values, *full)


SCHEDULE = {
    "R": (2000,),
    "B": (),
    "D0": (),
    "D1": (2001,),
    "D2": (),
    "D3": (0, 10, 20, 100, 110, 120,),
    "U0": (2002, 1, 200, 210, 220, 300, 310, 320,),
    "U1": (11, 21, 101,),
    "U2": (111, 121, 201, 211, 221, 400, 410, 420, 500, 510, 520,),
    "U3": (2003, 301,),
    "U4": (2, 12, 102,),
    "U5": (321, 22, 122,),
    "U6": (112, 202, 212, 311, 421, 600, 610, 620, 700, 710, 720,),
    "U7": (222,),
    "L0": (3000, 3, 13, 103, 302, 401,),
    "L1": (2004, 23, 322, 521, 800, 810, 820,),
    "L2": (123, 411, 501,),
    "P0": (3001, 113, 203,),
    "P1": (4, 14, 213, 223, 104, 621,),
    "P2": (24, 312, 511,),
    "P3": (124, 303, 323, 721,),
    "P4": (114, 204, 402, 422,),
    "P5": (214, 412, 224, 5, 502, 522, 601, 821,),
    "P6": (2005, 15, 25, 105, 611,),
    "P7": (3002, 115, 125, 304, 313, 324, 512, 205,),
    "P8": (215, 403, 622,),
    "P9": (225, 413, 423, 503, 701,),
    "P10": (711,),
    "P11": (305, 325, 523, 314,),
    "Q": (4000, 602, 801,),
    "W0": (404, 414, 513, 722, 900, 910, 920,),
    "W1": (424, 504, 612, 623, 1000, 1010, 1020,),
    "W2": (3003, 315, 811, 822, 1100, 4001, 1110, 1120,),
    "I0": (405, 514, 524, 921,),
    "I1": (415, 425, 603, 702, 712, 1021,),
    "I2": (505, 723, 802, 624, 901, 911,),
    "T0": (1001, 1011, 1101, 1111, 1121, 613, 515, 3004, 525, 823, 922, 812, 604, 713, 703, 625, 4002, 724, 803,),
    "T1": (1022, 605, 902, 912, 725, 3005, 1122, 614, 714, 1002, 704, 1012, 804, 1102, 615, 1112, 715, 813, 824,),
    "T2": (705, 805, 1023, 923, 913, 814, 903, 825, 4003, 1013, 1123, 1113, 914, 924, 1003, 904, 815, 1103, 1014,),
    "T3": (1124, 1024, 1114, 4004, 1004, 915, 925, 1104, 905, 1015, 1125, 1025, 1115, 1005, 1105, 4005,),
}


def spread(states, input_grad, logits, sums, small, late, gathered, classes):
    width = small.shape[1]
    half = width // 2
    parts, block, lanes_part = sums.shape
    count = parts * lanes_part // half
    parts = parts // count
    devices = gathered.shape[0]
    times = (count - 4) // 2
    lanes = width // 128

    def kernel(states_ref, grad_ref, logits_ref, sums_ref, small_ref, late_ref, got_ref, states_out, grad_out, logits_out, up, down,
               out, query, key, value, pool, query_bias, value_bias, out_bias, first_gain, first_shift, up_bias,
               down_bias, second_gain, second_shift, pool_bias, class_weight, class_bias, loss, left, right, sem):
        copies = [
            pltpu.make_async_copy(states_ref, states_out, sem.at[0]), pltpu.make_async_copy(grad_ref, grad_out, sem.at[1])]
        for copy in copies:
            copy.start()
        logits_out[...] = logits_ref[...]
        dp, head = lax.axis_index("dp"), lax.axis_index("head")
        for m in range(parts):
            at = slice(m * lanes_part, (m + 1) * lanes_part)
            for t in range(times):
                down[t * block : (t + 1) * block, at] = sums_ref[t * parts + m]
                up[:, t * half + m * lanes_part : t * half + (m + 1) * lanes_part] = sums_ref[(times + t) * parts + m]
            for k, ref in enumerate((out, query, key, value)):
                ref[:, at] = sums_ref[(2 * times + k) * parts + m]
        got = got_ref[...].astype(F32)

        def wide(k):
            return jnp.concatenate([got[:, k * lanes + j, :] for j in range(lanes)], 1)

        lead, grad_pooled, pooled = wide(0), wide(1), wide(2)
        grad_logits = got[:, 3 * lanes, :]
        left[...] = lead.T
        right[...] = grad_pooled
        at = pl.ds(pl.multiple_of(head * half, half), half)
        pool[...] = matmul(
            left[pl.ds(pl.multiple_of(dp * block, 8), block), :].astype(BF16), right[:, at].astype(BF16))
        pool_bias[...] = jnp.sum(grad_pooled, 0)
        class_weight[...] = tn(grad_logits.astype(BF16), pooled.astype(BF16))[0:classes, :]
        class_bias[...] = jnp.sum(grad_logits, 0, keepdims=True)[:, 0:classes].reshape(classes)
        query_bias[...] = late_ref[0:1, at].reshape(half)
        value_bias[...] = late_ref[1:2, at].reshape(half)
        for ref, row in ((out_bias, OUT_BIAS), (first_gain, FIRST_GAIN), (first_shift, FIRST_SHIFT),
                         (down_bias, DOWN_BIAS), (second_gain, SECOND_GAIN), (second_shift, SECOND_SHIFT)):
            ref[...] = small_ref[row, :]
        up_bias[...] = jnp.concatenate(
            [small_ref[UP_BIAS + t : UP_BIAS + t + 1, :] for t in range(times)], 1).reshape(times * width)
        loss[()] = small_ref[LOSS, 0]
        for copy in copies:
            copy.wait()

    def f32(*shape):
        return jax.ShapeDtypeStruct(shape, F32)

    square = f32(block, half)
    row = f32(width)
    act = jax.ShapeDtypeStruct(states.shape, BF16)
    vmem = pl.BlockSpec(memory_space=pltpu.VMEM)
    anywhere = pl.BlockSpec(memory_space=pl.ANY)
    return pl.pallas_call(
        kernel,
        out_shape=[
            act, act, f32(1, classes), f32(block, times * half), f32(times * block, half), square, square, square, square,
            square, f32(half), f32(half), row, row, row, f32(times * width), row, row, row, row, f32(classes, width),
            f32(classes), f32(),
        ],
        in_specs=[vmem] * 7,
        out_specs=[anywhere] * 2 + [vmem] * 20 + [pl.BlockSpec(memory_space=pltpu.SMEM)],
        scratch_shapes=[
            pltpu.VMEM((width, devices), F32), pltpu.VMEM((devices, width), F32), pltpu.SemaphoreType.DMA((2,))],
        compiler_params=pltpu.CompilerParams(vmem_limit_bytes=VMEM_LIMIT),
        name="spread",
    )(states, input_grad, logits, sums, small, late, gathered)


def plain_body(
    inputs, lengths, labels, state_cotangent, query_weight, query_bias, key_weight, value_weight, value_bias,
    out_weight, out_bias, first_gain, first_shift, up_weight, up_bias, down_weight, down_bias, second_gain,
    second_shift, pool_weight, pool_bias, class_weight, class_bias,
):
    scale = HEAD_DIM ** (-0.5)
    dp_size, head_size = lax.axis_size("dp"), lax.axis_size("head")
    dp_at, head_at = lax.axis_index("dp"), lax.axis_index("head")
    devices = dp_size * head_size
    width = inputs.shape[1]
    block_columns = width // head_size
    row_seqs = labels.shape[0]
    assert row_seqs == 1 and inputs.shape[0] == SEQ_LEN
    length = lax.dynamic_index_in_dim(lengths, head_at, keepdims=False)

    weights = [query_weight, key_weight, value_weight]
    full = [lax.all_gather(w, "head", axis=1, tiled=True) for w in weights]
    biases = lax.all_gather(jnp.stack([query_bias, value_bias]), "head", axis=1, tiled=True)
    query_bias, value_bias = biases[0], biases[1]
    wq, wk, wv = full
    head_count = width // HEAD_DIM

    def heads(matrix):
        return matrix.reshape(SEQ_LEN, head_count, HEAD_DIM)

    queries = (matmul(inputs, wq) + query_bias).astype(BF16)
    keys_low = matmul(inputs, wk).astype(BF16)
    values_low = (matmul(inputs, wv) + value_bias).astype(BF16)
    visible = lax.broadcasted_iota(jnp.int32, (1, 1, SEQ_LEN), 2) < length

    def scores_of():
        raw = jnp.einsum("qhd,khd->hqk", heads(queries), heads(keys_low), preferred_element_type=F32) * scale
        return jnp.where(visible, raw, NEGATIVE)

    scores = scores_of()
    peak = jnp.max(scores, -1, keepdims=True)
    raised = jnp.exp(scores - peak)
    denominator = jnp.sum(raised, -1, keepdims=True)
    probs = raised / denominator
    log_total = peak + jnp.log(denominator)
    context = jnp.einsum("hqk,khd->qhd", probs.astype(BF16), heads(values_low), preferred_element_type=F32)
    context_rows = context.astype(BF16).reshape(SEQ_LEN, width)
    attended = matmul(context_rows, out_weight) + out_bias
    first_out, first_back = jax.vjp(
        normalize, inputs.astype(F32) + attended, first_gain.astype(F32), first_shift.astype(F32))
    first_low = first_out.astype(BF16)
    hidden_pre = matmul(first_low, up_weight) + up_bias
    hidden_act, gelu_back = jax.vjp(partial(jax.nn.gelu, approximate=False), hidden_pre)
    hidden_low = hidden_act.astype(BF16)
    branch = matmul(hidden_low, down_weight) + down_bias
    normed, second_back = jax.vjp(normalize, first_out + branch, second_gain.astype(F32), second_shift.astype(F32))
    leading_low = normed.reshape(row_seqs, SEQ_LEN, -1)[:, 0].astype(BF16)
    pooled = jnp.tanh(matmul(leading_low, pool_weight) + pool_bias)
    pooled_low = pooled.astype(BF16)
    logits = matmul(pooled_low, class_weight) + class_bias
    classes = lax.broadcasted_iota(jnp.int32, logits.shape, 1)
    target = (classes == labels[:, None]).astype(F32)
    log_norm = jax.nn.logsumexp(logits, axis=-1)
    loss_part = jnp.sum(log_norm - jnp.sum(target * logits, -1)) / devices
    grad_logits = ((jnp.exp(logits - log_norm[:, None]) - target) / devices).astype(BF16)
    grad_class_weight = matmul(pooled_low.T, grad_logits)
    grad_class_bias = column_sums(grad_logits)
    grad_pooled = (matmul(grad_logits, class_weight.T) * (1.0 - pooled * pooled)).astype(BF16)
    grad_pool_bias = column_sums(grad_pooled)
    grad_leading = matmul(grad_pooled, pool_weight.T)
    grad_normed = state_cotangent.astype(F32).reshape(row_seqs, SEQ_LEN, -1)
    grad_normed = grad_normed.at[:, 0].add(grad_leading).reshape(normed.shape)
    grad_second, grad_second_gain, grad_second_shift = second_back(grad_normed)
    grad_branch = grad_second.astype(BF16)
    grad_down_weight = matmul(hidden_low.T, grad_branch)
    grad_down_bias = column_sums(grad_branch)
    grad_hidden = gelu_back(matmul(grad_branch, down_weight.T))[0].astype(BF16)
    grad_up_weight = matmul(first_low.T, grad_hidden)
    grad_up_bias = column_sums(grad_hidden)
    grad_first_out = grad_second + matmul(grad_hidden, up_weight.T)
    grad_first, grad_first_gain, grad_first_shift = first_back(grad_first_out)
    grad_attended = grad_first.astype(BF16)
    grad_out_weight = matmul(context_rows.T, grad_attended)
    grad_out_bias = column_sums(grad_attended)
    grad_context = heads(matmul(grad_attended, out_weight.T).astype(BF16))
    probs_again = jnp.exp(scores_of() - log_total)
    grad_values = jnp.einsum(
        "hqk,qhd->khd", probs_again.astype(BF16), grad_context, preferred_element_type=F32).astype(BF16)
    grad_probs = jnp.einsum("qhd,khd->hqk", grad_context, heads(values_low), preferred_element_type=F32)
    grad_scores = probs_again * (grad_probs - jnp.sum(probs_again * grad_probs, -1, keepdims=True))
    grad_scores = grad_scores.astype(BF16)
    grad_queries = (
        jnp.einsum("hqk,khd->qhd", grad_scores, heads(keys_low), preferred_element_type=F32) * scale).astype(BF16)
    grad_keys = (
        jnp.einsum("hqk,qhd->khd", grad_scores, heads(queries), preferred_element_type=F32) * scale).astype(BF16)
    grad_queries = grad_queries.reshape(SEQ_LEN, width)
    grad_keys = grad_keys.reshape(SEQ_LEN, width)
    grad_values = grad_values.reshape(SEQ_LEN, width)
    grad_query_weight = matmul(inputs.T, grad_queries)
    grad_key_weight = matmul(inputs.T, grad_keys)
    grad_value_weight = matmul(inputs.T, grad_values)
    input_grad = (
        grad_first + matmul(grad_queries, wq.T) + matmul(grad_keys, wk.T) + matmul(grad_values, wv.T)).astype(BF16)

    small_parts = (
        grad_out_bias, grad_first_gain, grad_first_shift, grad_up_bias, grad_down_bias, grad_second_gain,
        grad_second_shift, grad_pool_bias, column_sums(grad_queries), column_sums(grad_values),
        grad_class_weight.reshape(-1), grad_class_bias, loss_part.reshape(1),
    )
    grads = (grad_up_weight, grad_down_weight, grad_out_weight, grad_query_weight, grad_key_weight, grad_value_weight)
    grads = grads + (matmul(leading_low.T, grad_pooled),)

    def scatter(matrix):
        part = lax.psum_scatter(matrix, "dp", scatter_dimension=0, tiled=True)
        return lax.psum_scatter(part.astype(BF16), "head", scatter_dimension=1, tiled=True).astype(F32)

    up_total, down_total, out_total, query_total, key_total, value_total, pool_total = map(scatter, grads)
    totals = lax.psum(small_parts, ("dp", "head"))
    (
        out_bias_total, first_gain_total, first_shift_total, up_bias_total, down_bias_total, second_gain_total,
        second_shift_total, pool_bias_total, query_bias_total, value_bias_total, class_weight_total,
        class_bias_total, loss,
    ) = totals
    query_bias_total = lax.dynamic_slice_in_dim(query_bias_total, head_at * block_columns, block_columns)
    value_bias_total = lax.dynamic_slice_in_dim(value_bias_total, head_at * block_columns, block_columns)
    return (
        normed.astype(BF16), input_grad, logits, loss.reshape(()), query_total, query_bias_total, key_total,
        value_total, value_bias_total, out_total, out_bias_total, first_gain_total, first_shift_total, up_total,
        up_bias_total, down_total, down_bias_total, second_gain_total, second_shift_total, pool_total,
        pool_bias_total, class_weight_total.reshape(class_weight.shape), class_bias_total,
    )


def body(*args):
    (
        inputs, lengths, labels, state_cotangent, query_weight, query_bias, key_weight, value_weight, value_bias,
        out_weight, out_bias, first_gain, first_shift, up_weight, up_bias, down_weight, down_bias, second_gain,
        second_shift, pool_weight, pool_bias, class_weight, class_bias,
    ) = args
    dp_size, head_size = lax.axis_size("dp"), lax.axis_size("head")
    devices = dp_size * head_size
    bits = devices.bit_length() - 1
    rows, width = inputs.shape
    hidden = up_weight.shape[1]
    classes = class_weight.shape[1]
    direct = (
        (width // dp_size) % 16 == 0 and head_size == 2 and bits == 5 and hidden == 4 * width and rows == SEQ_LEN
        and labels.shape[0] == 1
    )
    if not direct:
        return plain_body(*args)

    queries, keys, values, context, log_totals, *full = attention_forward(
        inputs, [query_weight, key_weight, value_weight], [query_bias, value_bias], lengths, bits)
    vectors = (out_bias, first_gain, first_shift, down_bias, second_gain, second_shift, pool_bias, class_bias, up_bias)
    states, input_grad, logits, sums, small, late, gathered = rest_of_layer(
        context, inputs, class_weight.T, out_weight, vectors, log_totals, state_cotangent, up_weight, down_weight,
        pool_weight, queries, keys, values, full, lengths, labels, bits)
    (
        states, input_grad, logits, up, down, out, query, key, value, pool, query_sum, value_sum, out_sum, first_gain_sum,
        first_shift_sum, up_sum, down_sum, second_gain_sum, second_shift_sum, pool_sum, class_sum, class_bias_sum, loss,
    ) = spread(states, input_grad, logits, sums, small, late, gathered, classes)
    return (
        states, input_grad, logits, loss, query, query_sum, key, value, value_sum, out, out_sum, first_gain_sum,
        first_shift_sum, up, up_sum, down, down_sum, second_gain_sum, second_shift_sum, pool, pool_sum, class_sum.T,
        class_bias_sum,
    )


def solution(mesh):
    rows, column, both = P(("dp", "head"), None), P(None, "head"), P("dp", "head")
    one, none = P("head"), P()
    return jax.shard_map(
        body,
        mesh=mesh,
        in_specs=(rows, P("dp"), P(("dp", "head")), rows, column, one, column, column, one) + (none,) * 14,
        out_specs=(
            rows, rows, rows, none, both, one, both, both, one, both, none, none, none, both, none, both, none,
            none, none, both, none, none, none,
        ),
        check_vma=False,
    )
```

```python
from functools import partial

import jax
import jax.numpy as jnp
from jax import lax
from jax.experimental import pallas as pl
from jax.experimental.pallas import tpu as pltpu
from jax.sharding import PartitionSpec as P

HEAD_DIM = 64
SEQ_LEN = 512
NEGATIVE = -1e30
EPSILON = 1e-06
MESH = pl.DeviceIdType.MESH
F32 = jnp.float32
BF16 = jnp.bfloat16
VMEM_LIMIT = 67_000_000


def normalize(values, gain, shift):
    center = values - jnp.mean(values, -1, keepdims=True)
    spread = jnp.mean(center * center, -1, keepdims=True)
    return center * lax.rsqrt(spread + EPSILON) * gain + shift


def matmul(left, right):
    return jnp.dot(left, right, preferred_element_type=F32)


def column_sums(values):
    return jnp.sum(values.astype(F32), 0)


class Place:
    def __init__(self, bits):
        self.bits = bits
        self.dp = lax.axis_index("dp")
        self.head = lax.axis_index("head")
        self.mine = [lax.rem(self.dp // (1 << b), 2) for b in range(bits - 1)] + [self.head]

    def partner(self, bit):
        if bit == self.bits - 1:
            return (self.dp, 1 - self.head)
        return (self.dp + (1 - 2 * self.mine[bit]) * (1 << bit), self.head)

    def greet(self, bits):
        barrier = pltpu.get_barrier_semaphore()
        for bit in bits:
            pl.semaphore_signal(barrier, inc=1, device_id=self.partner(bit), device_id_type=MESH)
        pl.semaphore_wait(barrier, len(bits))


def shared_rows(bits):
    return 1, 2


def lane_iota(shape):
    return lax.broadcasted_iota(jnp.int32, shape, 1)


def first_lanes(shape):
    return lane_iota(shape) < HEAD_DIM


def pair_operands(q2, k2, length, parity):
    lanes = lane_iota(q2.shape)
    rows = lax.broadcasted_iota(jnp.int32, q2.shape, 0)
    mine = (lanes < HEAD_DIM) if parity == 0 else (lanes >= HEAD_DIM)
    spare = lanes == (HEAD_DIM if parity == 0 else 0)
    hidden = jnp.where(rows < length, 0.0, NEGATIVE)
    qa = jnp.where(mine, q2.astype(F32) * HEAD_DIM ** -0.5, jnp.where(spare, 1.0, 0.0)).astype(BF16)
    ka = jnp.where(mine, k2.astype(F32), jnp.where(spare, hidden, 0.0)).astype(BF16)
    return qa, ka


def nt(left, right):
    return lax.dot_general(left, right, (((1,), (1,)), ((), ())), preferred_element_type=F32)


def tn(left, right):
    return lax.dot_general(left, right, (((0,), (0,)), ((), ())), preferred_element_type=F32)


def attend_pair(q_ref, k_ref, v_ref, ctx_ref, lse_ref, pair, length):
    at = pl.ds(pl.multiple_of(pair * 128, 128), 128)
    q2, k2, v2 = q_ref[:, at], k_ref[:, at], v_ref[:, at]
    v2t = v2.T
    rows = lax.broadcasted_iota(jnp.int32, (128, SEQ_LEN), 0)
    parts = []
    for parity in range(2):
        qa, ka = pair_operands(q2, k2, length, parity)
        scores = nt(ka, qa)
        peak = jnp.max(scores, 0, keepdims=True)
        raised = jnp.exp(scores - peak)
        total = jnp.sum(raised, 0, keepdims=True)
        probs = (raised * (1.0 / total)).astype(BF16)
        parts.append(matmul(v2t, probs))
        lse_ref[pair, parity : parity + 1, :] = peak + jnp.log(total)
    joined = jnp.where(rows < HEAD_DIM, parts[0], parts[1])
    ctx_ref[:, at] = joined.T.astype(BF16)


def attention_forward(inputs, weights, biases, lengths, bits):
    rows, width = inputs.shape
    depth, half = weights[0].shape
    part = depth // 8
    pairs = half // 128
    kinds = 10

    def kernel(lengths_ref, x_ref, wq_ref, wk_ref, wv_ref, qb_ref, vb_ref, q_out, k_out, v_out, ctx_ref, lse_ref,
               fq_out, fk_out, fv_out, q_ref, k_ref, v_ref, fq_ref, fk_ref, fv_ref, qb_got, vb_got, send, recv,
               bias_send, bias_recv, out_sem):
        place = Place(bits)
        head = place.head
        bit_x, bit_z = shared_rows(bits)
        place.greet([0, bit_x, bit_z, bits - 1])
        length = lengths_ref[head]
        own_refs, full_refs = (wq_ref, wk_ref, wv_ref), (fq_ref, fk_ref, fv_ref)
        own = pl.ds(pl.multiple_of(head * half, half), half)
        other = pl.ds(pl.multiple_of((1 - head) * half, half), half)
        core, x, z = place.mine[0], place.mine[bit_x], place.mine[bit_z]

        def rows_of(at_x, at_z, lower=None):
            start = core * (4 * part) + (at_z * 2 + at_x) * part
            if lower is None:
                return pl.ds(pl.multiple_of(start, part), part)
            return pl.ds(pl.multiple_of(start + lower * (part // 2), part // 2), part // 2)

        started = {}

        def start(j, kind, source, where, bit):
            copy = pltpu.make_async_remote_copy(
                src_ref=source, dst_ref=full_refs[j].at[where], send_sem=send.at[j, kind], recv_sem=recv.at[j, kind],
                device_id=place.partner(bit), device_id_type=MESH)
            copy.start()
            started[j, kind] = copy

        bias_copies = [
            pltpu.make_async_remote_copy(
                src_ref=source, dst_ref=target, send_sem=bias_send.at[n], recv_sem=bias_recv.at[n],
                device_id=place.partner(bits - 1), device_id_type=MESH)
            for n, (source, target) in enumerate(((qb_ref, qb_got), (vb_ref, vb_got)))
        ]
        for j in range(3):
            mine = rows_of(x, z)
            start(j, 0, own_refs[j].at[mine, :], (mine, own), bits - 1)
        for copy in bias_copies:
            copy.start()

        def forward(j, kind, where, bit):
            start(j, kind, full_refs[j].at[where], where, bit)

        def stage_one(j):
            started[j, 0].wait_recv()
            where = (rows_of(x, z), other)
            forward(j, 1, where, bit_x)
            forward(j, 2, where, bit_z)
            forward(j, 5, where, 0)

        def stage_two(j):
            started[j, 1].wait_recv()
            forward(j, 4, (rows_of(1 - x, z, 1), other), bit_z)
            forward(j, 6, (rows_of(1 - x, z), other), 0)
            started[j, 2].wait_recv()
            forward(j, 3, (rows_of(x, 1 - z, 0), other), bit_x)
            forward(j, 7, (rows_of(x, 1 - z), other), 0)

        def stage_three(j):
            for kind, lower in ((3, 0), (4, 1)):
                started[j, kind].wait_recv()
                forward(j, kind + 5, (rows_of(1 - x, 1 - z, lower), other), 0)

        def stage_four(j):
            for kind in range(5, 10):
                started[j, kind].wait_recv()

        def project(j, where, bias):
            value = matmul(x_ref[...], full_refs[j][:, where])
            if bias is not None:
                value = value + bias[...].astype(F32).reshape(1, half)
            (q_ref, k_ref, v_ref)[j][:, where] = value.astype(BF16)

        for j in range(3):
            full_refs[j][:, own] = own_refs[j][...]
        project(0, own, qb_ref)
        project(1, own, None)
        project(2, own, vb_ref)

        def attend(pair):
            attend_pair(q_ref, k_ref, v_ref, ctx_ref, lse_ref, pair, length)

        stage_one(0)
        attend(head * pairs)
        stage_one(1)
        stage_two(0)
        attend(head * pairs + 1)
        stage_one(2)
        stage_two(1)
        stage_three(0)
        attend(head * pairs + 2)
        stage_two(2)
        stage_three(1)
        stage_three(2)
        for copy in bias_copies:
            copy.wait_recv()
        stage_four(0)
        project(0, other, qb_got)
        stage_four(1)
        project(1, other, None)
        stage_four(2)
        project(2, other, vb_got)

        outs = []
        for n, (source, target) in enumerate((
            (q_ref, q_out), (k_ref, k_out), (v_ref, v_out), (fq_ref, fq_out), (fk_ref, fk_out), (fv_ref, fv_out))):
            copy = pltpu.make_async_copy(source, target, out_sem.at[n])
            copy.start()
            outs.append(copy)

        def late(n, carry):
            attend((1 - head) * pairs + n)
            return carry

        lax.fori_loop(0, pairs, late, 0)
        for copy in outs:
            copy.wait()
        for copy in started.values():
            copy.wait_send()
        for copy in bias_copies:
            copy.wait_send()

    anywhere = pl.BlockSpec(memory_space=pl.ANY)
    vmem = pl.BlockSpec(memory_space=pltpu.VMEM)
    act = jax.ShapeDtypeStruct((rows, width), BF16)
    full = jax.ShapeDtypeStruct((depth, width), BF16)
    return pl.pallas_call(
        kernel,
        out_shape=[act] * 4 + [jax.ShapeDtypeStruct((2 * pairs, 2, rows), F32)] + [full] * 3,
        in_specs=[pl.BlockSpec(memory_space=pltpu.SMEM)] + [vmem] * 6,
        out_specs=[anywhere] * 3 + [vmem] * 2 + [anywhere] * 3,
        scratch_shapes=[pltpu.VMEM((rows, width), BF16)] * 3 + [pltpu.VMEM((depth, width), BF16)] * 3
        + [pltpu.VMEM((half,), BF16)] * 2 + [pltpu.SemaphoreType.DMA((3, kinds))] * 2
        + [pltpu.SemaphoreType.DMA((2,))] * 2 + [pltpu.SemaphoreType.DMA((6,))],
        compiler_params=pltpu.CompilerParams(collective_id=0, has_side_effects=True, vmem_limit_bytes=VMEM_LIMIT),
        name="attention_forward",
    )(lengths, inputs, *weights, *biases)


def gelu_parts(v):
    x = jnp.abs(v) * 0.7071067811865476
    t = 1.0 / (1.0 + 0.3275911 * x)
    bell = jnp.exp(-0.5 * (v * v))
    tail = 0.5 * bell * t * (
        0.254829592 + t * (-0.284496736 + t * (1.421413741 + t * (-1.453152027 + t * 1.061405429))))
    phi = jnp.where(v >= 0, 1.0 - tail, tail)
    return v * phi, phi + v * bell * 0.3989422804014327


ROW_BLOCK = 64


def over_rows(rows, step, carry):
    def one(n, kept):
        return step(pl.ds(pl.multiple_of(n * ROW_BLOCK, ROW_BLOCK), ROW_BLOCK), kept)

    return lax.fori_loop(0, rows // ROW_BLOCK, one, carry)


OUT_BIAS, FIRST_GAIN, FIRST_SHIFT, DOWN_BIAS, SECOND_GAIN, SECOND_SHIFT, POOL_BIAS, CLASS_BIAS, UP_BIAS = range(9)
LOSS = 12
CLASS_ROWS = (6, 7, 13)


def orders(bits):
    head = bits - 1
    rest = list(range(2, head))
    both = [[0, 1, head] + rest, [0, head, 1] + rest]
    return [both + [[0] + rest[:1] + pair + rest[1:]] for pair in ([1, head], [head, 1])]


def rest_of_layer(context, inputs, class_turned, out_weight, vectors, log_totals, cotangent, up_weight, down_weight,
                  pool_weight, queries, keys, values, full, lengths, labels, bits):
    rows, width = inputs.shape
    hidden = up_weight.shape[1]
    half = width // 2
    times = hidden // width
    devices = 1 << bits
    block = 2 * width // devices
    classes = class_turned.shape[0]
    per_width = width // 128
    fact_rows = -(-2 * per_width // 16) * 16
    small_half = 8
    late_lanes = width // 3
    plans = orders(bits)
    parts = len(plans[0])
    lanes_part = half // parts
    count = 2 * times + 4
    out_at, query_at = 2 * times, 2 * times + 1
    stages = bits
    head = bits - 1
    small_order = [1, head] + list(range(2, head)) + [0]
    pairs = width // 128
    dp_dims = (2,) * (bits - 1)

    def kernel(lengths_ref, labels_ref, ctx_ref, x_ref, cls_in, ow_ref, v0, v1, v2, v3, v4, v5, v6, v7, v8, lse_ref,
               cot_hbm, up_hbm, down_hbm, pool_hbm, q_hbm, k_hbm, v_hbm, wq_hbm, wk_hbm, wv_hbm,
               states_out, grad_out, logit_ref, sums_ref, small_out, late_out, factor_out, held, *rest):
        got = rest[:stages]
        (gb_ref, up_w, down_w, pool_w, low_ref, n1, r1, n2, r2, hid_even, hid_odd, slope_even, slope_odd, acc, whole, frow, vec_ref, cls_ref, small_ref,
         small_buf, small_got, late_buf, late_got, load_sem, late_sem, send, recv, side_send, side_recv, whole_sem) = rest[stages:]
        place = Place(bits)
        loads = []
        for i, (source, target) in enumerate(
            ((up_hbm, up_w), (down_hbm, down_w), (pool_hbm, pool_w), (cot_hbm, gb_ref))):
            load = pltpu.make_async_copy(source, target, load_sem.at[i])
            load.start()
            loads.append(load)
        place.greet(range(bits))
        length = lengths_ref[place.head]
        slot = sum(place.mine[bit] * (1 << k) for k, bit in enumerate(small_order))
        hids, slopes = (hid_even, hid_odd), (slope_even, slope_odd)

        def index(i, done, fixed):
            out = [i]
            for bit in reversed(range(bits)):
                out.append(fixed[bit] if bit in fixed else place.mine[bit] if bit in done else slice(None))
            return tuple(out)

        def part_copy(i, s):
            plan = plans[i // parts % 2][i % parts]
            bit = plan[s]
            return pltpu.make_async_remote_copy(
                src_ref=held.at[index(i, plan[:s], {bit: 1 - place.mine[bit]})], dst_ref=got[s].at[i],
                send_sem=send.at[i, s], recv_sem=recv.at[i, s], device_id=place.partner(bit), device_id_type=MESH)

        def add_part(i, s):
            part_copy(i, s).wait_recv()
            where = index(i, plans[i // parts % 2][i % parts][: s + 1], {})
            if s == stages - 1:
                sums_ref[i] = held[where].astype(F32) + got[s][i].astype(F32)
            else:
                held[where] = held[where] + got[s][i]

        def take(name):
            for code in SCHEDULE[name]:
                if code >= 2000:
                    side_advance(code // 1000 - 2, code % 10)
                    continue
                i, s = code // 100 * parts + code // 10 % 10, code % 10
                if s > 0:
                    add_part(i, s - 1)
                if s < stages:
                    part_copy(i, s).start()

        def take_after(step, prefix, steps):
            for n in steps:
                if not SCHEDULE[prefix + str(n)]:
                    continue

                @pl.when(step == n)
                def _():
                    take(prefix + str(n))

        def put(i, wide, lead):
            for h in range(2):
                for m in range(parts):
                    at = h * half + m * lanes_part
                    held[(i * parts + m, h) + lead] = wide[..., at : at + lanes_part]

        def side_copy(kind, s):
            bit = small_order[s % stages]
            if kind == 0:
                start = (slot // (1 << s)) * (1 << s)
                source = target = factor_out.at[pl.ds(start, 1 << s)]
            elif kind == 2:
                source, target = late_buf.at[s], late_got.at[s]
            else:
                bit = small_order[(s - 1) % stages]
                if s == 0:
                    source, target = small_ref.at[rows_of_core(1 - place.mine[0])], small_got.at[0]
                elif s == stages:
                    source = target = small_out.at[rows_of_core(place.mine[0])]
                else:
                    source, target = small_buf.at[s], small_got.at[s]
            return pltpu.make_async_remote_copy(
                src_ref=source, dst_ref=target, send_sem=side_send.at[kind, s], recv_sem=side_recv.at[kind, s],
                device_id=place.partner(bit), device_id_type=MESH)

        def rows_of_core(core):
            return pl.ds(pl.multiple_of(core * small_half, small_half), small_half)

        def side_advance(kind, s):
            last = stages + (kind == 1)
            if s > 0:
                side_copy(kind, s - 1).wait_recv()
            if kind == 1 and 0 < s < last:
                mine = rows_of_core(place.mine[0])
                total = (small_ref[mine, :] if s == 1 else small_buf[s - 1]) + small_got[s - 1]
                if s < stages:
                    small_buf[s] = total
                else:
                    small_out[mine, :] = total
            if kind == 2 and s > 0:
                total = late_buf[s - 1] + late_got[s - 1]
                if s < stages:
                    late_buf[s] = total
                else:
                    late_out[...] = total
            if s < last:
                side_copy(kind, s).start()

        for i, ref in enumerate((v0, v1, v2, v3, v4, v5, v6)):
            vec_ref[i : i + 1, :] = ref[...].astype(F32).reshape(1, width)
        vec_ref[CLASS_BIAS : CLASS_BIAS + 1, 0:classes] = v7[...].astype(F32).reshape(1, classes)
        wide_bias = v8[...].astype(F32).reshape(1, hidden)
        for t in range(times):
            vec_ref[UP_BIAS + t : UP_BIAS + t + 1, :] = wide_bias[:, t * width : (t + 1) * width]
        cls_ref[...] = jnp.zeros_like(cls_ref)
        cls_ref[0:classes, :] = cls_in[...]

        def vec(i):
            return vec_ref[i : i + 1, :]

        acc[...] = matmul(ctx_ref[...], ow_ref[...])

        def norm_one(at, carry):
            value = x_ref[at, :].astype(F32) + (acc[at, :] + vec(OUT_BIAS))
            center = value - jnp.mean(value, -1, keepdims=True)
            scale = lax.rsqrt(jnp.mean(center * center, -1, keepdims=True) + EPSILON)
            normal = center * scale
            n1[at, :] = normal
            r1[at, :] = scale
            low_ref[at, :] = (normal * vec(FIRST_GAIN) + vec(FIRST_SHIFT)).astype(BF16)
            acc[at, :] = jnp.zeros_like(normal)
            return carry

        over_rows(rows, norm_one, 0)
        loads[0].wait()
        loads[1].wait()

        def at_chunk(c):
            return pl.ds(pl.multiple_of(c * width, width), width)

        def pre_of(c, parity):
            slopes[parity][:, at_chunk(c // 2)] = matmul(low_ref[...], up_w[:, at_chunk(c)]) + vec_ref[pl.ds(UP_BIAS + c, 1), :]

        def activate(c, parity):
            at = at_chunk(c // 2)
            act, deriv = gelu_parts(slopes[parity][:, at])
            hids[parity][:, at] = act.astype(BF16)
            slopes[parity][:, at] = deriv

        def add_branch(c, parity):
            acc[...] += matmul(hids[parity][:, at_chunk(c // 2)], down_w[at_chunk(c), :])

        pre_of(0, 0)
        pre_of(1, 1)
        activate(0, 0)

        def forward(n, carry):
            c = 2 * n
            pre_of(c + 2, 0)
            activate(c + 1, 1)
            add_branch(c, 0)
            pre_of(c + 3, 1)
            activate(c + 2, 0)
            add_branch(c + 1, 1)
            return carry

        lax.fori_loop(0, times // 2 - 1, forward, 0)
        activate(times - 1, 1)
        add_branch(times - 2, 0)
        add_branch(times - 1, 1)

        def norm_two(at, carry):
            first = n1[at, :] * vec(FIRST_GAIN) + vec(FIRST_SHIFT)
            value = first + (acc[at, :] + vec(DOWN_BIAS))
            center = value - jnp.mean(value, -1, keepdims=True)
            scale = lax.rsqrt(jnp.mean(center * center, -1, keepdims=True) + EPSILON)
            normal = center * scale
            n2[at, :] = normal
            r2[at, :] = scale
            whole[at, :] = (normal * vec(SECOND_GAIN) + vec(SECOND_SHIFT)).astype(BF16)
            return carry

        over_rows(rows, norm_two, 0)
        states_copy = pltpu.make_async_copy(whole, states_out, whole_sem.at[0])
        states_copy.start()

        loads[2].wait()
        loads[3].wait()
        lead = whole[0:16, :]
        pooled = jnp.tanh(matmul(lead, pool_w[...]) + vec(POOL_BIAS))
        pooled_low = pooled.astype(BF16)
        logits = nt(pooled_low, cls_ref[...]) + vec_ref[CLASS_BIAS : CLASS_BIAS + 1, 0:128]
        lanes = lane_iota(logits.shape)
        logits = jnp.where(lanes < classes, logits, NEGATIVE)
        top = jnp.max(logits, -1, keepdims=True)
        norm = top + jnp.log(jnp.sum(jnp.exp(logits - top), -1, keepdims=True))
        target = jnp.where(lanes == labels_ref[0], 1.0, 0.0)
        loss = (norm - jnp.sum(jnp.where(lanes < classes, target * logits, 0.0), -1, keepdims=True)) / devices
        grad_logits = (jnp.where(lanes < classes, jnp.exp(logits - norm) - target, 0.0) / devices).astype(BF16)
        grad_pooled = (matmul(grad_logits, cls_ref[...]) * (1.0 - pooled * pooled)).astype(BF16)
        grad_lead = nt(grad_pooled, pool_w[...])
        logit_ref[...] = logits[0:1, 0:classes]
        frow[...] = jnp.zeros_like(frow)
        for k, value in enumerate((lead, grad_pooled)):
            wide = value.astype(F32)
            for j in range(per_width):
                frow[k * per_width + j : k * per_width + j + 1, :] = wide[0:1, j * 128 : (j + 1) * 128]
        small_ref[...] = jnp.zeros(small_ref.shape, F32)
        logit_row = grad_logits.astype(F32)[0:1, :]
        pooled_row = pooled_low.astype(F32)[0:1, :]
        for k in range(classes):
            small_ref[CLASS_ROWS[k] : CLASS_ROWS[k] + 1, :] = logit_row[:, k : k + 1] * pooled_row
        factor_out[slot] = frow[...].astype(BF16)
        take("R")

        def back_two(at, sums):
            gain_sum, shift_sum, bias_sum = sums
            row = at.start + lax.broadcasted_iota(jnp.int32, (ROW_BLOCK, width), 0)
            grad = gb_ref[at, :].astype(F32) + jnp.where(row == 0, grad_lead[0:1, :], 0.0)
            normal = n2[at, :]
            e = grad * vec(SECOND_GAIN)
            value = (e - jnp.mean(e, -1, keepdims=True) - normal * jnp.mean(e * normal, -1, keepdims=True)) * r2[at, :]
            rounded = value.astype(BF16)
            acc[at, :] = value
            gb_ref[at, :] = rounded
            return (gain_sum + jnp.sum(grad * normal, 0, keepdims=True), shift_sum + jnp.sum(grad, 0, keepdims=True),
                    bias_sum + jnp.sum(rounded.astype(F32), 0, keepdims=True))

        zero = jnp.zeros((1, width), F32)
        gain_sum, shift_sum, bias_sum = over_rows(rows, back_two, (zero, zero, zero))
        small_ref[SECOND_GAIN : SECOND_GAIN + 1, :] = gain_sum
        small_ref[SECOND_SHIFT : SECOND_SHIFT + 1, :] = shift_sum
        small_ref[DOWN_BIAS : DOWN_BIAS + 1, :] = bias_sum
        small_ref[LOSS : LOSS + 1, 0:128] = jnp.broadcast_to(loss[0:1, 0:1], (1, 128))
        small_ref[LOSS : LOSS + 1, 128:256] = logit_row

        take("B")

        def down_grads(n, carry):
            for parity in range(2):
                c = 2 * n + parity
                wide = tn(hids[parity][:, at_chunk(n)], gb_ref[...]).astype(BF16).reshape(2, 2, times, block, width)
                for t in range(times):
                    put(t, wide[:, :, t], (lax.rem(c // 2, 2), lax.rem(c, 2)))
                take_after(c, "D", range(parity, times, 2))
            return carry

        lax.fori_loop(0, times // 2, down_grads, 0)

        for parity in range(2):

            def up_grads(h, carry):
                c = 2 * h + parity
                step = 4 * parity + 2 * h
                grad = (nt(gb_ref[...], down_w[at_chunk(c), :]) * slopes[parity][:, at_chunk(h)]).astype(BF16)
                small_ref[pl.ds(UP_BIAS + c, 1), :] = jnp.sum(grad.astype(F32), 0, keepdims=True)
                wide = tn(low_ref[...], grad).astype(BF16)
                for t in range(2):
                    for m in range(parts):
                        at = t * half + m * lanes_part
                        held[(times + 2 * parity + t) * parts + m, h] = wide[:, at : at + lanes_part].reshape(
                            dp_dims + (block, lanes_part))
                take_after(step, "U", range(4 * parity, 4 * parity + 4, 2))
                acc[...] += nt(grad, up_w[:, at_chunk(c)])
                take_after(step + 1, "U", range(4 * parity + 1, 4 * parity + 4, 2))
                return carry

            lax.fori_loop(0, 2, up_grads, 0)

        late = []
        for i, (source, target) in enumerate((
            (q_hbm, down_w.at[0:rows, :]), (k_hbm, down_w.at[rows : 2 * rows, :]),
            (v_hbm, down_w.at[2 * rows : 3 * rows, :]), (wq_hbm, up_w.at[:, 0:width]),
            (wk_hbm, up_w.at[:, width : 2 * width]), (wv_hbm, up_w.at[:, 2 * width : 3 * width]),
        )):
            load = pltpu.make_async_copy(source, target, late_sem.at[i])
            load.start()
            late.append(load)

        def back_one(at, sums):
            gain_sum, shift_sum, bias_sum = sums
            grad = acc[at, :]
            normal = n1[at, :]
            e = grad * vec(FIRST_GAIN)
            value = (e - jnp.mean(e, -1, keepdims=True) - normal * jnp.mean(e * normal, -1, keepdims=True)) * r1[at, :]
            rounded = value.astype(BF16)
            acc[at, :] = value
            low_ref[at, :] = rounded
            return (gain_sum + jnp.sum(grad * normal, 0, keepdims=True), shift_sum + jnp.sum(grad, 0, keepdims=True),
                    bias_sum + jnp.sum(rounded.astype(F32), 0, keepdims=True))

        gain_sum, shift_sum, bias_sum = over_rows(rows, back_one, (zero, zero, zero))
        small_ref[FIRST_GAIN : FIRST_GAIN + 1, :] = gain_sum
        small_ref[FIRST_SHIFT : FIRST_SHIFT + 1, :] = shift_sum
        small_ref[OUT_BIAS : OUT_BIAS + 1, :] = bias_sum
        take("L0")
        put(out_at, tn(ctx_ref[...], low_ref[...]).astype(BF16).reshape(dp_dims + (block, width)), ())
        take("L1")
        hids[1][:, width : 2 * width] = nt(low_ref[...], ow_ref[...]).astype(BF16)
        take("L2")

        lanes_row = lax.broadcasted_iota(jnp.int32, (128, rows), 0)
        pair_lanes = lane_iota((rows, 128))
        for load in late:
            load.wait()

        def attend(pair, carry):
            def at(n):
                return pl.ds(pl.multiple_of(n % 2 * width + pair * 128, 128), 128)

            q2 = down_w[0:rows, at(0)]
            k2 = down_w[rows : 2 * rows, at(0)]
            v2 = down_w[2 * rows : 3 * rows, at(0)]
            g2 = hids[1][:, at(3)]
            k2t = k2.T
            heads_of = []
            for parity in range(2):
                qa, ka = pair_operands(q2, k2, length, parity)
                mine = (pair_lanes < HEAD_DIM) if parity == 0 else (pair_lanes >= HEAD_DIM)
                va = jnp.where(mine, v2.astype(F32), 0.0).astype(BF16)
                probs = jnp.exp(nt(ka, qa) - lse_ref[pair, parity : parity + 1, :])
                grad_v = matmul(probs.astype(BF16), g2)
                grad_probs = nt(va, g2)
                inner = jnp.sum(probs * grad_probs, 0, keepdims=True)
                grad_scores = (probs * (grad_probs - inner)).astype(BF16)
                heads_of.append((grad_v, matmul(grad_scores, qa), matmul(k2t, grad_scores)))
                take_after(2 * pair + parity, "P", range(parity, 2 * pairs, 2))
            first = pair_lanes < HEAD_DIM
            turned = jnp.where(lanes_row < HEAD_DIM, heads_of[0][2], heads_of[1][2]) * HEAD_DIM ** -0.5
            hids[0][:, at(0)] = turned.T.astype(BF16)
            hids[0][:, at(1)] = jnp.where(first, heads_of[0][1], heads_of[1][1]).astype(BF16)
            hids[1][:, at(2)] = jnp.where(first, heads_of[0][0], heads_of[1][0]).astype(BF16)
            return carry

        lax.fori_loop(0, pairs, attend, 0)

        def grads_of(n):
            return hids[n // 2][:, n % 2 * width : (n % 2 + 1) * width]

        late_buf[0] = jnp.zeros(late_buf.shape[1:], F32)
        for n in range(2):
            total = jnp.sum(grads_of(2 * n).astype(F32), 0, keepdims=True)
            for t in range(3):
                late_buf[0, 3 * n + t : 3 * n + t + 1, :] = total[:, t * late_lanes : (t + 1) * late_lanes]
        take("Q")
        for n in range(3):
            put(query_at + n, tn(x_ref[...], grads_of(n)).astype(BF16).reshape(dp_dims + (block, width)), ())
            take("W" + str(n))
        states_copy.wait()
        for n in range(3):
            acc[...] += nt(grads_of(n), up_w[:, n * width : (n + 1) * width])
            take("I" + str(n))
        whole[...] = acc[...].astype(BF16)
        grad_copy = pltpu.make_async_copy(whole, grad_out, whole_sem.at[1])
        grad_copy.start()
        for n in range(4):
            take("T" + str(n))
        grad_copy.wait()
        for i in range(count * parts):
            for s in range(stages):
                part_copy(i, s).wait_send()
        for s in range(stages):
            for kind in range(3):
                side_copy(kind, s).wait_send()
        side_copy(1, stages).wait_send()

    vmem = pl.BlockSpec(memory_space=pltpu.VMEM)
    anywhere = pl.BlockSpec(memory_space=pl.ANY)
    smem = pl.BlockSpec(memory_space=pltpu.SMEM)
    act = jax.ShapeDtypeStruct((rows, width), BF16)
    return pl.pallas_call(
        kernel,
        out_shape=[
            act, act, jax.ShapeDtypeStruct((1, classes), F32), jax.ShapeDtypeStruct((count * parts, block, lanes_part), F32),
            jax.ShapeDtypeStruct((16, width), F32), jax.ShapeDtypeStruct((8, late_lanes), F32),
            jax.ShapeDtypeStruct((devices, fact_rows, 128), BF16),
        ],
        in_specs=[smem] * 2 + [vmem] * 14 + [anywhere] * 10,
        out_specs=[anywhere] * 2 + [vmem] * 5,
        scratch_shapes=[pltpu.VMEM((count * parts, 2) + dp_dims + (block, lanes_part), BF16)]
        + [pltpu.VMEM((count * parts,) + (2,) * (stages - 1 - s) + (block, lanes_part), BF16) for s in range(stages)]
        + [
            pltpu.VMEM((rows, width), BF16),
            pltpu.VMEM((width, hidden), BF16),
            pltpu.VMEM((hidden, width), BF16),
            pltpu.VMEM((width, width), BF16),
            pltpu.VMEM((rows, width), BF16),
            pltpu.VMEM((rows, width), F32),
            pltpu.VMEM((rows, 1), F32),
            pltpu.VMEM((rows, width), F32),
            pltpu.VMEM((rows, 1), F32),
            pltpu.VMEM((rows, hidden // 2), BF16),
            pltpu.VMEM((rows, hidden // 2), BF16),
            pltpu.VMEM((rows, hidden // 2), F32),
            pltpu.VMEM((rows, hidden // 2), F32),
            pltpu.VMEM((rows, width), F32),
            pltpu.VMEM((rows, width), BF16),
            pltpu.VMEM((fact_rows, 128), F32),
            pltpu.VMEM((16, width), F32),
            pltpu.VMEM((128, width), BF16),
            pltpu.VMEM((16, width), F32),
            pltpu.VMEM((stages, small_half, width), F32),
            pltpu.VMEM((stages, small_half, width), F32),
            pltpu.VMEM((stages, 8, late_lanes), F32),
            pltpu.VMEM((stages, 8, late_lanes), F32),
            pltpu.SemaphoreType.DMA((4,)),
            pltpu.SemaphoreType.DMA((6,)),
            pltpu.SemaphoreType.DMA((count * parts, stages)),
            pltpu.SemaphoreType.DMA((count * parts, stages)),
            pltpu.SemaphoreType.DMA((3, stages + 1)),
            pltpu.SemaphoreType.DMA((3, stages + 1)),
            pltpu.SemaphoreType.DMA((2,)),
        ],
        compiler_params=pltpu.CompilerParams(collective_id=1, has_side_effects=True, vmem_limit_bytes=VMEM_LIMIT),
        name="rest_of_layer",
    )(lengths, labels, context, inputs, class_turned, out_weight, *vectors, log_totals, cotangent, up_weight,
      down_weight, pool_weight, queries, keys, values, *full)


SCHEDULE = {
    "R": (),
    "B": (),
    "D0": (),
    "D1": (),
    "D2": (),
    "D3": (0, 10, 20, 100, 110, 120,),
    "U0": (200, 210, 220, 300, 310,),
    "U1": (1, 11, 320,),
    "U2": (21, 101, 111, 121, 400, 410, 420, 500, 510, 520,),
    "U3": (201, 211,),
    "U4": (2, 12, 221,),
    "U5": (301, 311,),
    "U6": (22, 321, 102, 600, 610, 620, 700, 710, 720,),
    "U7": (421, 112, 122,),
    "L0": (3000,),
    "L1": (202, 212, 800, 810, 820,),
    "L2": (3, 222, 411,),
    "P0": (13, 312, 521,),
    "P1": (401, 23, 2000,),
    "P2": (103, 302,),
    "P3": (113, 123, 203, 322, 4, 3001,),
    "P4": (14, 213, 223, 422, 511, 621,),
    "P5": (412, 2001,),
    "P6": (24, 104, 313, 522, 5, 501, 721,),
    "P7": (15, 114, 124, 204, 402, 323, 3002,),
    "P8": (214, 224, 303, 423, 601, 611,),
    "P9": (25, 413, 821, 105, 2002,),
    "P10": (115, 314, 512, 711,),
    "P11": (125, 205, 523, 215, 622, 3003,),
    "Q": (225, 324, 403, 4000,),
    "W0": (304, 424, 502, 701, 900, 910, 920,),
    "W1": (414, 315, 722, 1000, 1010, 1020, 2003,),
    "W2": (602, 612, 1100, 1110, 1120,),
    "I0": (325, 524, 404, 513, 822, 811, 921, 3004,),
    "I1": (305, 425, 712,),
    "I2": (415, 503, 623, 801, 1021, 4001,),
    "T0": (901, 911, 1001, 1011, 1101, 1111, 1121, 514, 702, 723, 525, 405, 613, 603, 922, 823, 504, 713, 515, 812,
        2004, 3005, 4002,),
    "T1": (624, 1022, 802, 505, 912, 625, 1122, 614, 902, 604, 1012, 714, 1002, 615, 1112, 605, 715, 703, 1102,
        724, 4003, 3006,),
    "T2": (923, 824, 813, 704, 803, 1023, 1123, 725, 913, 814, 825, 903, 804, 705, 1013, 1003, 1113, 914, 924,
        1103, 2005, 4004,),
    "T3": (904, 815, 1124, 1024, 1014, 805, 1004, 1114, 1104, 915, 925, 905, 1125, 1025, 1015, 1005, 1115, 1105,
        4005,),
}


def spread(states, input_grad, logits, sums, small, late, gathered, classes):
    width = small.shape[1]
    half = width // 2
    parts, block, lanes_part = sums.shape
    count = parts * lanes_part // half
    parts = parts // count
    devices = gathered.shape[0]
    times = (count - 4) // 2
    lanes = width // 128

    def kernel(states_ref, grad_ref, logits_ref, sums_ref, small_ref, late_ref, got_ref, states_out, grad_out, logits_out, up, down,
               out, query, key, value, pool, query_bias, value_bias, out_bias, first_gain, first_shift, up_bias,
               down_bias, second_gain, second_shift, pool_bias, class_weight, class_bias, loss, left, right, late_wide, sem):
        copies = [
            pltpu.make_async_copy(states_ref, states_out, sem.at[0]), pltpu.make_async_copy(grad_ref, grad_out, sem.at[1])]
        for copy in copies:
            copy.start()
        logits_out[...] = logits_ref[...]
        dp, head = lax.axis_index("dp"), lax.axis_index("head")
        for m in range(parts):
            at = slice(m * lanes_part, (m + 1) * lanes_part)
            for t in range(times):
                down[t * block : (t + 1) * block, at] = sums_ref[t * parts + m]
                up[:, t * half + m * lanes_part : t * half + (m + 1) * lanes_part] = sums_ref[(times + t) * parts + m]
            for k, ref in enumerate((out, query, key, value)):
                ref[:, at] = sums_ref[(2 * times + k) * parts + m]
        got = got_ref[...].astype(F32)

        def wide(k):
            return jnp.concatenate([got[:, k * lanes + j, :] for j in range(lanes)], 1)

        lead, grad_pooled = wide(0), wide(1)
        left[...] = lead.T
        right[...] = grad_pooled
        at = pl.ds(pl.multiple_of(head * half, half), half)
        pool[...] = matmul(
            left[pl.ds(pl.multiple_of(dp * block, 8), block), :].astype(BF16), right[:, at].astype(BF16))
        pool_bias[...] = jnp.sum(grad_pooled, 0)
        for k in range(classes):
            class_weight[k : k + 1, :] = small_ref[CLASS_ROWS[k] : CLASS_ROWS[k] + 1, :]
        class_bias[...] = small_ref[LOSS : LOSS + 1, 128 : 128 + classes].reshape(classes)
        for n in range(2):
            late_wide[n : n + 1, :] = jnp.concatenate([late_ref[3 * n + t : 3 * n + t + 1, :] for t in range(3)], 1)
        query_bias[...] = late_wide[0:1, at].reshape(half)
        value_bias[...] = late_wide[1:2, at].reshape(half)
        for ref, row in ((out_bias, OUT_BIAS), (first_gain, FIRST_GAIN), (first_shift, FIRST_SHIFT),
                         (down_bias, DOWN_BIAS), (second_gain, SECOND_GAIN), (second_shift, SECOND_SHIFT)):
            ref[...] = small_ref[row, :]
        up_bias[...] = jnp.concatenate(
            [small_ref[UP_BIAS + t : UP_BIAS + t + 1, :] for t in range(times)], 1).reshape(times * width)
        loss[()] = small_ref[LOSS, 0]
        for copy in copies:
            copy.wait()

    def f32(*shape):
        return jax.ShapeDtypeStruct(shape, F32)

    square = f32(block, half)
    row = f32(width)
    act = jax.ShapeDtypeStruct(states.shape, BF16)
    vmem = pl.BlockSpec(memory_space=pltpu.VMEM)
    anywhere = pl.BlockSpec(memory_space=pl.ANY)
    return pl.pallas_call(
        kernel,
        out_shape=[
            act, act, f32(1, classes), f32(block, times * half), f32(times * block, half), square, square, square, square,
            square, f32(half), f32(half), row, row, row, f32(times * width), row, row, row, row, f32(classes, width),
            f32(classes), f32(),
        ],
        in_specs=[vmem] * 7,
        out_specs=[anywhere] * 2 + [vmem] * 20 + [pl.BlockSpec(memory_space=pltpu.SMEM)],
        scratch_shapes=[
            pltpu.VMEM((width, devices), F32), pltpu.VMEM((devices, width), F32),
            pltpu.VMEM((8, width), F32), pltpu.SemaphoreType.DMA((2,))],
        compiler_params=pltpu.CompilerParams(vmem_limit_bytes=VMEM_LIMIT),
        name="spread",
    )(states, input_grad, logits, sums, small, late, gathered)


def plain_body(
    inputs, lengths, labels, state_cotangent, query_weight, query_bias, key_weight, value_weight, value_bias,
    out_weight, out_bias, first_gain, first_shift, up_weight, up_bias, down_weight, down_bias, second_gain,
    second_shift, pool_weight, pool_bias, class_weight, class_bias,
):
    scale = HEAD_DIM ** (-0.5)
    dp_size, head_size = lax.axis_size("dp"), lax.axis_size("head")
    dp_at, head_at = lax.axis_index("dp"), lax.axis_index("head")
    devices = dp_size * head_size
    width = inputs.shape[1]
    block_columns = width // head_size
    row_seqs = labels.shape[0]
    assert row_seqs == 1 and inputs.shape[0] == SEQ_LEN
    length = lax.dynamic_index_in_dim(lengths, head_at, keepdims=False)

    weights = [query_weight, key_weight, value_weight]
    full = [lax.all_gather(w, "head", axis=1, tiled=True) for w in weights]
    biases = lax.all_gather(jnp.stack([query_bias, value_bias]), "head", axis=1, tiled=True)
    query_bias, value_bias = biases[0], biases[1]
    wq, wk, wv = full
    head_count = width // HEAD_DIM

    def heads(matrix):
        return matrix.reshape(SEQ_LEN, head_count, HEAD_DIM)

    queries = (matmul(inputs, wq) + query_bias).astype(BF16)
    keys_low = matmul(inputs, wk).astype(BF16)
    values_low = (matmul(inputs, wv) + value_bias).astype(BF16)
    visible = lax.broadcasted_iota(jnp.int32, (1, 1, SEQ_LEN), 2) < length

    def scores_of():
        raw = jnp.einsum("qhd,khd->hqk", heads(queries), heads(keys_low), preferred_element_type=F32) * scale
        return jnp.where(visible, raw, NEGATIVE)

    scores = scores_of()
    peak = jnp.max(scores, -1, keepdims=True)
    raised = jnp.exp(scores - peak)
    denominator = jnp.sum(raised, -1, keepdims=True)
    probs = raised / denominator
    log_total = peak + jnp.log(denominator)
    context = jnp.einsum("hqk,khd->qhd", probs.astype(BF16), heads(values_low), preferred_element_type=F32)
    context_rows = context.astype(BF16).reshape(SEQ_LEN, width)
    attended = matmul(context_rows, out_weight) + out_bias
    first_out, first_back = jax.vjp(
        normalize, inputs.astype(F32) + attended, first_gain.astype(F32), first_shift.astype(F32))
    first_low = first_out.astype(BF16)
    hidden_pre = matmul(first_low, up_weight) + up_bias
    hidden_act, gelu_back = jax.vjp(partial(jax.nn.gelu, approximate=False), hidden_pre)
    hidden_low = hidden_act.astype(BF16)
    branch = matmul(hidden_low, down_weight) + down_bias
    normed, second_back = jax.vjp(normalize, first_out + branch, second_gain.astype(F32), second_shift.astype(F32))
    leading_low = normed.reshape(row_seqs, SEQ_LEN, -1)[:, 0].astype(BF16)
    pooled = jnp.tanh(matmul(leading_low, pool_weight) + pool_bias)
    pooled_low = pooled.astype(BF16)
    logits = matmul(pooled_low, class_weight) + class_bias
    classes = lax.broadcasted_iota(jnp.int32, logits.shape, 1)
    target = (classes == labels[:, None]).astype(F32)
    log_norm = jax.nn.logsumexp(logits, axis=-1)
    loss_part = jnp.sum(log_norm - jnp.sum(target * logits, -1)) / devices
    grad_logits = ((jnp.exp(logits - log_norm[:, None]) - target) / devices).astype(BF16)
    grad_class_weight = matmul(pooled_low.T, grad_logits)
    grad_class_bias = column_sums(grad_logits)
    grad_pooled = (matmul(grad_logits, class_weight.T) * (1.0 - pooled * pooled)).astype(BF16)
    grad_pool_bias = column_sums(grad_pooled)
    grad_leading = matmul(grad_pooled, pool_weight.T)
    grad_normed = state_cotangent.astype(F32).reshape(row_seqs, SEQ_LEN, -1)
    grad_normed = grad_normed.at[:, 0].add(grad_leading).reshape(normed.shape)
    grad_second, grad_second_gain, grad_second_shift = second_back(grad_normed)
    grad_branch = grad_second.astype(BF16)
    grad_down_weight = matmul(hidden_low.T, grad_branch)
    grad_down_bias = column_sums(grad_branch)
    grad_hidden = gelu_back(matmul(grad_branch, down_weight.T))[0].astype(BF16)
    grad_up_weight = matmul(first_low.T, grad_hidden)
    grad_up_bias = column_sums(grad_hidden)
    grad_first_out = grad_second + matmul(grad_hidden, up_weight.T)
    grad_first, grad_first_gain, grad_first_shift = first_back(grad_first_out)
    grad_attended = grad_first.astype(BF16)
    grad_out_weight = matmul(context_rows.T, grad_attended)
    grad_out_bias = column_sums(grad_attended)
    grad_context = heads(matmul(grad_attended, out_weight.T).astype(BF16))
    probs_again = jnp.exp(scores_of() - log_total)
    grad_values = jnp.einsum(
        "hqk,qhd->khd", probs_again.astype(BF16), grad_context, preferred_element_type=F32).astype(BF16)
    grad_probs = jnp.einsum("qhd,khd->hqk", grad_context, heads(values_low), preferred_element_type=F32)
    grad_scores = probs_again * (grad_probs - jnp.sum(probs_again * grad_probs, -1, keepdims=True))
    grad_scores = grad_scores.astype(BF16)
    grad_queries = (
        jnp.einsum("hqk,khd->qhd", grad_scores, heads(keys_low), preferred_element_type=F32) * scale).astype(BF16)
    grad_keys = (
        jnp.einsum("hqk,qhd->khd", grad_scores, heads(queries), preferred_element_type=F32) * scale).astype(BF16)
    grad_queries = grad_queries.reshape(SEQ_LEN, width)
    grad_keys = grad_keys.reshape(SEQ_LEN, width)
    grad_values = grad_values.reshape(SEQ_LEN, width)
    grad_query_weight = matmul(inputs.T, grad_queries)
    grad_key_weight = matmul(inputs.T, grad_keys)
    grad_value_weight = matmul(inputs.T, grad_values)
    input_grad = (
        grad_first + matmul(grad_queries, wq.T) + matmul(grad_keys, wk.T) + matmul(grad_values, wv.T)).astype(BF16)

    small_parts = (
        grad_out_bias, grad_first_gain, grad_first_shift, grad_up_bias, grad_down_bias, grad_second_gain,
        grad_second_shift, grad_pool_bias, column_sums(grad_queries), column_sums(grad_values),
        grad_class_weight.reshape(-1), grad_class_bias, loss_part.reshape(1),
    )
    grads = (grad_up_weight, grad_down_weight, grad_out_weight, grad_query_weight, grad_key_weight, grad_value_weight)
    grads = grads + (matmul(leading_low.T, grad_pooled),)

    def scatter(matrix):
        part = lax.psum_scatter(matrix, "dp", scatter_dimension=0, tiled=True)
        return lax.psum_scatter(part.astype(BF16), "head", scatter_dimension=1, tiled=True).astype(F32)

    up_total, down_total, out_total, query_total, key_total, value_total, pool_total = map(scatter, grads)
    totals = lax.psum(small_parts, ("dp", "head"))
    (
        out_bias_total, first_gain_total, first_shift_total, up_bias_total, down_bias_total, second_gain_total,
        second_shift_total, pool_bias_total, query_bias_total, value_bias_total, class_weight_total,
        class_bias_total, loss,
    ) = totals
    query_bias_total = lax.dynamic_slice_in_dim(query_bias_total, head_at * block_columns, block_columns)
    value_bias_total = lax.dynamic_slice_in_dim(value_bias_total, head_at * block_columns, block_columns)
    return (
        normed.astype(BF16), input_grad, logits, loss.reshape(()), query_total, query_bias_total, key_total,
        value_total, value_bias_total, out_total, out_bias_total, first_gain_total, first_shift_total, up_total,
        up_bias_total, down_total, down_bias_total, second_gain_total, second_shift_total, pool_total,
        pool_bias_total, class_weight_total.reshape(class_weight.shape), class_bias_total,
    )


def body(*args):
    (
        inputs, lengths, labels, state_cotangent, query_weight, query_bias, key_weight, value_weight, value_bias,
        out_weight, out_bias, first_gain, first_shift, up_weight, up_bias, down_weight, down_bias, second_gain,
        second_shift, pool_weight, pool_bias, class_weight, class_bias,
    ) = args
    dp_size, head_size = lax.axis_size("dp"), lax.axis_size("head")
    devices = dp_size * head_size
    bits = devices.bit_length() - 1
    rows, width = inputs.shape
    hidden = up_weight.shape[1]
    classes = class_weight.shape[1]
    direct = (
        (width // dp_size) % 16 == 0 and head_size == 2 and bits == 5 and hidden == 4 * width and rows == SEQ_LEN
        and labels.shape[0] == 1 and classes == len(CLASS_ROWS)
    )
    if not direct:
        return plain_body(*args)

    queries, keys, values, context, log_totals, *full = attention_forward(
        inputs, [query_weight, key_weight, value_weight], [query_bias, value_bias], lengths, bits)
    vectors = (out_bias, first_gain, first_shift, down_bias, second_gain, second_shift, pool_bias, class_bias, up_bias)
    states, input_grad, logits, sums, small, late, gathered = rest_of_layer(
        context, inputs, class_weight.T, out_weight, vectors, log_totals, state_cotangent, up_weight, down_weight,
        pool_weight, queries, keys, values, full, lengths, labels, bits)
    (
        states, input_grad, logits, up, down, out, query, key, value, pool, query_sum, value_sum, out_sum, first_gain_sum,
        first_shift_sum, up_sum, down_sum, second_gain_sum, second_shift_sum, pool_sum, class_sum, class_bias_sum, loss,
    ) = spread(states, input_grad, logits, sums, small, late, gathered, classes)
    return (
        states, input_grad, logits, loss, query, query_sum, key, value, value_sum, out, out_sum, first_gain_sum,
        first_shift_sum, up, up_sum, down, down_sum, second_gain_sum, second_shift_sum, pool, pool_sum, class_sum.T,
        class_bias_sum,
    )


def solution(mesh):
    rows, column, both = P(("dp", "head"), None), P(None, "head"), P("dp", "head")
    one, none = P("head"), P()
    return jax.shard_map(
        body,
        mesh=mesh,
        in_specs=(rows, P("dp"), P(("dp", "head")), rows, column, one, column, column, one) + (none,) * 14,
        out_specs=(
            rows, rows, rows, none, both, one, both, both, one, both, none, none, none, both, none, both, none,
            none, none, both, none, none, none,
        ),
        check_vma=False,
    )
```

```python
from functools import partial

import jax
import jax.numpy as jnp
from jax import lax
from jax.experimental import pallas as pl
from jax.experimental.pallas import tpu as pltpu
from jax.sharding import PartitionSpec as P

HEAD_DIM = 64
SEQ_LEN = 512
NEGATIVE = -1e30
EPSILON = 1e-06
MESH = pl.DeviceIdType.MESH
F32 = jnp.float32
BF16 = jnp.bfloat16
VMEM_LIMIT = 67_000_000


def normalize(values, gain, shift):
    center = values - jnp.mean(values, -1, keepdims=True)
    spread = jnp.mean(center * center, -1, keepdims=True)
    return center * lax.rsqrt(spread + EPSILON) * gain + shift


def matmul(left, right):
    return jnp.dot(left, right, preferred_element_type=F32)


def column_sums(values):
    return jnp.sum(values.astype(F32), 0)


class Place:
    def __init__(self, bits):
        self.bits = bits
        self.dp = lax.axis_index("dp")
        self.head = lax.axis_index("head")
        self.mine = [lax.rem(self.dp // (1 << b), 2) for b in range(bits - 1)] + [self.head]

    def partner(self, bit):
        if bit == self.bits - 1:
            return (self.dp, 1 - self.head)
        return (self.dp + (1 - 2 * self.mine[bit]) * (1 << bit), self.head)

    def greet(self, bits):
        barrier = pltpu.get_barrier_semaphore()
        for bit in bits:
            pl.semaphore_signal(barrier, inc=1, device_id=self.partner(bit), device_id_type=MESH)
        pl.semaphore_wait(barrier, len(bits))


def shared_rows(bits):
    return 1, 2


def lane_iota(shape):
    return lax.broadcasted_iota(jnp.int32, shape, 1)


def first_lanes(shape):
    return lane_iota(shape) < HEAD_DIM


def pair_operands(q2, k2, length, parity):
    lanes = lane_iota(q2.shape)
    rows = lax.broadcasted_iota(jnp.int32, q2.shape, 0)
    mine = (lanes < HEAD_DIM) if parity == 0 else (lanes >= HEAD_DIM)
    spare = lanes == (HEAD_DIM if parity == 0 else 0)
    hidden = jnp.where(rows < length, 0.0, NEGATIVE)
    qa = jnp.where(mine, q2.astype(F32) * HEAD_DIM ** -0.5, jnp.where(spare, 1.0, 0.0)).astype(BF16)
    ka = jnp.where(mine, k2.astype(F32), jnp.where(spare, hidden, 0.0)).astype(BF16)
    return qa, ka


def nt(left, right):
    return lax.dot_general(left, right, (((1,), (1,)), ((), ())), preferred_element_type=F32)


def tn(left, right):
    return lax.dot_general(left, right, (((0,), (0,)), ((), ())), preferred_element_type=F32)


def attend_pair(q_ref, k_ref, v_ref, ctx_ref, lse_ref, pair, length):
    at = pl.ds(pl.multiple_of(pair * 128, 128), 128)
    q2, k2, v2 = q_ref[:, at], k_ref[:, at], v_ref[:, at]
    v2t = v2.T
    rows = lax.broadcasted_iota(jnp.int32, (128, SEQ_LEN), 0)
    parts = []
    for parity in range(2):
        qa, ka = pair_operands(q2, k2, length, parity)
        scores = nt(ka, qa)
        peak = jnp.max(scores, 0, keepdims=True)
        raised = jnp.exp(scores - peak)
        total = jnp.sum(raised, 0, keepdims=True)
        probs = (raised * (1.0 / total)).astype(BF16)
        parts.append(matmul(v2t, probs))
        lse_ref[pair, parity : parity + 1, :] = peak + jnp.log(total)
    joined = jnp.where(rows < HEAD_DIM, parts[0], parts[1])
    ctx_ref[:, at] = joined.T.astype(BF16)


def attention_forward(inputs, weights, biases, lengths, bits):
    rows, width = inputs.shape
    depth, half = weights[0].shape
    part = depth // 8
    pairs = half // 128
    kinds = 10

    def kernel(lengths_ref, x_ref, wq_ref, wk_ref, wv_ref, qb_ref, vb_ref, q_out, k_out, v_out, ctx_ref, lse_ref,
               fq_out, fk_out, fv_out, q_ref, k_ref, v_ref, fq_ref, fk_ref, fv_ref, qb_got, vb_got, send, recv,
               bias_send, bias_recv, out_sem):
        place = Place(bits)
        head = place.head
        bit_x, bit_z = shared_rows(bits)
        place.greet([0, bit_x, bit_z, bits - 1])
        length = lengths_ref[head]
        own_refs, full_refs = (wq_ref, wk_ref, wv_ref), (fq_ref, fk_ref, fv_ref)
        own = pl.ds(pl.multiple_of(head * half, half), half)
        other = pl.ds(pl.multiple_of((1 - head) * half, half), half)
        core, x, z = place.mine[0], place.mine[bit_x], place.mine[bit_z]

        def rows_of(at_x, at_z, lower=None):
            start = core * (4 * part) + (at_z * 2 + at_x) * part
            if lower is None:
                return pl.ds(pl.multiple_of(start, part), part)
            return pl.ds(pl.multiple_of(start + lower * (part // 2), part // 2), part // 2)

        started = {}

        def start(j, kind, source, where, bit):
            copy = pltpu.make_async_remote_copy(
                src_ref=source, dst_ref=full_refs[j].at[where], send_sem=send.at[j, kind], recv_sem=recv.at[j, kind],
                device_id=place.partner(bit), device_id_type=MESH)
            copy.start()
            started[j, kind] = copy

        bias_copies = [
            pltpu.make_async_remote_copy(
                src_ref=source, dst_ref=target, send_sem=bias_send.at[n], recv_sem=bias_recv.at[n],
                device_id=place.partner(bits - 1), device_id_type=MESH)
            for n, (source, target) in enumerate(((qb_ref, qb_got), (vb_ref, vb_got)))
        ]
        for j in range(3):
            mine = rows_of(x, z)
            start(j, 0, own_refs[j].at[mine, :], (mine, own), bits - 1)
        for copy in bias_copies:
            copy.start()

        def forward(j, kind, where, bit):
            start(j, kind, full_refs[j].at[where], where, bit)

        def stage_one(j):
            started[j, 0].wait_recv()
            where = (rows_of(x, z), other)
            forward(j, 1, where, bit_x)
            forward(j, 2, where, bit_z)
            forward(j, 5, where, 0)

        def stage_two(j):
            started[j, 1].wait_recv()
            forward(j, 4, (rows_of(1 - x, z, 1), other), bit_z)
            forward(j, 6, (rows_of(1 - x, z), other), 0)
            started[j, 2].wait_recv()
            forward(j, 3, (rows_of(x, 1 - z, 0), other), bit_x)
            forward(j, 7, (rows_of(x, 1 - z), other), 0)

        def stage_three(j):
            for kind, lower in ((3, 0), (4, 1)):
                started[j, kind].wait_recv()
                forward(j, kind + 5, (rows_of(1 - x, 1 - z, lower), other), 0)

        def stage_four(j):
            for kind in range(5, 10):
                started[j, kind].wait_recv()

        def project(j, where, bias):
            value = matmul(x_ref[...], full_refs[j][:, where])
            if bias is not None:
                value = value + bias[...].astype(F32).reshape(1, half)
            (q_ref, k_ref, v_ref)[j][:, where] = value.astype(BF16)

        for j in range(3):
            full_refs[j][:, own] = own_refs[j][...]
        project(0, own, qb_ref)
        project(1, own, None)
        project(2, own, vb_ref)

        def attend(pair):
            attend_pair(q_ref, k_ref, v_ref, ctx_ref, lse_ref, pair, length)

        stage_one(0)
        attend(head * pairs)
        stage_one(1)
        stage_two(0)
        attend(head * pairs + 1)
        stage_one(2)
        stage_two(1)
        stage_three(0)
        attend(head * pairs + 2)
        stage_two(2)
        stage_three(1)
        stage_three(2)
        for copy in bias_copies:
            copy.wait_recv()
        stage_four(0)
        project(0, other, qb_got)
        stage_four(1)
        project(1, other, None)
        stage_four(2)
        project(2, other, vb_got)

        outs = []
        for n, (source, target) in enumerate((
            (q_ref, q_out), (k_ref, k_out), (v_ref, v_out), (fq_ref, fq_out), (fk_ref, fk_out), (fv_ref, fv_out))):
            copy = pltpu.make_async_copy(source, target, out_sem.at[n])
            copy.start()
            outs.append(copy)

        def late(n, carry):
            attend((1 - head) * pairs + n)
            return carry

        lax.fori_loop(0, pairs, late, 0)
        for copy in outs:
            copy.wait()
        for copy in started.values():
            copy.wait_send()
        for copy in bias_copies:
            copy.wait_send()

    anywhere = pl.BlockSpec(memory_space=pl.ANY)
    vmem = pl.BlockSpec(memory_space=pltpu.VMEM)
    act = jax.ShapeDtypeStruct((rows, width), BF16)
    full = jax.ShapeDtypeStruct((depth, width), BF16)
    return pl.pallas_call(
        kernel,
        out_shape=[act] * 4 + [jax.ShapeDtypeStruct((2 * pairs, 2, rows), F32)] + [full] * 3,
        in_specs=[pl.BlockSpec(memory_space=pltpu.SMEM)] + [vmem] * 6,
        out_specs=[anywhere] * 3 + [vmem] * 2 + [anywhere] * 3,
        scratch_shapes=[pltpu.VMEM((rows, width), BF16)] * 3 + [pltpu.VMEM((depth, width), BF16)] * 3
        + [pltpu.VMEM((half,), BF16)] * 2 + [pltpu.SemaphoreType.DMA((3, kinds))] * 2
        + [pltpu.SemaphoreType.DMA((2,))] * 2 + [pltpu.SemaphoreType.DMA((6,))],
        compiler_params=pltpu.CompilerParams(collective_id=0, has_side_effects=True, vmem_limit_bytes=VMEM_LIMIT),
        name="attention_forward",
    )(lengths, inputs, *weights, *biases)


def gelu_parts(v):
    x = jnp.abs(v) * 0.7071067811865476
    t = 1.0 / (1.0 + 0.3275911 * x)
    bell = jnp.exp(-0.5 * (v * v))
    tail = 0.5 * bell * t * (
        0.254829592 + t * (-0.284496736 + t * (1.421413741 + t * (-1.453152027 + t * 1.061405429))))
    phi = jnp.where(v >= 0, 1.0 - tail, tail)
    return v * phi, phi + v * bell * 0.3989422804014327


ROW_BLOCK = 64


def over_rows(rows, step, carry):
    def one(n, kept):
        return step(pl.ds(pl.multiple_of(n * ROW_BLOCK, ROW_BLOCK), ROW_BLOCK), kept)

    return lax.fori_loop(0, rows // ROW_BLOCK, one, carry)


OUT_BIAS, FIRST_GAIN, FIRST_SHIFT, DOWN_BIAS, SECOND_GAIN, SECOND_SHIFT, POOL_BIAS, CLASS_BIAS, UP_BIAS = range(9)
LOSS = 12
CLASS_ROWS = (6, 7, 13)


def orders(bits):
    head = bits - 1
    rest = list(range(2, head))
    both = [[0, 1, head] + rest, [0, head, 1] + rest]
    return [both + [[0] + rest[:1] + pair + rest[1:]] for pair in ([1, head], [head, 1])]


def rest_of_layer(context, inputs, class_turned, out_weight, vectors, log_totals, cotangent, up_weight, down_weight,
                  pool_weight, queries, keys, values, full, lengths, labels, bits):
    rows, width = inputs.shape
    hidden = up_weight.shape[1]
    half = width // 2
    times = hidden // width
    devices = 1 << bits
    block = 2 * width // devices
    classes = class_turned.shape[0]
    per_width = width // 128
    fact_rows = -(-2 * per_width // 16) * 16
    small_half = 8
    late_lanes = width // 3
    plans = orders(bits)
    parts = len(plans[0])
    lanes_part = half // parts
    count = 2 * times + 4
    out_at, query_at = 2 * times, 2 * times + 1
    stages = bits
    head = bits - 1
    small_order = [1, head] + list(range(2, head)) + [0]
    pairs = width // 128
    dp_dims = (2,) * (bits - 1)

    def kernel(lengths_ref, labels_ref, ctx_ref, x_ref, cls_in, ow_ref, v0, v1, v2, v3, v4, v5, v6, v7, v8, lse_ref,
               cot_hbm, up_hbm, down_hbm, pool_hbm, q_hbm, k_hbm, v_hbm, wq_hbm, wk_hbm, wv_hbm,
               states_out, grad_out, logit_ref, sums_ref, small_out, late_out, factor_out, held, *rest):
        got = rest[:stages]
        (gb_ref, up_w, down_w, pool_w, low_ref, n1, r1, n2, r2, hid_even, hid_odd, slope_even, slope_odd, acc, whole, frow, vec_ref, cls_ref, small_ref,
         small_buf, small_got, late_buf, late_got, load_sem, late_sem, send, recv, side_send, side_recv, whole_sem) = rest[stages:]
        place = Place(bits)
        loads = []
        for i, (source, target) in enumerate(
            ((up_hbm, up_w), (down_hbm, down_w), (pool_hbm, pool_w), (cot_hbm, gb_ref))):
            load = pltpu.make_async_copy(source, target, load_sem.at[i])
            load.start()
            loads.append(load)
        place.greet(range(bits))
        length = lengths_ref[place.head]
        slot = sum(place.mine[bit] * (1 << k) for k, bit in enumerate(small_order))
        hids, slopes = (hid_even, hid_odd), (slope_even, slope_odd)

        def index(i, done, fixed):
            out = [i]
            for bit in reversed(range(bits)):
                out.append(fixed[bit] if bit in fixed else place.mine[bit] if bit in done else slice(None))
            return tuple(out)

        def part_copy(i, s):
            plan = plans[i // parts % 2][i % parts]
            bit = plan[s]
            return pltpu.make_async_remote_copy(
                src_ref=held.at[index(i, plan[:s], {bit: 1 - place.mine[bit]})], dst_ref=got[s].at[i],
                send_sem=send.at[i, s], recv_sem=recv.at[i, s], device_id=place.partner(bit), device_id_type=MESH)

        def add_part(i, s):
            part_copy(i, s).wait_recv()
            where = index(i, plans[i // parts % 2][i % parts][: s + 1], {})
            if s == stages - 1:
                sums_ref[i] = held[where].astype(F32) + got[s][i].astype(F32)
            else:
                held[where] = held[where] + got[s][i]

        def take(name):
            for code in SCHEDULE[name]:
                if code >= 2000:
                    side_advance(code // 1000 - 2, code % 10)
                    continue
                i, s = code // 100 * parts + code // 10 % 10, code % 10
                if s > 0:
                    add_part(i, s - 1)
                if s < stages:
                    part_copy(i, s).start()

        def take_after(step, prefix, steps):
            for n in steps:
                if not SCHEDULE[prefix + str(n)]:
                    continue

                @pl.when(step == n)
                def _():
                    take(prefix + str(n))

        def put(i, wide, lead):
            for h in range(2):
                for m in range(parts):
                    at = h * half + m * lanes_part
                    held[(i * parts + m, h) + lead] = wide[..., at : at + lanes_part]

        def side_copy(kind, s):
            bit = small_order[s % stages]
            if kind == 0:
                start = (slot // (1 << s)) * (1 << s)
                source = target = factor_out.at[pl.ds(start, 1 << s)]
            elif kind == 2:
                source, target = late_buf.at[s], late_got.at[s]
            else:
                bit = small_order[(s - 1) % stages]
                if s == 0:
                    source, target = small_ref.at[rows_of_core(1 - place.mine[0])], small_got.at[0]
                elif s == stages:
                    source = target = small_out.at[rows_of_core(place.mine[0])]
                else:
                    source, target = small_buf.at[s], small_got.at[s]
            return pltpu.make_async_remote_copy(
                src_ref=source, dst_ref=target, send_sem=side_send.at[kind, s], recv_sem=side_recv.at[kind, s],
                device_id=place.partner(bit), device_id_type=MESH)

        def rows_of_core(core):
            return pl.ds(pl.multiple_of(core * small_half, small_half), small_half)

        def side_advance(kind, s):
            last = stages + (kind == 1)
            if s > 0:
                side_copy(kind, s - 1).wait_recv()
            if kind == 1 and 0 < s < last:
                mine = rows_of_core(place.mine[0])
                total = (small_ref[mine, :] if s == 1 else small_buf[s - 1]) + small_got[s - 1]
                if s < stages:
                    small_buf[s] = total
                else:
                    small_out[mine, :] = total
            if kind == 2 and s > 0:
                total = late_buf[s - 1] + late_got[s - 1]
                if s < stages:
                    late_buf[s] = total
                else:
                    late_out[...] = total
            if s < last:
                side_copy(kind, s).start()

        for i, ref in enumerate((v0, v1, v2, v3, v4, v5, v6)):
            vec_ref[i : i + 1, :] = ref[...].astype(F32).reshape(1, width)
        vec_ref[CLASS_BIAS : CLASS_BIAS + 1, 0:classes] = v7[...].astype(F32).reshape(1, classes)
        wide_bias = v8[...].astype(F32).reshape(1, hidden)
        for t in range(times):
            vec_ref[UP_BIAS + t : UP_BIAS + t + 1, :] = wide_bias[:, t * width : (t + 1) * width]
        cls_ref[...] = jnp.zeros_like(cls_ref)
        cls_ref[0:classes, :] = cls_in[...]

        def vec(i):
            return vec_ref[i : i + 1, :]

        acc[...] = matmul(ctx_ref[...], ow_ref[...])

        def norm_one(at, carry):
            value = x_ref[at, :].astype(F32) + (acc[at, :] + vec(OUT_BIAS))
            center = value - jnp.mean(value, -1, keepdims=True)
            scale = lax.rsqrt(jnp.mean(center * center, -1, keepdims=True) + EPSILON)
            normal = center * scale
            n1[at, :] = normal
            r1[at, :] = scale
            low_ref[at, :] = (normal * vec(FIRST_GAIN) + vec(FIRST_SHIFT)).astype(BF16)
            acc[at, :] = jnp.zeros_like(normal)
            return carry

        over_rows(rows, norm_one, 0)
        loads[0].wait()
        loads[1].wait()

        def at_chunk(c):
            return pl.ds(pl.multiple_of(c * width, width), width)

        def pre_of(c, parity):
            slopes[parity][:, at_chunk(c // 2)] = matmul(low_ref[...], up_w[:, at_chunk(c)]) + vec_ref[pl.ds(UP_BIAS + c, 1), :]

        def activate(c, parity):
            at = at_chunk(c // 2)
            act, deriv = gelu_parts(slopes[parity][:, at])
            hids[parity][:, at] = act.astype(BF16)
            slopes[parity][:, at] = deriv

        def add_branch(c, parity):
            acc[...] += matmul(hids[parity][:, at_chunk(c // 2)], down_w[at_chunk(c), :])

        pre_of(0, 0)
        pre_of(1, 1)
        activate(0, 0)

        def forward(n, carry):
            c = 2 * n
            pre_of(c + 2, 0)
            activate(c + 1, 1)
            add_branch(c, 0)
            pre_of(c + 3, 1)
            activate(c + 2, 0)
            add_branch(c + 1, 1)
            return carry

        lax.fori_loop(0, times // 2 - 1, forward, 0)
        activate(times - 1, 1)
        add_branch(times - 2, 0)
        add_branch(times - 1, 1)

        def norm_two(at, carry):
            first = n1[at, :] * vec(FIRST_GAIN) + vec(FIRST_SHIFT)
            value = first + (acc[at, :] + vec(DOWN_BIAS))
            center = value - jnp.mean(value, -1, keepdims=True)
            scale = lax.rsqrt(jnp.mean(center * center, -1, keepdims=True) + EPSILON)
            normal = center * scale
            n2[at, :] = normal
            r2[at, :] = scale
            whole[at, :] = (normal * vec(SECOND_GAIN) + vec(SECOND_SHIFT)).astype(BF16)
            return carry

        over_rows(rows, norm_two, 0)
        states_copy = pltpu.make_async_copy(whole, states_out, whole_sem.at[0])
        states_copy.start()

        loads[2].wait()
        loads[3].wait()
        lead = whole[0:16, :]
        pooled = jnp.tanh(matmul(lead, pool_w[...]) + vec(POOL_BIAS))
        pooled_low = pooled.astype(BF16)
        logits = nt(pooled_low, cls_ref[...]) + vec_ref[CLASS_BIAS : CLASS_BIAS + 1, 0:128]
        lanes = lane_iota(logits.shape)
        logits = jnp.where(lanes < classes, logits, NEGATIVE)
        top = jnp.max(logits, -1, keepdims=True)
        norm = top + jnp.log(jnp.sum(jnp.exp(logits - top), -1, keepdims=True))
        target = jnp.where(lanes == labels_ref[0], 1.0, 0.0)
        loss = (norm - jnp.sum(jnp.where(lanes < classes, target * logits, 0.0), -1, keepdims=True)) / devices
        grad_logits = (jnp.where(lanes < classes, jnp.exp(logits - norm) - target, 0.0) / devices).astype(BF16)
        grad_pooled = (matmul(grad_logits, cls_ref[...]) * (1.0 - pooled * pooled)).astype(BF16)
        grad_lead = nt(grad_pooled, pool_w[...])
        logit_ref[...] = logits[0:1, 0:classes]
        frow[...] = jnp.zeros_like(frow)
        for k, value in enumerate((lead, grad_pooled)):
            wide = value.astype(F32)
            for j in range(per_width):
                frow[k * per_width + j : k * per_width + j + 1, :] = wide[0:1, j * 128 : (j + 1) * 128]
        small_ref[...] = jnp.zeros(small_ref.shape, F32)
        logit_row = grad_logits.astype(F32)[0:1, :]
        pooled_row = pooled_low.astype(F32)[0:1, :]
        for k in range(classes):
            small_ref[CLASS_ROWS[k] : CLASS_ROWS[k] + 1, :] = logit_row[:, k : k + 1] * pooled_row
        factor_out[slot] = frow[...].astype(BF16)
        take("R")

        def back_two(at, sums):
            gain_sum, shift_sum, bias_sum = sums
            row = at.start + lax.broadcasted_iota(jnp.int32, (ROW_BLOCK, width), 0)
            grad = gb_ref[at, :].astype(F32) + jnp.where(row == 0, grad_lead[0:1, :], 0.0)
            normal = n2[at, :]
            e = grad * vec(SECOND_GAIN)
            value = (e - jnp.mean(e, -1, keepdims=True) - normal * jnp.mean(e * normal, -1, keepdims=True)) * r2[at, :]
            rounded = value.astype(BF16)
            acc[at, :] = value
            gb_ref[at, :] = rounded
            return (gain_sum + jnp.sum(grad * normal, 0, keepdims=True), shift_sum + jnp.sum(grad, 0, keepdims=True),
                    bias_sum + jnp.sum(rounded.astype(F32), 0, keepdims=True))

        zero = jnp.zeros((1, width), F32)
        gain_sum, shift_sum, bias_sum = over_rows(rows, back_two, (zero, zero, zero))
        small_ref[SECOND_GAIN : SECOND_GAIN + 1, :] = gain_sum
        small_ref[SECOND_SHIFT : SECOND_SHIFT + 1, :] = shift_sum
        small_ref[DOWN_BIAS : DOWN_BIAS + 1, :] = bias_sum
        small_ref[LOSS : LOSS + 1, 0:128] = jnp.broadcast_to(loss[0:1, 0:1], (1, 128))
        small_ref[LOSS : LOSS + 1, 128:256] = logit_row

        take("B")

        def down_grads(n, carry):
            for parity in range(2):
                c = 2 * n + parity
                wide = tn(hids[parity][:, at_chunk(n)], gb_ref[...]).astype(BF16).reshape(2, 2, times, block, width)
                for t in range(times):
                    put(t, wide[:, :, t], (lax.rem(c // 2, 2), lax.rem(c, 2)))
                take_after(c, "D", range(parity, times, 2))
            return carry

        lax.fori_loop(0, times // 2, down_grads, 0)

        for parity in range(2):

            def up_grads(h, carry):
                c = 2 * h + parity
                step = 4 * parity + 2 * h
                grad = (nt(gb_ref[...], down_w[at_chunk(c), :]) * slopes[parity][:, at_chunk(h)]).astype(BF16)
                small_ref[pl.ds(UP_BIAS + c, 1), :] = jnp.sum(grad.astype(F32), 0, keepdims=True)
                wide = tn(low_ref[...], grad).astype(BF16)
                for t in range(2):
                    for m in range(parts):
                        at = t * half + m * lanes_part
                        held[(times + 2 * parity + t) * parts + m, h] = wide[:, at : at + lanes_part].reshape(
                            dp_dims + (block, lanes_part))
                take_after(step, "U", range(4 * parity, 4 * parity + 4, 2))
                acc[...] += nt(grad, up_w[:, at_chunk(c)])
                take_after(step + 1, "U", range(4 * parity + 1, 4 * parity + 4, 2))
                return carry

            lax.fori_loop(0, 2, up_grads, 0)

        late = []
        for i, (source, target) in enumerate((
            (q_hbm, down_w.at[0:rows, :]), (k_hbm, down_w.at[rows : 2 * rows, :]),
            (v_hbm, down_w.at[2 * rows : 3 * rows, :]), (wq_hbm, up_w.at[:, 0:width]),
            (wk_hbm, up_w.at[:, width : 2 * width]), (wv_hbm, up_w.at[:, 2 * width : 3 * width]),
        )):
            load = pltpu.make_async_copy(source, target, late_sem.at[i])
            load.start()
            late.append(load)

        def back_one(at, sums):
            gain_sum, shift_sum, bias_sum = sums
            grad = acc[at, :]
            normal = n1[at, :]
            e = grad * vec(FIRST_GAIN)
            value = (e - jnp.mean(e, -1, keepdims=True) - normal * jnp.mean(e * normal, -1, keepdims=True)) * r1[at, :]
            rounded = value.astype(BF16)
            acc[at, :] = value
            low_ref[at, :] = rounded
            return (gain_sum + jnp.sum(grad * normal, 0, keepdims=True), shift_sum + jnp.sum(grad, 0, keepdims=True),
                    bias_sum + jnp.sum(rounded.astype(F32), 0, keepdims=True))

        gain_sum, shift_sum, bias_sum = over_rows(rows, back_one, (zero, zero, zero))
        small_ref[FIRST_GAIN : FIRST_GAIN + 1, :] = gain_sum
        small_ref[FIRST_SHIFT : FIRST_SHIFT + 1, :] = shift_sum
        small_ref[OUT_BIAS : OUT_BIAS + 1, :] = bias_sum
        take("L0")
        put(out_at, tn(ctx_ref[...], low_ref[...]).astype(BF16).reshape(dp_dims + (block, width)), ())
        take("L1")
        hids[1][:, width : 2 * width] = nt(low_ref[...], ow_ref[...]).astype(BF16)
        take("L2")

        lanes_row = lax.broadcasted_iota(jnp.int32, (128, rows), 0)
        pair_lanes = lane_iota((rows, 128))
        for load in late:
            load.wait()

        def attend(pair, carry):
            def at(n):
                return pl.ds(pl.multiple_of(n % 2 * width + pair * 128, 128), 128)

            q2 = down_w[0:rows, at(0)]
            k2 = down_w[rows : 2 * rows, at(0)]
            v2 = down_w[2 * rows : 3 * rows, at(0)]
            g2 = hids[1][:, at(3)]
            k2t = k2.T
            heads_of = []
            for parity in range(2):
                qa, ka = pair_operands(q2, k2, length, parity)
                mine = (pair_lanes < HEAD_DIM) if parity == 0 else (pair_lanes >= HEAD_DIM)
                va = jnp.where(mine, v2.astype(F32), 0.0).astype(BF16)
                probs = jnp.exp(nt(ka, qa) - lse_ref[pair, parity : parity + 1, :])
                grad_v = matmul(probs.astype(BF16), g2)
                grad_probs = nt(va, g2)
                inner = jnp.sum(probs * grad_probs, 0, keepdims=True)
                grad_scores = (probs * (grad_probs - inner)).astype(BF16)
                heads_of.append((grad_v, matmul(grad_scores, qa), matmul(k2t, grad_scores)))
                take_after(2 * pair + parity, "P", range(parity, 2 * pairs, 2))
            first = pair_lanes < HEAD_DIM
            turned = jnp.where(lanes_row < HEAD_DIM, heads_of[0][2], heads_of[1][2]) * HEAD_DIM ** -0.5
            hids[0][:, at(0)] = turned.T.astype(BF16)
            hids[0][:, at(1)] = jnp.where(first, heads_of[0][1], heads_of[1][1]).astype(BF16)
            hids[1][:, at(2)] = jnp.where(first, heads_of[0][0], heads_of[1][0]).astype(BF16)
            return carry

        lax.fori_loop(0, pairs, attend, 0)

        def grads_of(n):
            return hids[n // 2][:, n % 2 * width : (n % 2 + 1) * width]

        late_buf[0] = jnp.zeros(late_buf.shape[1:], F32)
        for n in range(2):
            total = jnp.sum(grads_of(2 * n).astype(F32), 0, keepdims=True)
            for t in range(3):
                late_buf[0, 3 * n + t : 3 * n + t + 1, :] = total[:, t * late_lanes : (t + 1) * late_lanes]
        take("Q")
        for n in range(3):
            put(query_at + n, tn(x_ref[...], grads_of(n)).astype(BF16).reshape(dp_dims + (block, width)), ())
            take("W" + str(n))
        states_copy.wait()
        for n in range(3):
            acc[...] += nt(grads_of(n), up_w[:, n * width : (n + 1) * width])
            take("I" + str(n))
        whole[...] = acc[...].astype(BF16)
        grad_copy = pltpu.make_async_copy(whole, grad_out, whole_sem.at[1])
        grad_copy.start()
        for n in range(4):
            take("T" + str(n))
        grad_copy.wait()
        for i in range(count * parts):
            for s in range(stages):
                part_copy(i, s).wait_send()
        for s in range(stages):
            for kind in range(3):
                side_copy(kind, s).wait_send()
        side_copy(1, stages).wait_send()

    vmem = pl.BlockSpec(memory_space=pltpu.VMEM)
    anywhere = pl.BlockSpec(memory_space=pl.ANY)
    smem = pl.BlockSpec(memory_space=pltpu.SMEM)
    act = jax.ShapeDtypeStruct((rows, width), BF16)
    return pl.pallas_call(
        kernel,
        out_shape=[
            act, act, jax.ShapeDtypeStruct((1, classes), F32), jax.ShapeDtypeStruct((count * parts, block, lanes_part), F32),
            jax.ShapeDtypeStruct((16, width), F32), jax.ShapeDtypeStruct((8, late_lanes), F32),
            jax.ShapeDtypeStruct((devices, fact_rows, 128), BF16),
        ],
        in_specs=[smem] * 2 + [vmem] * 14 + [anywhere] * 10,
        out_specs=[anywhere] * 2 + [vmem] * 5,
        scratch_shapes=[pltpu.VMEM((count * parts, 2) + dp_dims + (block, lanes_part), BF16)]
        + [pltpu.VMEM((count * parts,) + (2,) * (stages - 1 - s) + (block, lanes_part), BF16) for s in range(stages)]
        + [
            pltpu.VMEM((rows, width), BF16),
            pltpu.VMEM((width, hidden), BF16),
            pltpu.VMEM((hidden, width), BF16),
            pltpu.VMEM((width, width), BF16),
            pltpu.VMEM((rows, width), BF16),
            pltpu.VMEM((rows, width), F32),
            pltpu.VMEM((rows, 1), F32),
            pltpu.VMEM((rows, width), F32),
            pltpu.VMEM((rows, 1), F32),
            pltpu.VMEM((rows, hidden // 2), BF16),
            pltpu.VMEM((rows, hidden // 2), BF16),
            pltpu.VMEM((rows, hidden // 2), F32),
            pltpu.VMEM((rows, hidden // 2), F32),
            pltpu.VMEM((rows, width), F32),
            pltpu.VMEM((rows, width), BF16),
            pltpu.VMEM((fact_rows, 128), F32),
            pltpu.VMEM((16, width), F32),
            pltpu.VMEM((128, width), BF16),
            pltpu.VMEM((16, width), F32),
            pltpu.VMEM((stages, small_half, width), F32),
            pltpu.VMEM((stages, small_half, width), F32),
            pltpu.VMEM((stages, 8, late_lanes), F32),
            pltpu.VMEM((stages, 8, late_lanes), F32),
            pltpu.SemaphoreType.DMA((4,)),
            pltpu.SemaphoreType.DMA((6,)),
            pltpu.SemaphoreType.DMA((count * parts, stages)),
            pltpu.SemaphoreType.DMA((count * parts, stages)),
            pltpu.SemaphoreType.DMA((3, stages + 1)),
            pltpu.SemaphoreType.DMA((3, stages + 1)),
            pltpu.SemaphoreType.DMA((2,)),
        ],
        compiler_params=pltpu.CompilerParams(collective_id=1, has_side_effects=True, vmem_limit_bytes=VMEM_LIMIT),
        name="rest_of_layer",
    )(lengths, labels, context, inputs, class_turned, out_weight, *vectors, log_totals, cotangent, up_weight,
      down_weight, pool_weight, queries, keys, values, *full)


SCHEDULE = {
    "R": (),
    "B": (),
    "D0": (),
    "D1": (),
    "D2": (),
    "D3": (0, 10, 20, 100, 110,),
    "U0": (120, 200, 210, 220, 300,),
    "U1": (1, 11, 21, 310, 320,),
    "U2": (101, 111, 121, 400, 410, 420, 500, 510,),
    "U3": (201, 211, 221, 520,),
    "U4": (2, 12, 22, 311, 321,),
    "U5": (112, 421,),
    "U6": (102, 122, 212, 222, 521, 600, 610, 620, 700, 710,),
    "U7": (202, 301, 720,),
    "L0": (3, 23, 3000,),
    "L1": (13, 322, 312, 113, 800, 810, 820,),
    "L2": (411, 621,),
    "P0": (422, 123,),
    "P1": (103, 203, 223, 522, 401, 2000,),
    "P2": (4, 14, 24, 114, 213, 323, 302, 721, 501, 511,),
    "P3": (313, 3001,),
    "P4": (104, 124, 224, 423, 412, 204, 611, 821,),
    "P5": (5, 15, 214, 324, 303, 25, 523, 622, 2001,),
    "P6": (115, 402, 601,),
    "P7": (105, 125, 314, 424, 502, 512, 722, 225, 3002,),
    "P8": (205, 215, 325, 524, 304, 413, 822, 711,),
    "P9": (612, 701, 403, 623, 2002,),
    "P10": (315, 425, 503, 602,),
    "P11": (525, 414, 513, 305, 723, 801, 811, 3003,),
    "Q": (404, 4000,),
    "W0": (823, 900, 910, 920,),
    "W1": (504, 624, 613, 712, 1000, 1010, 1020, 2003,),
    "W2": (1100, 1110, 1120,),
    "I0": (415, 514, 603, 702, 724, 901, 3004,),
    "I1": (405, 911, 921, 812,),
    "I2": (505, 614, 824, 802, 1001, 625, 1021, 4001,),
    "T0": (1011, 1101, 1111, 1121, 604, 713, 703, 515, 725, 902, 912, 922, 615, 813, 825, 2004, 3005, 4002,),
    "T1": (605, 803, 1022, 1002, 1012, 1122, 1102, 714, 1112, 704, 913, 814, 903, 804, 1023, 4003, 3006,),
    "T2": (923, 715, 1013, 914, 705, 1003, 904, 815, 1113, 805, 1123, 924, 1014, 1103, 1004, 2005, 4004,),
    "T3": (915, 1024, 1114, 905, 1124, 925, 1104, 1015, 1005, 1025, 1115, 1125, 1105, 4005,),
}


def spread(states, input_grad, logits, sums, small, late, gathered, classes):
    width = small.shape[1]
    half = width // 2
    parts, block, lanes_part = sums.shape
    count = parts * lanes_part // half
    parts = parts // count
    devices = gathered.shape[0]
    times = (count - 4) // 2
    lanes = width // 128

    def kernel(states_ref, grad_ref, logits_ref, sums_ref, small_ref, late_ref, got_ref, states_out, grad_out, logits_out, up, down,
               out, query, key, value, pool, query_bias, value_bias, out_bias, first_gain, first_shift, up_bias,
               down_bias, second_gain, second_shift, pool_bias, class_weight, class_bias, loss, left, right, late_wide, sem):
        copies = [
            pltpu.make_async_copy(states_ref, states_out, sem.at[0]), pltpu.make_async_copy(grad_ref, grad_out, sem.at[1])]
        for copy in copies:
            copy.start()
        logits_out[...] = logits_ref[...]
        dp, head = lax.axis_index("dp"), lax.axis_index("head")
        for m in range(parts):
            at = slice(m * lanes_part, (m + 1) * lanes_part)
            for t in range(times):
                down[t * block : (t + 1) * block, at] = sums_ref[t * parts + m]
                up[:, t * half + m * lanes_part : t * half + (m + 1) * lanes_part] = sums_ref[(times + t) * parts + m]
            for k, ref in enumerate((out, query, key, value)):
                ref[:, at] = sums_ref[(2 * times + k) * parts + m]
        got = got_ref[...].astype(F32)

        def wide(k):
            return jnp.concatenate([got[:, k * lanes + j, :] for j in range(lanes)], 1)

        lead, grad_pooled = wide(0), wide(1)
        left[...] = lead.T
        right[...] = grad_pooled
        at = pl.ds(pl.multiple_of(head * half, half), half)
        pool[...] = matmul(
            left[pl.ds(pl.multiple_of(dp * block, 8), block), :].astype(BF16), right[:, at].astype(BF16))
        pool_bias[...] = jnp.sum(grad_pooled, 0)
        for k in range(classes):
            class_weight[k : k + 1, :] = small_ref[CLASS_ROWS[k] : CLASS_ROWS[k] + 1, :]
        class_bias[...] = small_ref[LOSS : LOSS + 1, 128 : 128 + classes].reshape(classes)
        for n in range(2):
            late_wide[n : n + 1, :] = jnp.concatenate([late_ref[3 * n + t : 3 * n + t + 1, :] for t in range(3)], 1)
        query_bias[...] = late_wide[0:1, at].reshape(half)
        value_bias[...] = late_wide[1:2, at].reshape(half)
        for ref, row in ((out_bias, OUT_BIAS), (first_gain, FIRST_GAIN), (first_shift, FIRST_SHIFT),
                         (down_bias, DOWN_BIAS), (second_gain, SECOND_GAIN), (second_shift, SECOND_SHIFT)):
            ref[...] = small_ref[row, :]
        up_bias[...] = jnp.concatenate(
            [small_ref[UP_BIAS + t : UP_BIAS + t + 1, :] for t in range(times)], 1).reshape(times * width)
        loss[()] = small_ref[LOSS, 0]
        for copy in copies:
            copy.wait()

    def f32(*shape):
        return jax.ShapeDtypeStruct(shape, F32)

    square = f32(block, half)
    row = f32(width)
    act = jax.ShapeDtypeStruct(states.shape, BF16)
    vmem = pl.BlockSpec(memory_space=pltpu.VMEM)
    anywhere = pl.BlockSpec(memory_space=pl.ANY)
    return pl.pallas_call(
        kernel,
        out_shape=[
            act, act, f32(1, classes), f32(block, times * half), f32(times * block, half), square, square, square, square,
            square, f32(half), f32(half), row, row, row, f32(times * width), row, row, row, row, f32(classes, width),
            f32(classes), f32(),
        ],
        in_specs=[vmem] * 7,
        out_specs=[anywhere] * 2 + [vmem] * 20 + [pl.BlockSpec(memory_space=pltpu.SMEM)],
        scratch_shapes=[
            pltpu.VMEM((width, devices), F32), pltpu.VMEM((devices, width), F32),
            pltpu.VMEM((8, width), F32), pltpu.SemaphoreType.DMA((2,))],
        compiler_params=pltpu.CompilerParams(vmem_limit_bytes=VMEM_LIMIT),
        name="spread",
    )(states, input_grad, logits, sums, small, late, gathered)


def plain_body(
    inputs, lengths, labels, state_cotangent, query_weight, query_bias, key_weight, value_weight, value_bias,
    out_weight, out_bias, first_gain, first_shift, up_weight, up_bias, down_weight, down_bias, second_gain,
    second_shift, pool_weight, pool_bias, class_weight, class_bias,
):
    scale = HEAD_DIM ** (-0.5)
    dp_size, head_size = lax.axis_size("dp"), lax.axis_size("head")
    dp_at, head_at = lax.axis_index("dp"), lax.axis_index("head")
    devices = dp_size * head_size
    width = inputs.shape[1]
    block_columns = width // head_size
    row_seqs = labels.shape[0]
    assert row_seqs == 1 and inputs.shape[0] == SEQ_LEN
    length = lax.dynamic_index_in_dim(lengths, head_at, keepdims=False)

    weights = [query_weight, key_weight, value_weight]
    full = [lax.all_gather(w, "head", axis=1, tiled=True) for w in weights]
    biases = lax.all_gather(jnp.stack([query_bias, value_bias]), "head", axis=1, tiled=True)
    query_bias, value_bias = biases[0], biases[1]
    wq, wk, wv = full
    head_count = width // HEAD_DIM

    def heads(matrix):
        return matrix.reshape(SEQ_LEN, head_count, HEAD_DIM)

    queries = (matmul(inputs, wq) + query_bias).astype(BF16)
    keys_low = matmul(inputs, wk).astype(BF16)
    values_low = (matmul(inputs, wv) + value_bias).astype(BF16)
    visible = lax.broadcasted_iota(jnp.int32, (1, 1, SEQ_LEN), 2) < length

    def scores_of():
        raw = jnp.einsum("qhd,khd->hqk", heads(queries), heads(keys_low), preferred_element_type=F32) * scale
        return jnp.where(visible, raw, NEGATIVE)

    scores = scores_of()
    peak = jnp.max(scores, -1, keepdims=True)
    raised = jnp.exp(scores - peak)
    denominator = jnp.sum(raised, -1, keepdims=True)
    probs = raised / denominator
    log_total = peak + jnp.log(denominator)
    context = jnp.einsum("hqk,khd->qhd", probs.astype(BF16), heads(values_low), preferred_element_type=F32)
    context_rows = context.astype(BF16).reshape(SEQ_LEN, width)
    attended = matmul(context_rows, out_weight) + out_bias
    first_out, first_back = jax.vjp(
        normalize, inputs.astype(F32) + attended, first_gain.astype(F32), first_shift.astype(F32))
    first_low = first_out.astype(BF16)
    hidden_pre = matmul(first_low, up_weight) + up_bias
    hidden_act, gelu_back = jax.vjp(partial(jax.nn.gelu, approximate=False), hidden_pre)
    hidden_low = hidden_act.astype(BF16)
    branch = matmul(hidden_low, down_weight) + down_bias
    normed, second_back = jax.vjp(normalize, first_out + branch, second_gain.astype(F32), second_shift.astype(F32))
    leading_low = normed.reshape(row_seqs, SEQ_LEN, -1)[:, 0].astype(BF16)
    pooled = jnp.tanh(matmul(leading_low, pool_weight) + pool_bias)
    pooled_low = pooled.astype(BF16)
    logits = matmul(pooled_low, class_weight) + class_bias
    classes = lax.broadcasted_iota(jnp.int32, logits.shape, 1)
    target = (classes == labels[:, None]).astype(F32)
    log_norm = jax.nn.logsumexp(logits, axis=-1)
    loss_part = jnp.sum(log_norm - jnp.sum(target * logits, -1)) / devices
    grad_logits = ((jnp.exp(logits - log_norm[:, None]) - target) / devices).astype(BF16)
    grad_class_weight = matmul(pooled_low.T, grad_logits)
    grad_class_bias = column_sums(grad_logits)
    grad_pooled = (matmul(grad_logits, class_weight.T) * (1.0 - pooled * pooled)).astype(BF16)
    grad_pool_bias = column_sums(grad_pooled)
    grad_leading = matmul(grad_pooled, pool_weight.T)
    grad_normed = state_cotangent.astype(F32).reshape(row_seqs, SEQ_LEN, -1)
    grad_normed = grad_normed.at[:, 0].add(grad_leading).reshape(normed.shape)
    grad_second, grad_second_gain, grad_second_shift = second_back(grad_normed)
    grad_branch = grad_second.astype(BF16)
    grad_down_weight = matmul(hidden_low.T, grad_branch)
    grad_down_bias = column_sums(grad_branch)
    grad_hidden = gelu_back(matmul(grad_branch, down_weight.T))[0].astype(BF16)
    grad_up_weight = matmul(first_low.T, grad_hidden)
    grad_up_bias = column_sums(grad_hidden)
    grad_first_out = grad_second + matmul(grad_hidden, up_weight.T)
    grad_first, grad_first_gain, grad_first_shift = first_back(grad_first_out)
    grad_attended = grad_first.astype(BF16)
    grad_out_weight = matmul(context_rows.T, grad_attended)
    grad_out_bias = column_sums(grad_attended)
    grad_context = heads(matmul(grad_attended, out_weight.T).astype(BF16))
    probs_again = jnp.exp(scores_of() - log_total)
    grad_values = jnp.einsum(
        "hqk,qhd->khd", probs_again.astype(BF16), grad_context, preferred_element_type=F32).astype(BF16)
    grad_probs = jnp.einsum("qhd,khd->hqk", grad_context, heads(values_low), preferred_element_type=F32)
    grad_scores = probs_again * (grad_probs - jnp.sum(probs_again * grad_probs, -1, keepdims=True))
    grad_scores = grad_scores.astype(BF16)
    grad_queries = (
        jnp.einsum("hqk,khd->qhd", grad_scores, heads(keys_low), preferred_element_type=F32) * scale).astype(BF16)
    grad_keys = (
        jnp.einsum("hqk,qhd->khd", grad_scores, heads(queries), preferred_element_type=F32) * scale).astype(BF16)
    grad_queries = grad_queries.reshape(SEQ_LEN, width)
    grad_keys = grad_keys.reshape(SEQ_LEN, width)
    grad_values = grad_values.reshape(SEQ_LEN, width)
    grad_query_weight = matmul(inputs.T, grad_queries)
    grad_key_weight = matmul(inputs.T, grad_keys)
    grad_value_weight = matmul(inputs.T, grad_values)
    input_grad = (
        grad_first + matmul(grad_queries, wq.T) + matmul(grad_keys, wk.T) + matmul(grad_values, wv.T)).astype(BF16)

    small_parts = (
        grad_out_bias, grad_first_gain, grad_first_shift, grad_up_bias, grad_down_bias, grad_second_gain,
        grad_second_shift, grad_pool_bias, column_sums(grad_queries), column_sums(grad_values),
        grad_class_weight.reshape(-1), grad_class_bias, loss_part.reshape(1),
    )
    grads = (grad_up_weight, grad_down_weight, grad_out_weight, grad_query_weight, grad_key_weight, grad_value_weight)
    grads = grads + (matmul(leading_low.T, grad_pooled),)

    def scatter(matrix):
        part = lax.psum_scatter(matrix, "dp", scatter_dimension=0, tiled=True)
        return lax.psum_scatter(part.astype(BF16), "head", scatter_dimension=1, tiled=True).astype(F32)

    up_total, down_total, out_total, query_total, key_total, value_total, pool_total = map(scatter, grads)
    totals = lax.psum(small_parts, ("dp", "head"))
    (
        out_bias_total, first_gain_total, first_shift_total, up_bias_total, down_bias_total, second_gain_total,
        second_shift_total, pool_bias_total, query_bias_total, value_bias_total, class_weight_total,
        class_bias_total, loss,
    ) = totals
    query_bias_total = lax.dynamic_slice_in_dim(query_bias_total, head_at * block_columns, block_columns)
    value_bias_total = lax.dynamic_slice_in_dim(value_bias_total, head_at * block_columns, block_columns)
    return (
        normed.astype(BF16), input_grad, logits, loss.reshape(()), query_total, query_bias_total, key_total,
        value_total, value_bias_total, out_total, out_bias_total, first_gain_total, first_shift_total, up_total,
        up_bias_total, down_total, down_bias_total, second_gain_total, second_shift_total, pool_total,
        pool_bias_total, class_weight_total.reshape(class_weight.shape), class_bias_total,
    )


def body(*args):
    (
        inputs, lengths, labels, state_cotangent, query_weight, query_bias, key_weight, value_weight, value_bias,
        out_weight, out_bias, first_gain, first_shift, up_weight, up_bias, down_weight, down_bias, second_gain,
        second_shift, pool_weight, pool_bias, class_weight, class_bias,
    ) = args
    dp_size, head_size = lax.axis_size("dp"), lax.axis_size("head")
    devices = dp_size * head_size
    bits = devices.bit_length() - 1
    rows, width = inputs.shape
    hidden = up_weight.shape[1]
    classes = class_weight.shape[1]
    direct = (
        (width // dp_size) % 16 == 0 and head_size == 2 and bits == 5 and hidden == 4 * width and rows == SEQ_LEN
        and labels.shape[0] == 1 and classes == len(CLASS_ROWS)
    )
    if not direct:
        return plain_body(*args)

    queries, keys, values, context, log_totals, *full = attention_forward(
        inputs, [query_weight, key_weight, value_weight], [query_bias, value_bias], lengths, bits)
    vectors = (out_bias, first_gain, first_shift, down_bias, second_gain, second_shift, pool_bias, class_bias, up_bias)
    states, input_grad, logits, sums, small, late, gathered = rest_of_layer(
        context, inputs, class_weight.T, out_weight, vectors, log_totals, state_cotangent, up_weight, down_weight,
        pool_weight, queries, keys, values, full, lengths, labels, bits)
    (
        states, input_grad, logits, up, down, out, query, key, value, pool, query_sum, value_sum, out_sum, first_gain_sum,
        first_shift_sum, up_sum, down_sum, second_gain_sum, second_shift_sum, pool_sum, class_sum, class_bias_sum, loss,
    ) = spread(states, input_grad, logits, sums, small, late, gathered, classes)
    return (
        states, input_grad, logits, loss, query, query_sum, key, value, value_sum, out, out_sum, first_gain_sum,
        first_shift_sum, up, up_sum, down, down_sum, second_gain_sum, second_shift_sum, pool, pool_sum, class_sum.T,
        class_bias_sum,
    )


def solution(mesh):
    rows, column, both = P(("dp", "head"), None), P(None, "head"), P("dp", "head")
    one, none = P("head"), P()
    return jax.shard_map(
        body,
        mesh=mesh,
        in_specs=(rows, P("dp"), P(("dp", "head")), rows, column, one, column, column, one) + (none,) * 14,
        out_specs=(
            rows, rows, rows, none, both, one, both, both, one, both, none, none, none, both, none, both, none,
            none, none, both, none, none, none,
        ),
        check_vma=False,
    )
```

```python
from functools import partial

import jax
import jax.numpy as jnp
from jax import lax
from jax.experimental import pallas as pl
from jax.experimental.pallas import tpu as pltpu
from jax.sharding import PartitionSpec as P

HEAD_DIM = 64
SEQ_LEN = 512
NEGATIVE = -1e30
EPSILON = 1e-06
MESH = pl.DeviceIdType.MESH
F32 = jnp.float32
BF16 = jnp.bfloat16
VMEM_LIMIT = 67_000_000


def normalize(values, gain, shift):
    center = values - jnp.mean(values, -1, keepdims=True)
    spread = jnp.mean(center * center, -1, keepdims=True)
    return center * lax.rsqrt(spread + EPSILON) * gain + shift


def matmul(left, right):
    return jnp.dot(left, right, preferred_element_type=F32)


def column_sums(values):
    return jnp.sum(values.astype(F32), 0)


class Place:
    def __init__(self, bits):
        self.bits = bits
        self.dp = lax.axis_index("dp")
        self.head = lax.axis_index("head")
        self.mine = [lax.rem(self.dp // (1 << b), 2) for b in range(bits - 1)] + [self.head]

    def partner(self, bit):
        if bit == self.bits - 1:
            return (self.dp, 1 - self.head)
        return (self.dp + (1 - 2 * self.mine[bit]) * (1 << bit), self.head)

    def greet(self, bits):
        barrier = pltpu.get_barrier_semaphore()
        for bit in bits:
            pl.semaphore_signal(barrier, inc=1, device_id=self.partner(bit), device_id_type=MESH)
        pl.semaphore_wait(barrier, len(bits))


def shared_rows(bits):
    return 1, 2


def lane_iota(shape):
    return lax.broadcasted_iota(jnp.int32, shape, 1)


def first_lanes(shape):
    return lane_iota(shape) < HEAD_DIM


def pair_operands(q2, k2, length, parity):
    lanes = lane_iota(q2.shape)
    rows = lax.broadcasted_iota(jnp.int32, q2.shape, 0)
    mine = (lanes < HEAD_DIM) if parity == 0 else (lanes >= HEAD_DIM)
    spare = lanes == (HEAD_DIM if parity == 0 else 0)
    hidden = jnp.where(rows < length, 0.0, NEGATIVE)
    qa = jnp.where(mine, q2.astype(F32) * HEAD_DIM ** -0.5, jnp.where(spare, 1.0, 0.0)).astype(BF16)
    ka = jnp.where(mine, k2.astype(F32), jnp.where(spare, hidden, 0.0)).astype(BF16)
    return qa, ka


def nt(left, right):
    return lax.dot_general(left, right, (((1,), (1,)), ((), ())), preferred_element_type=F32)


def tn(left, right):
    return lax.dot_general(left, right, (((0,), (0,)), ((), ())), preferred_element_type=F32)


def attend_pair(q_ref, k_ref, v_ref, ctx_ref, lse_ref, pair, length):
    at = pl.ds(pl.multiple_of(pair * 128, 128), 128)
    q2, k2, v2 = q_ref[:, at], k_ref[:, at], v_ref[:, at]
    v2t = v2.T
    rows = lax.broadcasted_iota(jnp.int32, (128, SEQ_LEN), 0)
    parts = []
    for parity in range(2):
        qa, ka = pair_operands(q2, k2, length, parity)
        scores = nt(ka, qa)
        peak = jnp.max(scores, 0, keepdims=True)
        raised = jnp.exp(scores - peak)
        total = jnp.sum(raised, 0, keepdims=True)
        probs = (raised * (1.0 / total)).astype(BF16)
        parts.append(matmul(v2t, probs))
        lse_ref[pair, parity : parity + 1, :] = peak + jnp.log(total)
    joined = jnp.where(rows < HEAD_DIM, parts[0], parts[1])
    ctx_ref[:, at] = joined.T.astype(BF16)


def attention_forward(inputs, weights, biases, lengths, bits):
    rows, width = inputs.shape
    depth, half = weights[0].shape
    part = depth // 8
    pairs = half // 128
    kinds = 10

    def kernel(lengths_ref, x_ref, wq_ref, wk_ref, wv_ref, qb_ref, vb_ref, q_out, k_out, v_out, ctx_ref, lse_ref,
               fq_out, fk_out, fv_out, q_ref, k_ref, v_ref, fq_ref, fk_ref, fv_ref, qb_got, vb_got, send, recv,
               bias_send, bias_recv, out_sem):
        place = Place(bits)
        head = place.head
        bit_x, bit_z = shared_rows(bits)
        place.greet([0, bit_x, bit_z, bits - 1])
        length = lengths_ref[head]
        own_refs, full_refs = (wq_ref, wk_ref, wv_ref), (fq_ref, fk_ref, fv_ref)
        own = pl.ds(pl.multiple_of(head * half, half), half)
        other = pl.ds(pl.multiple_of((1 - head) * half, half), half)
        core, x, z = place.mine[0], place.mine[bit_x], place.mine[bit_z]

        def rows_of(at_x, at_z, lower=None):
            start = core * (4 * part) + (at_z * 2 + at_x) * part
            if lower is None:
                return pl.ds(pl.multiple_of(start, part), part)
            return pl.ds(pl.multiple_of(start + lower * (part // 2), part // 2), part // 2)

        started = {}

        def start(j, kind, source, where, bit):
            copy = pltpu.make_async_remote_copy(
                src_ref=source, dst_ref=full_refs[j].at[where], send_sem=send.at[j, kind], recv_sem=recv.at[j, kind],
                device_id=place.partner(bit), device_id_type=MESH)
            copy.start()
            started[j, kind] = copy

        bias_copies = [
            pltpu.make_async_remote_copy(
                src_ref=source, dst_ref=target, send_sem=bias_send.at[n], recv_sem=bias_recv.at[n],
                device_id=place.partner(bits - 1), device_id_type=MESH)
            for n, (source, target) in enumerate(((qb_ref, qb_got), (vb_ref, vb_got)))
        ]
        for j in range(3):
            mine = rows_of(x, z)
            start(j, 0, own_refs[j].at[mine, :], (mine, own), bits - 1)
        far = rows_of(1 - x, 1 - z)
        start(2, 3, own_refs[2].at[far, :], (far, own), bits - 1)
        for copy in bias_copies:
            copy.start()

        def forward(j, kind, where, bit):
            start(j, kind, full_refs[j].at[where], where, bit)

        def stage_one(j):
            started[j, 0].wait_recv()
            where = (rows_of(x, z), other)
            forward(j, 1, where, bit_x)
            forward(j, 2, where, bit_z)
            forward(j, 5, where, 0)

        def stage_two(j):
            started[j, 1].wait_recv()
            if j < 2:
                forward(j, 4, (rows_of(1 - x, z, 1), other), bit_z)
            forward(j, 6, (rows_of(1 - x, z), other), 0)
            started[j, 2].wait_recv()
            if j < 2:
                forward(j, 3, (rows_of(x, 1 - z, 0), other), bit_x)
            forward(j, 7, (rows_of(x, 1 - z), other), 0)

        def stage_three(j):
            if j == 2:
                started[j, 3].wait_recv()
                forward(j, 8, (far, other), 0)
                return
            for kind, lower in ((3, 0), (4, 1)):
                started[j, kind].wait_recv()
                forward(j, kind + 5, (rows_of(1 - x, 1 - z, lower), other), 0)

        def stage_four(j):
            for kind in range(5, 10 if j < 2 else 9):
                started[j, kind].wait_recv()

        def project(j, where, bias):
            value = matmul(x_ref[...], full_refs[j][:, where])
            if bias is not None:
                value = value + bias[...].astype(F32).reshape(1, half)
            (q_ref, k_ref, v_ref)[j][:, where] = value.astype(BF16)

        for j in range(3):
            full_refs[j][:, own] = own_refs[j][...]
        project(0, own, qb_ref)
        project(1, own, None)
        project(2, own, vb_ref)

        def attend(pair):
            attend_pair(q_ref, k_ref, v_ref, ctx_ref, lse_ref, pair, length)

        stage_one(0)
        attend(head * pairs)
        stage_one(1)
        stage_two(0)
        attend(head * pairs + 1)
        stage_one(2)
        stage_two(1)
        stage_three(0)
        attend(head * pairs + 2)
        stage_two(2)
        stage_three(1)
        stage_three(2)
        for copy in bias_copies:
            copy.wait_recv()
        stage_four(0)
        project(0, other, qb_got)
        stage_four(1)
        project(1, other, None)
        stage_four(2)
        project(2, other, vb_got)

        outs = []
        for n, (source, target) in enumerate((
            (q_ref, q_out), (k_ref, k_out), (v_ref, v_out), (fq_ref, fq_out), (fk_ref, fk_out), (fv_ref, fv_out))):
            copy = pltpu.make_async_copy(source, target, out_sem.at[n])
            copy.start()
            outs.append(copy)

        def late(n, carry):
            attend((1 - head) * pairs + n)
            return carry

        lax.fori_loop(0, pairs, late, 0)
        for copy in outs:
            copy.wait()
        for copy in started.values():
            copy.wait_send()
        for copy in bias_copies:
            copy.wait_send()

    anywhere = pl.BlockSpec(memory_space=pl.ANY)
    vmem = pl.BlockSpec(memory_space=pltpu.VMEM)
    act = jax.ShapeDtypeStruct((rows, width), BF16)
    full = jax.ShapeDtypeStruct((depth, width), BF16)
    return pl.pallas_call(
        kernel,
        out_shape=[act] * 4 + [jax.ShapeDtypeStruct((2 * pairs, 2, rows), F32)] + [full] * 3,
        in_specs=[pl.BlockSpec(memory_space=pltpu.SMEM)] + [vmem] * 6,
        out_specs=[anywhere] * 3 + [vmem] * 2 + [anywhere] * 3,
        scratch_shapes=[pltpu.VMEM((rows, width), BF16)] * 3 + [pltpu.VMEM((depth, width), BF16)] * 3
        + [pltpu.VMEM((half,), BF16)] * 2 + [pltpu.SemaphoreType.DMA((3, kinds))] * 2
        + [pltpu.SemaphoreType.DMA((2,))] * 2 + [pltpu.SemaphoreType.DMA((6,))],
        compiler_params=pltpu.CompilerParams(collective_id=0, has_side_effects=True, vmem_limit_bytes=VMEM_LIMIT),
        name="attention_forward",
    )(lengths, inputs, *weights, *biases)


def gelu_parts(v):
    x = jnp.abs(v) * 0.7071067811865476
    t = 1.0 / (1.0 + 0.3275911 * x)
    bell = jnp.exp(-0.5 * (v * v))
    tail = 0.5 * bell * t * (
        0.254829592 + t * (-0.284496736 + t * (1.421413741 + t * (-1.453152027 + t * 1.061405429))))
    phi = jnp.where(v >= 0, 1.0 - tail, tail)
    return v * phi, phi + v * bell * 0.3989422804014327


ROW_BLOCK = 64


def over_rows(rows, step, carry):
    def one(n, kept):
        return step(pl.ds(pl.multiple_of(n * ROW_BLOCK, ROW_BLOCK), ROW_BLOCK), kept)

    return lax.fori_loop(0, rows // ROW_BLOCK, one, carry)


OUT_BIAS, FIRST_GAIN, FIRST_SHIFT, DOWN_BIAS, SECOND_GAIN, SECOND_SHIFT, POOL_BIAS, CLASS_BIAS, UP_BIAS = range(9)
LOSS = 12
CLASS_ROWS = (6, 7, 13)


def orders(bits):
    head = bits - 1
    rest = list(range(2, head))
    both = [[0, 1, head] + rest, [0, head, 1] + rest]
    return [both + [[0] + rest[:1] + pair + rest[1:]] for pair in ([1, head], [head, 1])]


def rest_of_layer(context, inputs, class_turned, out_weight, vectors, log_totals, cotangent, up_weight, down_weight,
                  pool_weight, queries, keys, values, full, lengths, labels, bits):
    rows, width = inputs.shape
    hidden = up_weight.shape[1]
    half = width // 2
    times = hidden // width
    devices = 1 << bits
    block = 2 * width // devices
    classes = class_turned.shape[0]
    per_width = width // 128
    fact_rows = -(-2 * per_width // 16) * 16
    small_half = 8
    late_lanes = width // 3
    plans = orders(bits)
    parts = len(plans[0])
    lanes_part = half // parts
    count = 2 * times + 4
    out_at, query_at = 2 * times, 2 * times + 1
    stages = bits
    head = bits - 1
    small_order = [1, head] + list(range(2, head)) + [0]
    pairs = width // 128
    dp_dims = (2,) * (bits - 1)

    def kernel(lengths_ref, labels_ref, ctx_ref, x_ref, cls_in, ow_ref, v0, v1, v2, v3, v4, v5, v6, v7, v8, lse_ref,
               cot_hbm, up_hbm, down_hbm, pool_hbm, q_hbm, k_hbm, v_hbm, wq_hbm, wk_hbm, wv_hbm,
               states_out, grad_out, logit_ref, sums_ref, small_out, late_out, factor_out, held, *rest):
        got = rest[:stages]
        (gb_ref, up_w, down_w, pool_w, low_ref, n1, r1, n2, r2, hid_even, hid_odd, slope_even, slope_odd, acc, whole, frow, vec_ref, cls_ref, small_ref,
         small_buf, small_got, late_buf, late_got, load_sem, late_sem, send, recv, side_send, side_recv, whole_sem) = rest[stages:]
        place = Place(bits)
        loads = []
        for i, (source, target) in enumerate(
            ((up_hbm, up_w), (down_hbm, down_w), (pool_hbm, pool_w), (cot_hbm, gb_ref))):
            load = pltpu.make_async_copy(source, target, load_sem.at[i])
            load.start()
            loads.append(load)
        place.greet(range(bits))
        length = lengths_ref[place.head]
        slot = sum(place.mine[bit] * (1 << k) for k, bit in enumerate(small_order))
        hids, slopes = (hid_even, hid_odd), (slope_even, slope_odd)

        def index(i, done, fixed):
            out = [i]
            for bit in reversed(range(bits)):
                out.append(fixed[bit] if bit in fixed else place.mine[bit] if bit in done else slice(None))
            return tuple(out)

        def part_copy(i, s):
            plan = plans[i // parts % 2][i % parts]
            bit = plan[s]
            return pltpu.make_async_remote_copy(
                src_ref=held.at[index(i, plan[:s], {bit: 1 - place.mine[bit]})], dst_ref=got[s].at[i],
                send_sem=send.at[i, s], recv_sem=recv.at[i, s], device_id=place.partner(bit), device_id_type=MESH)

        def add_part(i, s):
            part_copy(i, s).wait_recv()
            where = index(i, plans[i // parts % 2][i % parts][: s + 1], {})
            if s == stages - 1:
                sums_ref[i] = held[where].astype(F32) + got[s][i].astype(F32)
            else:
                held[where] = held[where] + got[s][i]

        def take(name):
            for code in SCHEDULE[name]:
                if code >= 2000:
                    side_advance(code // 1000 - 2, code % 10)
                    continue
                i, s = code // 100 * parts + code // 10 % 10, code % 10
                if s > 0:
                    add_part(i, s - 1)
                if s < stages:
                    part_copy(i, s).start()

        def take_after(step, prefix, steps):
            for n in steps:
                if not SCHEDULE[prefix + str(n)]:
                    continue

                @pl.when(step == n)
                def _():
                    take(prefix + str(n))

        def put(i, wide, lead):
            for h in range(2):
                for m in range(parts):
                    at = h * half + m * lanes_part
                    held[(i * parts + m, h) + lead] = wide[..., at : at + lanes_part]

        def side_copy(kind, s):
            bit = small_order[s % stages]
            if kind == 0:
                start = (slot // (1 << s)) * (1 << s)
                source = target = factor_out.at[pl.ds(start, 1 << s)]
            elif kind == 2:
                source, target = late_buf.at[s], late_got.at[s]
            else:
                bit = small_order[(s - 1) % stages]
                if s == 0:
                    source, target = small_ref.at[rows_of_core(1 - place.mine[0])], small_got.at[0]
                elif s == stages:
                    source = target = small_out.at[rows_of_core(place.mine[0])]
                else:
                    source, target = small_buf.at[s], small_got.at[s]
            return pltpu.make_async_remote_copy(
                src_ref=source, dst_ref=target, send_sem=side_send.at[kind, s], recv_sem=side_recv.at[kind, s],
                device_id=place.partner(bit), device_id_type=MESH)

        def rows_of_core(core):
            return pl.ds(pl.multiple_of(core * small_half, small_half), small_half)

        def side_advance(kind, s):
            last = stages + (kind == 1)
            if s > 0:
                side_copy(kind, s - 1).wait_recv()
            if kind == 1 and 0 < s < last:
                mine = rows_of_core(place.mine[0])
                total = (small_ref[mine, :] if s == 1 else small_buf[s - 1]) + small_got[s - 1]
                if s < stages:
                    small_buf[s] = total
                else:
                    small_out[mine, :] = total
            if kind == 2 and s > 0:
                total = late_buf[s - 1] + late_got[s - 1]
                if s < stages:
                    late_buf[s] = total
                else:
                    late_out[...] = total
            if s < last:
                side_copy(kind, s).start()

        for i, ref in enumerate((v0, v1, v2, v3, v4, v5, v6)):
            vec_ref[i : i + 1, :] = ref[...].astype(F32).reshape(1, width)
        vec_ref[CLASS_BIAS : CLASS_BIAS + 1, 0:classes] = v7[...].astype(F32).reshape(1, classes)
        wide_bias = v8[...].astype(F32).reshape(1, hidden)
        for t in range(times):
            vec_ref[UP_BIAS + t : UP_BIAS + t + 1, :] = wide_bias[:, t * width : (t + 1) * width]
        cls_ref[...] = jnp.zeros_like(cls_ref)
        cls_ref[0:classes, :] = cls_in[...]

        def vec(i):
            return vec_ref[i : i + 1, :]

        acc[...] = matmul(ctx_ref[...], ow_ref[...])

        def norm_one(at, carry):
            value = x_ref[at, :].astype(F32) + (acc[at, :] + vec(OUT_BIAS))
            center = value - jnp.mean(value, -1, keepdims=True)
            scale = lax.rsqrt(jnp.mean(center * center, -1, keepdims=True) + EPSILON)
            normal = center * scale
            n1[at, :] = normal
            r1[at, :] = scale
            low_ref[at, :] = (normal * vec(FIRST_GAIN) + vec(FIRST_SHIFT)).astype(BF16)
            acc[at, :] = jnp.zeros_like(normal)
            return carry

        over_rows(rows, norm_one, 0)
        loads[0].wait()
        loads[1].wait()

        def at_chunk(c):
            return pl.ds(pl.multiple_of(c * width, width), width)

        def pre_of(c, parity):
            slopes[parity][:, at_chunk(c // 2)] = matmul(low_ref[...], up_w[:, at_chunk(c)]) + vec_ref[pl.ds(UP_BIAS + c, 1), :]

        def activate(c, parity):
            at = at_chunk(c // 2)
            act, deriv = gelu_parts(slopes[parity][:, at])
            hids[parity][:, at] = act.astype(BF16)
            slopes[parity][:, at] = deriv

        def add_branch(c, parity):
            acc[...] += matmul(hids[parity][:, at_chunk(c // 2)], down_w[at_chunk(c), :])

        pre_of(0, 0)
        pre_of(1, 1)
        activate(0, 0)

        def forward(n, carry):
            c = 2 * n
            pre_of(c + 2, 0)
            activate(c + 1, 1)
            add_branch(c, 0)
            pre_of(c + 3, 1)
            activate(c + 2, 0)
            add_branch(c + 1, 1)
            return carry

        lax.fori_loop(0, times // 2 - 1, forward, 0)
        activate(times - 1, 1)
        add_branch(times - 2, 0)
        add_branch(times - 1, 1)

        def norm_two(at, carry):
            first = n1[at, :] * vec(FIRST_GAIN) + vec(FIRST_SHIFT)
            value = first + (acc[at, :] + vec(DOWN_BIAS))
            center = value - jnp.mean(value, -1, keepdims=True)
            scale = lax.rsqrt(jnp.mean(center * center, -1, keepdims=True) + EPSILON)
            normal = center * scale
            n2[at, :] = normal
            r2[at, :] = scale
            whole[at, :] = (normal * vec(SECOND_GAIN) + vec(SECOND_SHIFT)).astype(BF16)
            return carry

        over_rows(rows, norm_two, 0)
        states_copy = pltpu.make_async_copy(whole, states_out, whole_sem.at[0])
        states_copy.start()

        loads[2].wait()
        loads[3].wait()
        lead = whole[0:16, :]
        pooled = jnp.tanh(matmul(lead, pool_w[...]) + vec(POOL_BIAS))
        pooled_low = pooled.astype(BF16)
        logits = nt(pooled_low, cls_ref[...]) + vec_ref[CLASS_BIAS : CLASS_BIAS + 1, 0:128]
        lanes = lane_iota(logits.shape)
        logits = jnp.where(lanes < classes, logits, NEGATIVE)
        top = jnp.max(logits, -1, keepdims=True)
        norm = top + jnp.log(jnp.sum(jnp.exp(logits - top), -1, keepdims=True))
        target = jnp.where(lanes == labels_ref[0], 1.0, 0.0)
        loss = (norm - jnp.sum(jnp.where(lanes < classes, target * logits, 0.0), -1, keepdims=True)) / devices
        grad_logits = (jnp.where(lanes < classes, jnp.exp(logits - norm) - target, 0.0) / devices).astype(BF16)
        grad_pooled = (matmul(grad_logits, cls_ref[...]) * (1.0 - pooled * pooled)).astype(BF16)
        grad_lead = nt(grad_pooled, pool_w[...])
        logit_ref[...] = logits[0:1, 0:classes]
        frow[...] = jnp.zeros_like(frow)
        for k, value in enumerate((lead, grad_pooled)):
            wide = value.astype(F32)
            for j in range(per_width):
                frow[k * per_width + j : k * per_width + j + 1, :] = wide[0:1, j * 128 : (j + 1) * 128]
        small_ref[...] = jnp.zeros(small_ref.shape, F32)
        logit_row = grad_logits.astype(F32)[0:1, :]
        pooled_row = pooled_low.astype(F32)[0:1, :]
        for k in range(classes):
            small_ref[CLASS_ROWS[k] : CLASS_ROWS[k] + 1, :] = logit_row[:, k : k + 1] * pooled_row
        factor_out[slot] = frow[...].astype(BF16)
        take("R")

        def back_two(at, sums):
            gain_sum, shift_sum, bias_sum = sums
            row = at.start + lax.broadcasted_iota(jnp.int32, (ROW_BLOCK, width), 0)
            grad = gb_ref[at, :].astype(F32) + jnp.where(row == 0, grad_lead[0:1, :], 0.0)
            normal = n2[at, :]
            e = grad * vec(SECOND_GAIN)
            value = (e - jnp.mean(e, -1, keepdims=True) - normal * jnp.mean(e * normal, -1, keepdims=True)) * r2[at, :]
            rounded = value.astype(BF16)
            acc[at, :] = value
            gb_ref[at, :] = rounded
            return (gain_sum + jnp.sum(grad * normal, 0, keepdims=True), shift_sum + jnp.sum(grad, 0, keepdims=True),
                    bias_sum + jnp.sum(rounded.astype(F32), 0, keepdims=True))

        zero = jnp.zeros((1, width), F32)
        gain_sum, shift_sum, bias_sum = over_rows(rows, back_two, (zero, zero, zero))
        small_ref[SECOND_GAIN : SECOND_GAIN + 1, :] = gain_sum
        small_ref[SECOND_SHIFT : SECOND_SHIFT + 1, :] = shift_sum
        small_ref[DOWN_BIAS : DOWN_BIAS + 1, :] = bias_sum
        small_ref[LOSS : LOSS + 1, 0:128] = jnp.broadcast_to(loss[0:1, 0:1], (1, 128))
        small_ref[LOSS : LOSS + 1, 128:256] = logit_row

        take("B")

        def down_grads(n, carry):
            for parity in range(2):
                c = 2 * n + parity
                wide = tn(hids[parity][:, at_chunk(n)], gb_ref[...]).astype(BF16).reshape(2, 2, times, block, width)
                for t in range(times):
                    put(t, wide[:, :, t], (lax.rem(c // 2, 2), lax.rem(c, 2)))
                take_after(c, "D", range(parity, times, 2))
            return carry

        lax.fori_loop(0, times // 2, down_grads, 0)

        for parity in range(2):

            def up_grads(h, carry):
                c = 2 * h + parity
                step = 4 * parity + 2 * h
                grad = (nt(gb_ref[...], down_w[at_chunk(c), :]) * slopes[parity][:, at_chunk(h)]).astype(BF16)
                small_ref[pl.ds(UP_BIAS + c, 1), :] = jnp.sum(grad.astype(F32), 0, keepdims=True)
                wide = tn(low_ref[...], grad).astype(BF16)
                for t in range(2):
                    for m in range(parts):
                        at = t * half + m * lanes_part
                        held[(times + 2 * parity + t) * parts + m, h] = wide[:, at : at + lanes_part].reshape(
                            dp_dims + (block, lanes_part))
                take_after(step, "U", range(4 * parity, 4 * parity + 4, 2))
                acc[...] += nt(grad, up_w[:, at_chunk(c)])
                take_after(step + 1, "U", range(4 * parity + 1, 4 * parity + 4, 2))
                return carry

            lax.fori_loop(0, 2, up_grads, 0)

        late = []
        for i, (source, target) in enumerate((
            (q_hbm, down_w.at[0:rows, :]), (k_hbm, down_w.at[rows : 2 * rows, :]),
            (v_hbm, down_w.at[2 * rows : 3 * rows, :]), (wq_hbm, up_w.at[:, 0:width]),
            (wk_hbm, up_w.at[:, width : 2 * width]), (wv_hbm, up_w.at[:, 2 * width : 3 * width]),
        )):
            load = pltpu.make_async_copy(source, target, late_sem.at[i])
            load.start()
            late.append(load)

        def back_one(at, sums):
            gain_sum, shift_sum, bias_sum = sums
            grad = acc[at, :]
            normal = n1[at, :]
            e = grad * vec(FIRST_GAIN)
            value = (e - jnp.mean(e, -1, keepdims=True) - normal * jnp.mean(e * normal, -1, keepdims=True)) * r1[at, :]
            rounded = value.astype(BF16)
            acc[at, :] = value
            low_ref[at, :] = rounded
            return (gain_sum + jnp.sum(grad * normal, 0, keepdims=True), shift_sum + jnp.sum(grad, 0, keepdims=True),
                    bias_sum + jnp.sum(rounded.astype(F32), 0, keepdims=True))

        gain_sum, shift_sum, bias_sum = over_rows(rows, back_one, (zero, zero, zero))
        small_ref[FIRST_GAIN : FIRST_GAIN + 1, :] = gain_sum
        small_ref[FIRST_SHIFT : FIRST_SHIFT + 1, :] = shift_sum
        small_ref[OUT_BIAS : OUT_BIAS + 1, :] = bias_sum
        take("L0")
        put(out_at, tn(ctx_ref[...], low_ref[...]).astype(BF16).reshape(dp_dims + (block, width)), ())
        take("L1")
        hids[1][:, width : 2 * width] = nt(low_ref[...], ow_ref[...]).astype(BF16)
        take("L2")

        lanes_row = lax.broadcasted_iota(jnp.int32, (128, rows), 0)
        pair_lanes = lane_iota((rows, 128))
        for load in late:
            load.wait()

        def attend(pair, carry):
            def at(n):
                return pl.ds(pl.multiple_of(n % 2 * width + pair * 128, 128), 128)

            q2 = down_w[0:rows, at(0)]
            k2 = down_w[rows : 2 * rows, at(0)]
            v2 = down_w[2 * rows : 3 * rows, at(0)]
            g2 = hids[1][:, at(3)]
            k2t = k2.T
            heads_of = []
            for parity in range(2):
                qa, ka = pair_operands(q2, k2, length, parity)
                mine = (pair_lanes < HEAD_DIM) if parity == 0 else (pair_lanes >= HEAD_DIM)
                va = jnp.where(mine, v2.astype(F32), 0.0).astype(BF16)
                probs = jnp.exp(nt(ka, qa) - lse_ref[pair, parity : parity + 1, :])
                grad_v = matmul(probs.astype(BF16), g2)
                grad_probs = nt(va, g2)
                inner = jnp.sum(probs * grad_probs, 0, keepdims=True)
                grad_scores = (probs * (grad_probs - inner)).astype(BF16)
                heads_of.append((grad_v, matmul(grad_scores, qa), matmul(k2t, grad_scores)))
                take_after(2 * pair + parity, "P", range(parity, 2 * pairs, 2))
            first = pair_lanes < HEAD_DIM
            turned = jnp.where(lanes_row < HEAD_DIM, heads_of[0][2], heads_of[1][2]) * HEAD_DIM ** -0.5
            hids[0][:, at(0)] = turned.T.astype(BF16)
            hids[0][:, at(1)] = jnp.where(first, heads_of[0][1], heads_of[1][1]).astype(BF16)
            hids[1][:, at(2)] = jnp.where(first, heads_of[0][0], heads_of[1][0]).astype(BF16)
            return carry

        lax.fori_loop(0, pairs, attend, 0)

        def grads_of(n):
            return hids[n // 2][:, n % 2 * width : (n % 2 + 1) * width]

        late_buf[0] = jnp.zeros(late_buf.shape[1:], F32)
        for n in range(2):
            total = jnp.sum(grads_of(2 * n).astype(F32), 0, keepdims=True)
            for t in range(3):
                late_buf[0, 3 * n + t : 3 * n + t + 1, :] = total[:, t * late_lanes : (t + 1) * late_lanes]
        take("Q")
        for n in range(3):
            put(query_at + n, tn(x_ref[...], grads_of(n)).astype(BF16).reshape(dp_dims + (block, width)), ())
            take("W" + str(n))
        states_copy.wait()
        for n in range(3):
            acc[...] += nt(grads_of(n), up_w[:, n * width : (n + 1) * width])
            take("I" + str(n))
        whole[...] = acc[...].astype(BF16)
        grad_copy = pltpu.make_async_copy(whole, grad_out, whole_sem.at[1])
        grad_copy.start()
        for n in range(4):
            take("T" + str(n))
        grad_copy.wait()
        for i in range(count * parts):
            for s in range(stages):
                part_copy(i, s).wait_send()
        for s in range(stages):
            for kind in range(3):
                side_copy(kind, s).wait_send()
        side_copy(1, stages).wait_send()

    vmem = pl.BlockSpec(memory_space=pltpu.VMEM)
    anywhere = pl.BlockSpec(memory_space=pl.ANY)
    smem = pl.BlockSpec(memory_space=pltpu.SMEM)
    act = jax.ShapeDtypeStruct((rows, width), BF16)
    return pl.pallas_call(
        kernel,
        out_shape=[
            act, act, jax.ShapeDtypeStruct((1, classes), F32), jax.ShapeDtypeStruct((count * parts, block, lanes_part), F32),
            jax.ShapeDtypeStruct((16, width), F32), jax.ShapeDtypeStruct((8, late_lanes), F32),
            jax.ShapeDtypeStruct((devices, fact_rows, 128), BF16),
        ],
        in_specs=[smem] * 2 + [vmem] * 14 + [anywhere] * 10,
        out_specs=[anywhere] * 2 + [vmem] * 5,
        scratch_shapes=[pltpu.VMEM((count * parts, 2) + dp_dims + (block, lanes_part), BF16)]
        + [pltpu.VMEM((count * parts,) + (2,) * (stages - 1 - s) + (block, lanes_part), BF16) for s in range(stages)]
        + [
            pltpu.VMEM((rows, width), BF16),
            pltpu.VMEM((width, hidden), BF16),
            pltpu.VMEM((hidden, width), BF16),
            pltpu.VMEM((width, width), BF16),
            pltpu.VMEM((rows, width), BF16),
            pltpu.VMEM((rows, width), F32),
            pltpu.VMEM((rows, 1), F32),
            pltpu.VMEM((rows, width), F32),
            pltpu.VMEM((rows, 1), F32),
            pltpu.VMEM((rows, hidden // 2), BF16),
            pltpu.VMEM((rows, hidden // 2), BF16),
            pltpu.VMEM((rows, hidden // 2), F32),
            pltpu.VMEM((rows, hidden // 2), F32),
            pltpu.VMEM((rows, width), F32),
            pltpu.VMEM((rows, width), BF16),
            pltpu.VMEM((fact_rows, 128), F32),
            pltpu.VMEM((16, width), F32),
            pltpu.VMEM((128, width), BF16),
            pltpu.VMEM((16, width), F32),
            pltpu.VMEM((stages, small_half, width), F32),
            pltpu.VMEM((stages, small_half, width), F32),
            pltpu.VMEM((stages, 8, late_lanes), F32),
            pltpu.VMEM((stages, 8, late_lanes), F32),
            pltpu.SemaphoreType.DMA((4,)),
            pltpu.SemaphoreType.DMA((6,)),
            pltpu.SemaphoreType.DMA((count * parts, stages)),
            pltpu.SemaphoreType.DMA((count * parts, stages)),
            pltpu.SemaphoreType.DMA((3, stages + 1)),
            pltpu.SemaphoreType.DMA((3, stages + 1)),
            pltpu.SemaphoreType.DMA((2,)),
        ],
        compiler_params=pltpu.CompilerParams(collective_id=1, has_side_effects=True, vmem_limit_bytes=VMEM_LIMIT),
        name="rest_of_layer",
    )(lengths, labels, context, inputs, class_turned, out_weight, *vectors, log_totals, cotangent, up_weight,
      down_weight, pool_weight, queries, keys, values, *full)


SCHEDULE = {
    "R": (),
    "B": (),
    "D0": (),
    "D1": (),
    "D2": (),
    "D3": (0, 10, 20, 100, 110,),
    "U0": (120, 200, 210, 220, 300,),
    "U1": (1, 11, 21, 310, 320,),
    "U2": (101, 111, 121, 400, 410, 420, 500, 510,),
    "U3": (201, 211, 221, 520,),
    "U4": (2, 12, 22, 311, 321,),
    "U5": (112, 421,),
    "U6": (102, 122, 212, 222, 521, 600, 610, 620, 700, 710,),
    "U7": (202, 301, 720,),
    "L0": (3, 23, 3000,),
    "L1": (13, 322, 312, 113, 800, 810, 820,),
    "L2": (411, 621,),
    "P0": (422, 123,),
    "P1": (103, 203, 223, 522, 401, 2000,),
    "P2": (4, 14, 24, 114, 213, 323, 302, 721, 501, 511,),
    "P3": (313, 3001,),
    "P4": (104, 124, 224, 423, 412, 204, 611, 821,),
    "P5": (5, 15, 214, 324, 303, 25, 523, 622, 2001,),
    "P6": (115, 402, 601,),
    "P7": (105, 125, 314, 424, 502, 512, 722, 225, 3002,),
    "P8": (205, 215, 325, 524, 304, 413, 822, 711,),
    "P9": (612, 701, 403, 623, 2002,),
    "P10": (315, 425, 503, 602,),
    "P11": (525, 414, 513, 305, 723, 801, 811, 3003,),
    "Q": (404, 4000,),
    "W0": (823, 900, 910, 920,),
    "W1": (504, 624, 613, 712, 1000, 1010, 1020, 2003,),
    "W2": (1100, 1110, 1120,),
    "I0": (415, 514, 603, 702, 724, 901, 3004,),
    "I1": (405, 911, 921, 812,),
    "I2": (505, 614, 824, 802, 1001, 625, 1021, 4001,),
    "T0": (1011, 1101, 1111, 1121, 604, 713, 703, 515, 725, 902, 912, 922, 615, 813, 825, 2004, 3005, 4002,),
    "T1": (605, 803, 1022, 1002, 1012, 1122, 1102, 714, 1112, 704, 913, 814, 903, 804, 1023, 4003, 3006,),
    "T2": (923, 715, 1013, 914, 705, 1003, 904, 815, 1113, 805, 1123, 924, 1014, 1103, 1004, 2005, 4004,),
    "T3": (915, 1024, 1114, 905, 1124, 925, 1104, 1015, 1005, 1025, 1115, 1125, 1105, 4005,),
}


def spread(states, input_grad, logits, sums, small, late, gathered, classes):
    width = small.shape[1]
    half = width // 2
    parts, block, lanes_part = sums.shape
    count = parts * lanes_part // half
    parts = parts // count
    devices = gathered.shape[0]
    times = (count - 4) // 2
    lanes = width // 128

    def kernel(states_ref, grad_ref, logits_ref, sums_ref, small_ref, late_ref, got_ref, states_out, grad_out, logits_out, up, down,
               out, query, key, value, pool, query_bias, value_bias, out_bias, first_gain, first_shift, up_bias,
               down_bias, second_gain, second_shift, pool_bias, class_weight, class_bias, loss, left, right, late_wide, sem):
        copies = [
            pltpu.make_async_copy(states_ref, states_out, sem.at[0]), pltpu.make_async_copy(grad_ref, grad_out, sem.at[1])]
        for copy in copies:
            copy.start()
        logits_out[...] = logits_ref[...]
        dp, head = lax.axis_index("dp"), lax.axis_index("head")
        for m in range(parts):
            at = slice(m * lanes_part, (m + 1) * lanes_part)
            for t in range(times):
                down[t * block : (t + 1) * block, at] = sums_ref[t * parts + m]
                up[:, t * half + m * lanes_part : t * half + (m + 1) * lanes_part] = sums_ref[(times + t) * parts + m]
            for k, ref in enumerate((out, query, key, value)):
                ref[:, at] = sums_ref[(2 * times + k) * parts + m]
        got = got_ref[...].astype(F32)

        def wide(k):
            return jnp.concatenate([got[:, k * lanes + j, :] for j in range(lanes)], 1)

        lead, grad_pooled = wide(0), wide(1)
        left[...] = lead.T
        right[...] = grad_pooled
        at = pl.ds(pl.multiple_of(head * half, half), half)
        pool[...] = matmul(
            left[pl.ds(pl.multiple_of(dp * block, 8), block), :].astype(BF16), right[:, at].astype(BF16))
        pool_bias[...] = jnp.sum(grad_pooled, 0)
        for k in range(classes):
            class_weight[k : k + 1, :] = small_ref[CLASS_ROWS[k] : CLASS_ROWS[k] + 1, :]
        class_bias[...] = small_ref[LOSS : LOSS + 1, 128 : 128 + classes].reshape(classes)
        for n in range(2):
            late_wide[n : n + 1, :] = jnp.concatenate([late_ref[3 * n + t : 3 * n + t + 1, :] for t in range(3)], 1)
        query_bias[...] = late_wide[0:1, at].reshape(half)
        value_bias[...] = late_wide[1:2, at].reshape(half)
        for ref, row in ((out_bias, OUT_BIAS), (first_gain, FIRST_GAIN), (first_shift, FIRST_SHIFT),
                         (down_bias, DOWN_BIAS), (second_gain, SECOND_GAIN), (second_shift, SECOND_SHIFT)):
            ref[...] = small_ref[row, :]
        up_bias[...] = jnp.concatenate(
            [small_ref[UP_BIAS + t : UP_BIAS + t + 1, :] for t in range(times)], 1).reshape(times * width)
        loss[()] = small_ref[LOSS, 0]
        for copy in copies:
            copy.wait()

    def f32(*shape):
        return jax.ShapeDtypeStruct(shape, F32)

    square = f32(block, half)
    row = f32(width)
    act = jax.ShapeDtypeStruct(states.shape, BF16)
    vmem = pl.BlockSpec(memory_space=pltpu.VMEM)
    anywhere = pl.BlockSpec(memory_space=pl.ANY)
    return pl.pallas_call(
        kernel,
        out_shape=[
            act, act, f32(1, classes), f32(block, times * half), f32(times * block, half), square, square, square, square,
            square, f32(half), f32(half), row, row, row, f32(times * width), row, row, row, row, f32(classes, width),
            f32(classes), f32(),
        ],
        in_specs=[vmem] * 7,
        out_specs=[anywhere] * 2 + [vmem] * 20 + [pl.BlockSpec(memory_space=pltpu.SMEM)],
        scratch_shapes=[
            pltpu.VMEM((width, devices), F32), pltpu.VMEM((devices, width), F32),
            pltpu.VMEM((8, width), F32), pltpu.SemaphoreType.DMA((2,))],
        compiler_params=pltpu.CompilerParams(vmem_limit_bytes=VMEM_LIMIT),
        name="spread",
    )(states, input_grad, logits, sums, small, late, gathered)


def plain_body(
    inputs, lengths, labels, state_cotangent, query_weight, query_bias, key_weight, value_weight, value_bias,
    out_weight, out_bias, first_gain, first_shift, up_weight, up_bias, down_weight, down_bias, second_gain,
    second_shift, pool_weight, pool_bias, class_weight, class_bias,
):
    scale = HEAD_DIM ** (-0.5)
    dp_size, head_size = lax.axis_size("dp"), lax.axis_size("head")
    dp_at, head_at = lax.axis_index("dp"), lax.axis_index("head")
    devices = dp_size * head_size
    width = inputs.shape[1]
    block_columns = width // head_size
    row_seqs = labels.shape[0]
    assert row_seqs == 1 and inputs.shape[0] == SEQ_LEN
    length = lax.dynamic_index_in_dim(lengths, head_at, keepdims=False)

    weights = [query_weight, key_weight, value_weight]
    full = [lax.all_gather(w, "head", axis=1, tiled=True) for w in weights]
    biases = lax.all_gather(jnp.stack([query_bias, value_bias]), "head", axis=1, tiled=True)
    query_bias, value_bias = biases[0], biases[1]
    wq, wk, wv = full
    head_count = width // HEAD_DIM

    def heads(matrix):
        return matrix.reshape(SEQ_LEN, head_count, HEAD_DIM)

    queries = (matmul(inputs, wq) + query_bias).astype(BF16)
    keys_low = matmul(inputs, wk).astype(BF16)
    values_low = (matmul(inputs, wv) + value_bias).astype(BF16)
    visible = lax.broadcasted_iota(jnp.int32, (1, 1, SEQ_LEN), 2) < length

    def scores_of():
        raw = jnp.einsum("qhd,khd->hqk", heads(queries), heads(keys_low), preferred_element_type=F32) * scale
        return jnp.where(visible, raw, NEGATIVE)

    scores = scores_of()
    peak = jnp.max(scores, -1, keepdims=True)
    raised = jnp.exp(scores - peak)
    denominator = jnp.sum(raised, -1, keepdims=True)
    probs = raised / denominator
    log_total = peak + jnp.log(denominator)
    context = jnp.einsum("hqk,khd->qhd", probs.astype(BF16), heads(values_low), preferred_element_type=F32)
    context_rows = context.astype(BF16).reshape(SEQ_LEN, width)
    attended = matmul(context_rows, out_weight) + out_bias
    first_out, first_back = jax.vjp(
        normalize, inputs.astype(F32) + attended, first_gain.astype(F32), first_shift.astype(F32))
    first_low = first_out.astype(BF16)
    hidden_pre = matmul(first_low, up_weight) + up_bias
    hidden_act, gelu_back = jax.vjp(partial(jax.nn.gelu, approximate=False), hidden_pre)
    hidden_low = hidden_act.astype(BF16)
    branch = matmul(hidden_low, down_weight) + down_bias
    normed, second_back = jax.vjp(normalize, first_out + branch, second_gain.astype(F32), second_shift.astype(F32))
    leading_low = normed.reshape(row_seqs, SEQ_LEN, -1)[:, 0].astype(BF16)
    pooled = jnp.tanh(matmul(leading_low, pool_weight) + pool_bias)
    pooled_low = pooled.astype(BF16)
    logits = matmul(pooled_low, class_weight) + class_bias
    classes = lax.broadcasted_iota(jnp.int32, logits.shape, 1)
    target = (classes == labels[:, None]).astype(F32)
    log_norm = jax.nn.logsumexp(logits, axis=-1)
    loss_part = jnp.sum(log_norm - jnp.sum(target * logits, -1)) / devices
    grad_logits = ((jnp.exp(logits - log_norm[:, None]) - target) / devices).astype(BF16)
    grad_class_weight = matmul(pooled_low.T, grad_logits)
    grad_class_bias = column_sums(grad_logits)
    grad_pooled = (matmul(grad_logits, class_weight.T) * (1.0 - pooled * pooled)).astype(BF16)
    grad_pool_bias = column_sums(grad_pooled)
    grad_leading = matmul(grad_pooled, pool_weight.T)
    grad_normed = state_cotangent.astype(F32).reshape(row_seqs, SEQ_LEN, -1)
    grad_normed = grad_normed.at[:, 0].add(grad_leading).reshape(normed.shape)
    grad_second, grad_second_gain, grad_second_shift = second_back(grad_normed)
    grad_branch = grad_second.astype(BF16)
    grad_down_weight = matmul(hidden_low.T, grad_branch)
    grad_down_bias = column_sums(grad_branch)
    grad_hidden = gelu_back(matmul(grad_branch, down_weight.T))[0].astype(BF16)
    grad_up_weight = matmul(first_low.T, grad_hidden)
    grad_up_bias = column_sums(grad_hidden)
    grad_first_out = grad_second + matmul(grad_hidden, up_weight.T)
    grad_first, grad_first_gain, grad_first_shift = first_back(grad_first_out)
    grad_attended = grad_first.astype(BF16)
    grad_out_weight = matmul(context_rows.T, grad_attended)
    grad_out_bias = column_sums(grad_attended)
    grad_context = heads(matmul(grad_attended, out_weight.T).astype(BF16))
    probs_again = jnp.exp(scores_of() - log_total)
    grad_values = jnp.einsum(
        "hqk,qhd->khd", probs_again.astype(BF16), grad_context, preferred_element_type=F32).astype(BF16)
    grad_probs = jnp.einsum("qhd,khd->hqk", grad_context, heads(values_low), preferred_element_type=F32)
    grad_scores = probs_again * (grad_probs - jnp.sum(probs_again * grad_probs, -1, keepdims=True))
    grad_scores = grad_scores.astype(BF16)
    grad_queries = (
        jnp.einsum("hqk,khd->qhd", grad_scores, heads(keys_low), preferred_element_type=F32) * scale).astype(BF16)
    grad_keys = (
        jnp.einsum("hqk,qhd->khd", grad_scores, heads(queries), preferred_element_type=F32) * scale).astype(BF16)
    grad_queries = grad_queries.reshape(SEQ_LEN, width)
    grad_keys = grad_keys.reshape(SEQ_LEN, width)
    grad_values = grad_values.reshape(SEQ_LEN, width)
    grad_query_weight = matmul(inputs.T, grad_queries)
    grad_key_weight = matmul(inputs.T, grad_keys)
    grad_value_weight = matmul(inputs.T, grad_values)
    input_grad = (
        grad_first + matmul(grad_queries, wq.T) + matmul(grad_keys, wk.T) + matmul(grad_values, wv.T)).astype(BF16)

    small_parts = (
        grad_out_bias, grad_first_gain, grad_first_shift, grad_up_bias, grad_down_bias, grad_second_gain,
        grad_second_shift, grad_pool_bias, column_sums(grad_queries), column_sums(grad_values),
        grad_class_weight.reshape(-1), grad_class_bias, loss_part.reshape(1),
    )
    grads = (grad_up_weight, grad_down_weight, grad_out_weight, grad_query_weight, grad_key_weight, grad_value_weight)
    grads = grads + (matmul(leading_low.T, grad_pooled),)

    def scatter(matrix):
        part = lax.psum_scatter(matrix, "dp", scatter_dimension=0, tiled=True)
        return lax.psum_scatter(part.astype(BF16), "head", scatter_dimension=1, tiled=True).astype(F32)

    up_total, down_total, out_total, query_total, key_total, value_total, pool_total = map(scatter, grads)
    totals = lax.psum(small_parts, ("dp", "head"))
    (
        out_bias_total, first_gain_total, first_shift_total, up_bias_total, down_bias_total, second_gain_total,
        second_shift_total, pool_bias_total, query_bias_total, value_bias_total, class_weight_total,
        class_bias_total, loss,
    ) = totals
    query_bias_total = lax.dynamic_slice_in_dim(query_bias_total, head_at * block_columns, block_columns)
    value_bias_total = lax.dynamic_slice_in_dim(value_bias_total, head_at * block_columns, block_columns)
    return (
        normed.astype(BF16), input_grad, logits, loss.reshape(()), query_total, query_bias_total, key_total,
        value_total, value_bias_total, out_total, out_bias_total, first_gain_total, first_shift_total, up_total,
        up_bias_total, down_total, down_bias_total, second_gain_total, second_shift_total, pool_total,
        pool_bias_total, class_weight_total.reshape(class_weight.shape), class_bias_total,
    )


def body(*args):
    (
        inputs, lengths, labels, state_cotangent, query_weight, query_bias, key_weight, value_weight, value_bias,
        out_weight, out_bias, first_gain, first_shift, up_weight, up_bias, down_weight, down_bias, second_gain,
        second_shift, pool_weight, pool_bias, class_weight, class_bias,
    ) = args
    dp_size, head_size = lax.axis_size("dp"), lax.axis_size("head")
    devices = dp_size * head_size
    bits = devices.bit_length() - 1
    rows, width = inputs.shape
    hidden = up_weight.shape[1]
    classes = class_weight.shape[1]
    direct = (
        (width // dp_size) % 16 == 0 and head_size == 2 and bits == 5 and hidden == 4 * width and rows == SEQ_LEN
        and labels.shape[0] == 1 and classes == len(CLASS_ROWS)
    )
    if not direct:
        return plain_body(*args)

    queries, keys, values, context, log_totals, *full = attention_forward(
        inputs, [query_weight, key_weight, value_weight], [query_bias, value_bias], lengths, bits)
    vectors = (out_bias, first_gain, first_shift, down_bias, second_gain, second_shift, pool_bias, class_bias, up_bias)
    states, input_grad, logits, sums, small, late, gathered = rest_of_layer(
        context, inputs, class_weight.T, out_weight, vectors, log_totals, state_cotangent, up_weight, down_weight,
        pool_weight, queries, keys, values, full, lengths, labels, bits)
    (
        states, input_grad, logits, up, down, out, query, key, value, pool, query_sum, value_sum, out_sum, first_gain_sum,
        first_shift_sum, up_sum, down_sum, second_gain_sum, second_shift_sum, pool_sum, class_sum, class_bias_sum, loss,
    ) = spread(states, input_grad, logits, sums, small, late, gathered, classes)
    return (
        states, input_grad, logits, loss, query, query_sum, key, value, value_sum, out, out_sum, first_gain_sum,
        first_shift_sum, up, up_sum, down, down_sum, second_gain_sum, second_shift_sum, pool, pool_sum, class_sum.T,
        class_bias_sum,
    )


def solution(mesh):
    rows, column, both = P(("dp", "head"), None), P(None, "head"), P("dp", "head")
    one, none = P("head"), P()
    return jax.shard_map(
        body,
        mesh=mesh,
        in_specs=(rows, P("dp"), P(("dp", "head")), rows, column, one, column, column, one) + (none,) * 14,
        out_specs=(
            rows, rows, rows, none, both, one, both, both, one, both, none, none, none, both, none, both, none,
            none, none, both, none, none, none,
        ),
        check_vma=False,
    )
```
